32 devices in a mesh: row: 8 (over y, x, core), col: 4 (over z).
Axes of the slice: x: 2, y: 2, z: 4, core: 2. Of those that a mesh axis runs over, the one named last changes fastest.
Arguments:
- matrix: float32 [12288, 12288], P('row', 'col'), may hold values from -10 to 10, as said below
- panel: float32 [12288, 64], P('row'), may hold values from -1.12763724 to 1.12763724
Outputs:
- updated: float32 [12288, 12288], P('row', 'col')
- band_block: float32 [64, 64], replicated
The draws below stay inside these ranges and needn't reach their ends.
Inputs may be any that keep to these rules, and one draw needn't show every extreme that they name: matrix is exactly symmetric.
All inputs are finite; a program needn't handle non-finite values.
Results may differ from the reference program's by a relative error of at most 0.0002.
Values sent between devices are 32-bit elements; how exact they have to be, the bound alone decides.
No kernel may reach another device: no remote copies, remote signals or barrier semaphores. Data moves between devices by JAX's collectives and lax.ppermute only.
A program may use at most 128 MiB of HBM per device.

```python
import jax
import jax.numpy as jnp
from jax import lax

N = 12288
PANEL_COLUMNS = 64


def draw_matrix(key, part):
    random_part = jax.random.normal(key, (N, N), jnp.float32)
    random_part = jnp.clip(random_part, -5.0, 5.0)
    symmetric = (random_part + random_part.T) * 0.7
    return symmetric


def draw_panel(key, part):
    random_part = jnp.clip(jax.random.normal(key, (N, PANEL_COLUMNS), jnp.float32), -5.0, 5.0)
    row_spread = 2.302
    row_scale = jnp.exp(jax.random.uniform(jax.random.fold_in(key, 1), (N,), jnp.float32, 0.0, row_spread))
    column_scale = jnp.exp(jax.random.uniform(jax.random.fold_in(key, 2), (PANEL_COLUMNS,), jnp.float32, 0.0, 2.302))
    return random_part * row_scale[:, None] * column_scale[None, :] / (4.0 * jnp.sqrt(jnp.float32(N)))


def setup_inputs(seed: int = 0) -> dict:
    splits = jax.random.split(jax.random.key(seed), 3)
    matrix = draw_matrix(jax.random.fold_in(splits[2], 71), 0)
    panel = draw_panel(jax.random.fold_in(splits[2], 71), 0)
    return dict(matrix=matrix, panel=panel)


precise = lax.Precision.HIGHEST

def reference(matrix, panel):
    row_number = jnp.arange(N)
    column_position = jnp.arange(PANEL_COLUMNS)

    def householder_column(current_column_index, iteration_state):
        reduced_matrix, householder_vectors, householder_scales = iteration_state
        column = lax.optimization_barrier(jnp.sum(jnp.where(column_position[None, :] == current_column_index, reduced_matrix, 0.0), axis=1))
        leading = jnp.sum(jnp.where(row_number == current_column_index, column, 0.0))
        length = jnp.sqrt(jnp.sum(jnp.where(row_number >= current_column_index, column * column, 0.0)))
        shifted = leading + length
        vector = jnp.where(row_number > current_column_index, column / shifted, 0.0) + jnp.where(row_number == current_column_index, 1.0, 0.0)
        householder_scale = shifted / length
        projected = jnp.dot(vector, reduced_matrix, precision=precise)
        reduced_matrix = reduced_matrix - householder_scale * vector[:, None] * projected[None, :]
        householder_vectors = jnp.where(column_position[None, :] == current_column_index, vector[:, None], householder_vectors)
        householder_scales = jnp.where(column_position == current_column_index, householder_scale, householder_scales)
        return (reduced_matrix, householder_vectors, householder_scales)
    initial_state = (panel, jnp.zeros((N, PANEL_COLUMNS), jnp.float32), jnp.zeros((PANEL_COLUMNS,), jnp.float32))
    reduced_matrix, householder_vectors, householder_scales = lax.fori_loop(0, PANEL_COLUMNS, householder_column, initial_state)
    band_block = jnp.triu(reduced_matrix[:PANEL_COLUMNS])
    correlation = jnp.dot(householder_vectors.T, householder_vectors, precision=precise)

    def extend_triangle(current_column_index, triangle):
        householder_scale = jnp.sum(jnp.where(column_position == current_column_index, householder_scales, 0.0))
        wanted = lax.optimization_barrier(jnp.sum(jnp.where(column_position[None, :] == current_column_index, correlation, 0.0), axis=1))
        new_column = -householder_scale * jnp.dot(triangle, wanted, precision=precise)
        new_column = jnp.where(column_position < current_column_index, new_column, 0.0) + jnp.where(column_position == current_column_index, householder_scale, 0.0)
        return jnp.where(column_position[None, :] == current_column_index, new_column[:, None], triangle)
    triangle = lax.fori_loop(0, PANEL_COLUMNS, extend_triangle, jnp.zeros((PANEL_COLUMNS, PANEL_COLUMNS), jnp.float32))
    product = jnp.dot(matrix, householder_vectors, precision=precise)
    applied = jnp.dot(product, triangle, precision=precise)
    coupling = jnp.dot(triangle.T, jnp.dot(householder_vectors.T, applied, precision=precise), precision=precise)
    corrected = applied - 0.5 * jnp.dot(householder_vectors, coupling, precision=precise)
    left_factor = jnp.concatenate([householder_vectors, corrected], 1)
    right_factor = jnp.concatenate([corrected, householder_vectors], 1)
    updated = matrix - jnp.dot(left_factor, right_factor.T, precision=precise)
    return (updated, band_block)
```

```python
import jax
import jax.numpy as jnp
from jax import lax
from jax.experimental import pallas as pl
from jax.experimental.pallas import tpu as pltpu
from jax.sharding import PartitionSpec as P

precise = lax.Precision.HIGHEST
f32 = jnp.float32
bf16 = jnp.bfloat16


def params(mib):
    return pltpu.CompilerParams(vmem_limit_bytes=mib * 1024 * 1024)


def split(value):
    high = value.astype(bf16)
    return high, (value - high.astype(f32)).astype(bf16)


def block_of(size, wanted):
    while size % wanted:
        wanted //= 2
    return wanted


def down_kernel(kt_ref, a_ref, out_ref, acc_ref):
    step = pl.program_id(0)
    width = kt_ref.shape[0]
    kh, kl = split(kt_ref[...])
    left = jnp.concatenate([kh, kl], 0)
    columns = a_ref.shape[1]
    chunk = block_of(columns, 512)
    for c in range(0, columns, chunk):
        ah, al = split(a_ref[:, c : c + chunk])
        term = jnp.dot(left, ah, preferred_element_type=f32) + jnp.dot(
            left, al, preferred_element_type=f32
        )

        @pl.when(step == 0)
        def _():
            acc_ref[:, c : c + chunk] = term

        @pl.when(step > 0)
        def _():
            acc_ref[:, c : c + chunk] += term

    @pl.when(step == pl.num_programs(0) - 1)
    def _():
        out_ref[...] = acc_ref[:width] + acc_ref[width:]


def product_down(kt, a):
    rows, columns = a.shape
    width = kt.shape[0]
    br = block_of(rows, 256)
    return pl.pallas_call(
        down_kernel,
        grid=(rows // br,),
        in_specs=[
            pl.BlockSpec((width, br), lambda i: (0, i)),
            pl.BlockSpec((br, columns), lambda i: (i, 0)),
        ],
        out_specs=pl.BlockSpec((width, columns), lambda i: (0, 0)),
        out_shape=jax.ShapeDtypeStruct((width, columns), f32),
        scratch_shapes=[pltpu.VMEM((2 * width, columns), f32)],
        compiler_params=params(24),
        cost_estimate=pl.CostEstimate(
            flops=8 * rows * columns * width, bytes_accessed=4 * rows * columns, transcendentals=0
        ),
        name="product_down",
    )(kt, a)


def across_kernel(kt_ref, a_ref, out_ref):
    width = kt_ref.shape[0]
    columns = a_ref.shape[1]
    chunk = block_of(columns, 512)
    total = None
    for c in range(0, columns, chunk):
        kh, kl = split(kt_ref[:, c : c + chunk])
        left = jnp.concatenate([kh, kl], 0)
        ah, al = split(a_ref[:, c : c + chunk])
        dims = (((1,), (1,)), ((), ()))
        term = lax.dot_general(left, ah, dims, preferred_element_type=f32) + lax.dot_general(
            left, al, dims, preferred_element_type=f32
        )
        total = term if total is None else total + term
    out_ref[...] = total[:width] + total[width:]


def product_across(kt, a):
    rows, columns = a.shape
    width = kt.shape[0]
    br = block_of(rows, 256)
    return pl.pallas_call(
        across_kernel,
        grid=(rows // br,),
        in_specs=[
            pl.BlockSpec((width, columns), lambda i: (0, 0)),
            pl.BlockSpec((br, columns), lambda i: (i, 0)),
        ],
        out_specs=pl.BlockSpec((width, br), lambda i: (0, i)),
        out_shape=jax.ShapeDtypeStruct((width, rows), f32),
        compiler_params=params(24),
        cost_estimate=pl.CostEstimate(
            flops=8 * rows * columns * width, bytes_accessed=4 * rows * columns, transcendentals=0
        ),
        name="product_across",
    )(kt, a)


def eliminate_kernel(gram_ref, band_ref, inverse_ref):
    order = gram_ref.shape[0]
    lane = lax.broadcasted_iota(jnp.int32, (8, order), 1)
    sub = lax.broadcasted_iota(jnp.int32, (8, order), 0)
    tiles = [gram_ref[8 * t : 8 * t + 8, :] for t in range(order // 8)]
    for j in range(order):
        at, off = divmod(j, 8)
        row = jnp.broadcast_to(tiles[at][off : off + 1, :], (8, order))
        pivot = jnp.broadcast_to(row[:, j : j + 1], (8, order))
        scaled = row / pivot
        here = lane == j
        for t in range(at, order // 8):
            column = jnp.broadcast_to(tiles[t][:, j : j + 1], (8, order))
            new = jnp.where(here, -(column / pivot), tiles[t] - column * scaled)
            tiles[t] = jnp.where(sub > off, new, tiles[t]) if t == at else new
    for t in range(order // 8):
        row_at = sub + 8 * t
        diagonal = jnp.sum(jnp.where(lane == row_at, tiles[t], 0.0), axis=1, keepdims=True)
        length = jnp.sqrt(diagonal)
        scaled = tiles[t] / length
        band_ref[8 * t : 8 * t + 8, :] = jnp.where(
            lane > row_at, -scaled, jnp.where(lane == row_at, -length, 0.0)
        )
        inverse_ref[8 * t : 8 * t + 8, :] = jnp.where(
            lane < row_at, -scaled, jnp.where(lane == row_at, -1.0 / length, 0.0)
        )


def eliminate(gram):
    shape = jax.ShapeDtypeStruct(gram.shape, f32)
    return pl.pallas_call(
        eliminate_kernel,
        out_shape=(shape, shape),
        compiler_params=params(8),
        cost_estimate=pl.CostEstimate(flops=20_000_000, bytes_accessed=50_000_000, transcendentals=0),
        name="eliminate",
    )(gram)


def invert_kernel(head_ref, band_ref, inverse_ref, out_ref):
    order = head_ref.shape[0]
    lane = lax.broadcasted_iota(jnp.int32, (8, order), 1)
    sub = lax.broadcasted_iota(jnp.int32, (8, order), 0)
    tiles = [
        head_ref[8 * t : 8 * t + 8, :] - band_ref[8 * t : 8 * t + 8, :] for t in range(order // 8)
    ]
    for j in range(order):
        at, off = divmod(j, 8)
        here = lane == j
        row = jnp.broadcast_to(tiles[at][off : off + 1, :], (8, order))
        pivot = jnp.broadcast_to(row[:, j : j + 1], (8, order))
        scaled = jnp.where(here, 1.0, row) / pivot
        for t in range(order // 8):
            column = jnp.broadcast_to(tiles[t][:, j : j + 1], (8, order))
            new = jnp.where(here, 0.0, tiles[t]) - column * scaled
            tiles[t] = jnp.where(sub == off, scaled, new) if t == at else new
    block_inverse = jnp.concatenate(tiles, 0)
    out_ref[...] = -jnp.dot(
        block_inverse, inverse_ref[...], precision=precise, preferred_element_type=f32
    )


def invert(head, band, band_inverse):
    return pl.pallas_call(
        invert_kernel,
        out_shape=jax.ShapeDtypeStruct(head.shape, f32),
        compiler_params=params(8),
        cost_estimate=pl.CostEstimate(flops=20_000_000, bytes_accessed=50_000_000, transcendentals=0),
        name="invert",
    )(head, band, band_inverse)


def update_kernel(krt, xrt, kct, xct, st, cm, a_ref, out_ref, right_ref):
    width = krt.shape[0]

    def corrected(xt, kt):
        return jnp.dot(st[...], xt, precision=precise, preferred_element_type=f32) - 0.5 * jnp.dot(
            cm[...], kt, precision=precise, preferred_element_type=f32
        )

    @pl.when(pl.program_id(0) == 0)
    def _():
        columns = kct.shape[1]
        chunk = block_of(columns, 512)
        for c in range(0, columns, chunk):
            k = kct[:, c : c + chunk]
            wh, wl = split(corrected(xct[:, c : c + chunk], k))
            kh, kl = split(k)
            right_ref[:, c : c + chunk] = jnp.concatenate([wh, kh, wh, kh, wl, kl, wl, kl], 0)

    k = krt[...]
    lh, ll = split(jnp.concatenate([k, corrected(xrt[...], k)], 0).T)
    left = jnp.concatenate([lh, ll, lh, ll], 1)
    columns = a_ref.shape[1]
    chunk = block_of(columns, 512)
    for c in range(0, columns, chunk):
        out_ref[:, c : c + chunk] = a_ref[:, c : c + chunk] - jnp.dot(
            left, right_ref[:, c : c + chunk], preferred_element_type=f32
        )


def update(krt, xrt, kct, xct, st, cm, a):
    rows, columns = a.shape
    width = krt.shape[0]
    br = block_of(rows, 256)
    narrow = pl.BlockSpec((width, br), lambda i: (0, i))
    wide = pl.BlockSpec((width, columns), lambda i: (0, 0))
    small = pl.BlockSpec((width, width), lambda i: (0, 0))
    return pl.pallas_call(
        update_kernel,
        grid=(rows // br,),
        in_specs=[narrow, narrow, wide, wide, small, small, pl.BlockSpec((br, columns), lambda i: (i, 0))],
        out_specs=pl.BlockSpec((br, columns), lambda i: (i, 0)),
        out_shape=jax.ShapeDtypeStruct((rows, columns), f32),
        scratch_shapes=[pltpu.VMEM((8 * width, columns), bf16)],
        compiler_params=params(32),
        cost_estimate=pl.CostEstimate(
            flops=16 * rows * columns * width, bytes_accessed=8 * rows * columns, transcendentals=0
        ),
        name="update",
    )(krt, xrt, kct, xct, st, cm, a)


def flip(value, bit, size, axis="row"):
    return lax.ppermute(value, axis, [(i, i ^ bit) for i in range(size)])


def small_sum(value, row_size):
    if row_size != 8:
        return lax.psum(value, "row")
    value = value + flip(value, 1, row_size)
    a, b, c = flip(value, 2, row_size), flip(value, 4, row_size), flip(value, 6, row_size)
    return (value + a) + (b + c)


def big_sum(value, row_size, core):
    half = value.shape[1] // 2
    first, second = value[:, :half], value[:, half:]
    keep = jnp.where(core == 0, first, second)
    give = jnp.where(core == 0, second, first)
    keep = keep + flip(give, 1, row_size)
    quarter = half // 2
    a, b = keep[:, :quarter], keep[:, quarter:]
    bits = []
    bit = 2
    while bit < row_size:
        bits.append(bit)
        bit *= 2
    for forward, backward in zip(bits, bits[::-1]):
        a, b = a + flip(a, forward, row_size), b + flip(b, backward, row_size)
    keep = jnp.concatenate([a, b], 1)
    other = flip(keep, 1, row_size)
    return jnp.where(
        core == 0, jnp.concatenate([keep, other], 1), jnp.concatenate([other, keep], 1)
    )


def column_rows(value, row_size, col_size, row_index, col_index):
    if row_size != 2 * col_size:
        gathered = lax.all_gather(value, "row", axis=1, tiled=True)
        size = gathered.shape[1] // col_size
        return lax.dynamic_slice_in_dim(gathered, col_index * size, size, 1)

    def send(piece, source_flips, bit):
        pairs = []
        for c in range(col_size):
            for source in source_flips:
                for core in range(2):
                    at = (2 * c + core) ^ source
                    pairs.append((at * col_size + c, (at ^ bit) * col_size + c))
        return lax.ppermute(piece, ("row", "col"), pairs)

    core = row_index % 2
    relation = (row_index // 2) ^ col_index
    held = jnp.where(relation == 0, value, 0.0)
    if row_size == 8:
        by_x, by_y = send(held, [0], 2), send(held, [0], 4)
        held = held + by_x + by_y
        half = value.shape[1] // 2
        far_x = send(held[:, :half], [2], 4)
        far_y = send(held[:, half:], [4], 2)
        held = held + jnp.concatenate([far_x, far_y], 1)
    else:
        reached = [0]
        bit = 2
        while bit < row_size:
            held = held + send(held, reached, bit)
            reached = reached + [r ^ bit for r in reached]
            bit *= 2
    other = flip(held, 1, row_size)
    return jnp.where(
        core == 0, jnp.concatenate([held, other], 1), jnp.concatenate([other, held], 1)
    )


def line_sum(value, col_size, col_index):
    if col_size != 4:
        return lax.psum(value, "col")
    size = value.shape[1] // col_size

    def shift(piece, by):
        return lax.ppermute(piece, "col", [(i, (i + by) % col_size) for i in range(col_size)])

    def part(index):
        return lax.dynamic_slice_in_dim(value, (index % col_size) * size, size, 1)

    mine = part(col_index)
    for by in (2, 1, 3):
        mine = mine + shift(part(col_index + by), by)
    total = jnp.zeros_like(value)
    total = lax.dynamic_update_slice_in_dim(total, mine, col_index * size, 1)
    for by in (2, 1, 3):
        got = shift(mine, by)
        start = ((col_index - by) % col_size) * size
        total = lax.dynamic_update_slice_in_dim(total, got, start, 1)
    return total


def small_line_sum(value, col_size):
    bit = 1
    while bit < col_size:
        value = value + flip(value, bit, col_size, "col")
        bit *= 2
    return value


def body_of(row_size, col_size):
    def body(matrix, panel):
        width = panel.shape[1]
        row_index = lax.axis_index("row")
        col_index = lax.axis_index("col")
        core = row_index % 2
        panel_t = panel.T
        local = jnp.dot(panel_t, panel, precision=precise)
        head = jnp.where(row_index == 0, panel[:width], 0.0)
        summed = small_sum(jnp.concatenate([local, head], 1), row_size)
        gram, head = summed[:, :width], summed[:, width:]
        panel_cols = column_rows(panel_t, row_size, col_size, row_index, col_index)
        down = product_down(panel_t, matrix)
        band, band_inverse = eliminate(gram)
        top_row = jnp.where(row_index == 0, band.T, 0.0)
        top_col = jnp.where(col_index == 0, band.T, 0.0)
        down = down - jnp.dot(top_row, matrix[:width], precision=precise)
        krt = panel_t.at[:, :width].add(-top_row)
        kct = panel_cols.at[:, :width].add(-top_col)
        across = product_across(kct, matrix)
        xct = big_sum(down, row_size, core)
        xrt = line_sum(across, col_size, col_index)
        st = invert(head, band, band_inverse)
        inner = lax.dot_general(kct, xct, (((1,), (1,)), ((), ())), precision=precise)
        inner = small_line_sum(inner, col_size)
        cm = jnp.dot(jnp.dot(st, inner, precision=precise), st.T, precision=precise)
        updated = update(krt, xrt, kct, xct, st, cm, matrix)
        return updated, band

    return body


def solution(mesh):
    return jax.shard_map(
        body_of(mesh.shape["row"], mesh.shape["col"]),
        mesh=mesh,
        in_specs=(P("row", "col"), P("row", None)),
        out_specs=(P("row", "col"), P()),
        check_vma=False,
    )
```

```python
import jax
import jax.numpy as jnp
from jax import lax
from jax.experimental import pallas as pl
from jax.experimental.pallas import tpu as pltpu
from jax.sharding import PartitionSpec as P

precise = lax.Precision.HIGHEST
f32 = jnp.float32
bf16 = jnp.bfloat16


def shape(*dims, dtype=f32):
    return jax.ShapeDtypeStruct(dims, dtype)


def params(mib):
    return pltpu.CompilerParams(vmem_limit_bytes=mib * 1024 * 1024)


def cost(flops, moved):
    return pl.CostEstimate(flops=flops, bytes_accessed=moved, transcendentals=0)


def dot(a, b):
    return jnp.dot(a, b, precision=precise, preferred_element_type=f32)


def fast(a, b):
    return jnp.dot(a, b, preferred_element_type=f32)


def split(value):
    high = value.astype(bf16)
    return high, (value - high.astype(f32)).astype(bf16)


def block_of(size, wanted):
    while size % wanted:
        wanted //= 2
    return wanted


def small_call(kernel, out, *operands, name, carry=None, flops=1_000_000, moved=1_000_000, mib=8):
    extra = {}
    body = kernel
    if carry is not None:
        outs = out if isinstance(out, tuple) else (out,)
        count = len(operands)
        anywhere = pl.BlockSpec(memory_space=pl.ANY)
        whole = pl.BlockSpec(memory_space=pltpu.VMEM)
        extra = dict(
            in_specs=[whole] * count + [anywhere],
            out_specs=(whole,) * len(outs) + (anywhere,),
            input_output_aliases={count: len(outs)},
        )
        operands = operands + (carry,)
        out = outs + (shape(*carry.shape),)

        def body(*refs):
            kernel(*refs[:count], *refs[count + 1 : -1])

    return pl.pallas_call(
        body,
        out_shape=out,
        compiler_params=params(mib),
        cost_estimate=cost(flops, moved),
        name=name,
        **extra,
    )(*operands)


def open_kernel(turned_ref, first_ref, second_ref, packed_ref):
    width = turned_ref.shape[0]
    half = first_ref.shape[1]
    turned = turned_ref[...]
    first_ref[...] = turned[:, :half]
    second_ref[...] = turned[:, half:]
    gram = lax.dot_general(
        turned, turned, (((1,), (1,)), ((), ())), precision=precise, preferred_element_type=f32
    )
    head = jnp.where(lax.axis_index("row") == 0, turned[:, : 2 * width].T[:width], 0.0)
    packed_ref[...] = jnp.concatenate([gram, head], 1)


def add_kernel(*refs):
    total = refs[0][...]
    for ref in refs[1:-1]:
        total = total + ref[...]
    refs[-1][...] = total


def spread(tile, at):
    return jnp.broadcast_to(tile[at : at + 1, :], tile.shape)


def pick(tile, at):
    return jnp.broadcast_to(tile[:, at : at + 1], tile.shape)


def sweep(tiles, order, full):
    lane = lax.broadcasted_iota(jnp.int32, (8, order), 1)
    sub = lax.broadcasted_iota(jnp.int32, (8, order), 0)
    tiles = list(tiles)
    for at in range(order // 8):
        base = 8 * at
        inside = (lane >= base) & (lane < base + 8)
        tile = tiles[at]
        others = [t for t in range(order // 8) if (t != at if full else t > at)]
        picked = {t: [pick(tiles[t], base + q) for q in range(8)] for t in others}
        columns = [pick(tile, base + q) for q in range(8)]
        rows = jnp.where(inside, jnp.where(lane - base == sub, 1.0, 0.0), tile)
        lower, upper = rows, tile
        for q in range(8):
            here = sub == q
            inverse = 1.0 / spread(columns[q], q)
            scaled = spread(rows, q) * inverse
            if not full:
                lower = jnp.where(here, rows, lower)
                upper = jnp.where(
                    sub > q, upper - columns[q] * (spread(upper, q) * inverse), upper
                )
            rows = jnp.where(here, scaled, rows - columns[q] * scaled)
            for p in range(q + 1, 8):
                part = spread(columns[p], q) * inverse
                columns[p] = jnp.where(here, part, columns[p] - columns[q] * part)
        finals = [spread(rows, q) for q in range(8)]
        for t in others:
            value = jnp.where(inside, 0.0, tiles[t])
            for q in range(8):
                value = value - picked[t][q] * finals[q]
            tiles[t] = value
        tiles[at] = rows if full else jnp.where(inside & (lane - base >= sub), upper, lower)
    return tiles


def eliminate_kernel(a_ref, b_ref, c_ref, d_ref, band_ref, inverse_ref, head_ref):
    order = band_ref.shape[0]
    lane = lax.broadcasted_iota(jnp.int32, (8, order), 1)
    sub = lax.broadcasted_iota(jnp.int32, (8, order), 0)
    total = (a_ref[...] + b_ref[...]) + (c_ref[...] + d_ref[...])
    head_ref[...] = total[:, order:]
    gram = total[:, :order]
    tiles = sweep([gram[8 * t : 8 * t + 8, :] for t in range(order // 8)], order, False)
    for t in range(order // 8):
        row_at = sub + 8 * t
        diagonal = jnp.sum(jnp.where(lane == row_at, tiles[t], 0.0), axis=1, keepdims=True)
        length = jnp.sqrt(diagonal)
        scaled = tiles[t] / length
        band_ref[8 * t : 8 * t + 8, :] = jnp.where(
            lane > row_at, -scaled, jnp.where(lane == row_at, -length, 0.0)
        )
        inverse_ref[8 * t : 8 * t + 8, :] = jnp.where(
            lane < row_at, -scaled, jnp.where(lane == row_at, -1.0 / length, 0.0)
        )


def invert_kernel(head_ref, band_ref, inverse_ref, out_ref):
    order = head_ref.shape[0]
    tiles = [
        head_ref[8 * t : 8 * t + 8, :] - band_ref[8 * t : 8 * t + 8, :] for t in range(order // 8)
    ]
    tiles = sweep(tiles, order, True)
    out_ref[...] = -dot(jnp.concatenate(tiles, 0), inverse_ref[...])


def down_kernel(first_ref, second_ref, a_ref, out_ref, kept_ref):
    width = first_ref.shape[0]
    kh, kl = split(jnp.concatenate([first_ref[...], second_ref[...]], 1))
    left = jnp.concatenate([kh, kl], 0)
    value = a_ref[...]
    kept_ref[...] = value
    ah, al = split(value)
    term = fast(left, ah) + fast(left, al)
    out_ref[...] = term[:width] + term[width:]


def product_down(first, second, a):
    rows, columns = a.shape
    width, half = first.shape
    bc = block_of(columns, 512)
    part = pl.BlockSpec((width, half), lambda i: (0, 0))
    block = pl.BlockSpec((rows, bc), lambda i: (0, i))
    return pl.pallas_call(
        down_kernel,
        grid=(columns // bc,),
        in_specs=[part, part, block],
        out_specs=(pl.BlockSpec((width, bc), lambda i: (0, i)), block),
        out_shape=(shape(width, columns), shape(rows, columns)),
        compiler_params=params(22),
        cost_estimate=cost(8 * rows * columns * width, 4 * rows * columns),
        name="product_down",
    )(first, second, pltpu.with_memory_space_constraint(a, pltpu.HBM))


def fix_kernel(raw_ref, band_ref, top_ref, keep_ref, give_ref, _):
    half = keep_ref.shape[1]
    row = lax.axis_index("row")
    core = lax.rem(row, 2)
    first, second = raw_ref[:, :half], raw_ref[:, half:]

    @pl.when(row == 0)
    def _():
        turned = band_ref[...].T
        keep_ref[...] = first - dot(turned, top_ref[:, :half])
        give_ref[...] = second - dot(turned, top_ref[:, half:])

    @pl.when((row != 0) & (core == 0))
    def _():
        keep_ref[...] = first
        give_ref[...] = second

    @pl.when(core == 1)
    def _():
        keep_ref[...] = second
        give_ref[...] = first


def fix_down(raw, band, a):
    width, columns = raw.shape
    half = shape(width, columns // 2)
    whole = pl.BlockSpec((width, columns), lambda i: (0, 0))
    halves = pl.BlockSpec((width, columns // 2), lambda i: (0, 0))
    return pl.pallas_call(
        fix_kernel,
        grid=(1,),
        in_specs=[whole, pl.BlockSpec((width, width), lambda i: (0, 0)), whole],
        out_specs=(halves, halves, pl.BlockSpec(memory_space=pl.ANY)),
        out_shape=(half, half, shape(*a.shape)),
        input_output_aliases={2: 2},
        compiler_params=params(12),
        cost_estimate=cost(12 * width * width * columns, 16 * width * columns),
        name="fix_down",
    )(raw, band, a)


def across_kernel(held_ref, other_ref, band_ref, a_ref, *refs):
    kct_ref, outs, right_ref = refs[0], refs[1:-2], refs[-1]
    width, half = held_ref.shape
    columns = a_ref.shape[1]
    step = pl.program_id(0)
    chunk = block_of(columns, 512)

    @pl.when(step == 0)
    def _():
        core = lax.rem(lax.axis_index("row"), 2)

        @pl.when(core == 0)
        def _():
            kct_ref[:, :half] = held_ref[...]
            kct_ref[:, half:] = other_ref[...]

        @pl.when(core == 1)
        def _():
            kct_ref[:, :half] = other_ref[...]
            kct_ref[:, half:] = held_ref[...]

        @pl.when(lax.axis_index("col") == 0)
        def _():
            kct_ref[:, :width] = kct_ref[:, :width] - band_ref[...].T

        for c in range(0, columns, chunk):
            right_ref[c : c + chunk, :] = jnp.concatenate(split(kct_ref[:, c : c + chunk].T), 1)

    total = None
    for c in range(0, columns, chunk):
        ah, al = split(a_ref[:, c : c + chunk])
        right = right_ref[c : c + chunk, :]
        term = fast(ah, right) + fast(al, right)
        total = term if total is None else total + term
    result = (total[:, :width] + total[:, width:]).T
    for at, out_ref in enumerate(outs):

        @pl.when(step == at)
        def _():
            out_ref[...] = result


def product_across(held, other, band, a, pieces):
    rows, columns = a.shape
    width, half = held.shape
    size = rows // pieces

    def turn(i):
        return (lax.rem(i + lax.axis_index("col"), pieces), 0)

    part = pl.BlockSpec((width, half), lambda i: (0, 0))
    one = pl.BlockSpec((width, size), lambda i: (0, 0))
    return pl.pallas_call(
        across_kernel,
        grid=(pieces,),
        in_specs=[
            part,
            part,
            pl.BlockSpec((width, width), lambda i: (0, 0)),
            pl.BlockSpec((size, columns), turn),
        ],
        out_specs=(pl.BlockSpec((width, columns), lambda i: (0, 0)),)
        + (one,) * pieces
        + (pl.BlockSpec(memory_space=pl.ANY),),
        out_shape=(shape(width, columns),)
        + (shape(width, size),) * pieces
        + (shape(rows, columns),),
        input_output_aliases={3: pieces + 1},
        scratch_shapes=[pltpu.VMEM((columns, 2 * width), bf16)],
        compiler_params=params(22),
        cost_estimate=cost(8 * rows * columns * width, 4 * rows * columns),
        name="product_across",
    )(held, other, band, a)


def merge_first_kernel(first_ref, second_ref, by_x_ref, by_y_ref, a_ref, b_ref):
    source = lax.div(lax.axis_index("row"), 2) == lax.axis_index("col")
    a_ref[...] = jnp.where(source, first_ref[...], by_x_ref[...])
    b_ref[...] = jnp.where(source, second_ref[...], by_y_ref[...])


def join_kernel(a_ref, b_ref, c_ref, d_ref, out_ref):
    half = a_ref.shape[1]
    out_ref[:, :half] = a_ref[...] + b_ref[...]
    out_ref[:, half:] = c_ref[...] + d_ref[...]


def halve_kernel(keep_ref, other_ref, a_ref, b_ref):
    half = a_ref.shape[1]
    a_ref[...] = keep_ref[:, :half] + other_ref[:, :half]
    b_ref[...] = keep_ref[:, half:] + other_ref[:, half:]


def pair_kernel(a_ref, b_ref, c_ref, d_ref, e_ref, f_ref):
    e_ref[...] = a_ref[...] + b_ref[...]
    f_ref[...] = c_ref[...] + d_ref[...]


def inner_kernel(kct_ref, held_ref, other_ref, xct_ref, inner_ref):
    half = held_ref.shape[1]
    core = lax.rem(lax.axis_index("row"), 2)

    @pl.when(core == 0)
    def _():
        xct_ref[:, :half] = held_ref[...]
        xct_ref[:, half:] = other_ref[...]

    @pl.when(core == 1)
    def _():
        xct_ref[:, :half] = other_ref[...]
        xct_ref[:, half:] = held_ref[...]

    inner_ref[...] = lax.dot_general(
        kct_ref[...],
        xct_ref[...],
        (((1,), (1,)), ((), ())),
        precision=precise,
        preferred_element_type=f32,
    )


def corrected(st, cm, xt, kt):
    return dot(st, xt) - 0.5 * dot(cm, kt)


def right_kernel(part_ref, more_ref, st_ref, xct_ref, kct_ref, cm_ref, right_ref):
    width, columns = kct_ref.shape
    st = st_ref[...]
    cm = dot(dot(st, part_ref[...] + more_ref[...]), st.T)
    cm_ref[...] = cm
    chunk = block_of(columns, 512)
    for c in range(0, columns, chunk):
        k = kct_ref[:, c : c + chunk]
        wh, wl = split(corrected(st, cm, xct_ref[:, c : c + chunk], k))
        kh, kl = split(k)
        right_ref[:, c : c + chunk] = jnp.concatenate([wh, kh, wl, kl], 0)


def left_kernel(first_ref, second_ref, band_ref, st_ref, cm_ref, *refs):
    chunks, left_ref, krt_ref = refs[:-2], refs[-2], refs[-1]
    width, half = first_ref.shape
    pieces = len(chunks)
    size = chunks[0].shape[1]
    krt_ref[:, :half] = first_ref[...]
    krt_ref[:, half:] = second_ref[...]

    @pl.when(lax.axis_index("row") == 0)
    def _():
        krt_ref[:, :width] = krt_ref[:, :width] - band_ref[...].T

    st, cm = st_ref[...], cm_ref[...]
    col = lax.axis_index("col")
    for at, ref in enumerate(chunks):
        start = pl.multiple_of(lax.rem(col + pieces - at, pieces) * size, size)
        k = krt_ref[:, pl.ds(start, size)]
        both = jnp.concatenate([k, corrected(st, cm, ref[...], k)], 0)
        left_ref[pl.ds(start, size), :] = jnp.concatenate(split(both.T), 1)


def subtract_kernel(left_ref, right_ref, a_ref, out_ref):
    width = left_ref.shape[1] // 2
    left = left_ref[...]
    left = jnp.concatenate([left, left], 1)
    columns = a_ref.shape[1]
    chunk = block_of(columns, 512)
    for c in range(0, columns, chunk):
        high = right_ref[:width, c : c + chunk]
        low = right_ref[width:, c : c + chunk]
        both = jnp.concatenate([high, high, low, low], 0)
        out_ref[:, c : c + chunk] = a_ref[:, c : c + chunk] - fast(left, both)


def subtract(left, right, a):
    rows, columns = a.shape
    deep = left.shape[1]
    br = block_of(rows, 256)
    return pl.pallas_call(
        subtract_kernel,
        grid=(rows // br,),
        in_specs=[
            pl.BlockSpec((br, deep), lambda i: (i, 0)),
            pl.BlockSpec((deep, columns), lambda i: (0, 0)),
            pl.BlockSpec((br, columns), lambda i: (i, 0)),
        ],
        out_specs=pl.BlockSpec((br, columns), lambda i: (i, 0)),
        out_shape=shape(rows, columns),
        compiler_params=params(22),
        cost_estimate=cost(4 * rows * columns * deep, 8 * rows * columns),
        name="subtract",
    )(left, right, a)


def flip(value, bit, size, axis="row"):
    return lax.ppermute(value, axis, [(i, i ^ bit) for i in range(size)])


def from_sources(piece, col_size, source_flips, bit):
    pairs = []
    for c in range(col_size):
        for source in source_flips:
            for core in range(2):
                at = (2 * c + core) ^ source
                pairs.append((at * col_size + c, (at ^ bit) * col_size + c))
    return lax.ppermute(piece, ("row", "col"), pairs)


def shift(piece, by, size):
    return lax.ppermute(piece, "col", [(i, (i + by) % size) for i in range(size)])


def body_of(row_size, col_size):
    assert row_size == 2 * col_size

    def body(matrix, panel):
        rows, width = panel.shape
        columns = matrix.shape[1]
        small = shape(width, width)
        packed = shape(width, 2 * width)
        half = shape(width, rows // 2)
        first, second, partial = small_call(
            open_kernel, (half, half, packed), panel.T, name="open", flops=100_000_000, mib=12
        )
        partial = small_call(add_kernel, packed, partial, flip(partial, 1, row_size), name="add_cores")
        if row_size == 8:
            terms = [partial] + [flip(partial, bit, row_size) for bit in (2, 4, 6)]
        else:
            bit = 2
            total = partial
            while bit < row_size // 2:
                total = total + flip(total, bit, row_size)
                bit *= 2
            zero = jnp.zeros_like(total)
            terms = [total, flip(total, row_size // 2, row_size), zero, zero]
        first, second, partial = lax.optimization_barrier((first, second, partial))
        raw, resident = product_down(first, second, matrix)
        if row_size == 8:
            by_x = from_sources(first, col_size, [0], 2)
            by_y = from_sources(second, col_size, [0], 4)
            one, two, resident = small_call(
                merge_first_kernel,
                (half, half),
                first,
                second,
                by_x,
                by_y,
                name="merge_first",
                carry=resident,
            )
            more_x = from_sources(two, col_size, [0, 4], 2)
            more_y = from_sources(one, col_size, [0, 2], 4)
        else:
            relation = (lax.axis_index("row") // 2) ^ lax.axis_index("col")
            held = jnp.where(relation == 0, jnp.concatenate([first, second], 1), 0.0)
            reached = [0]
            bit = 2
            while bit < row_size:
                held = held + from_sources(held, col_size, reached, bit)
                reached = reached + [r ^ bit for r in reached]
                bit *= 2
        band, band_inverse, head, resident = small_call(
            eliminate_kernel,
            (small, small, small),
            *terms,
            name="eliminate",
            flops=50_000_000,
            carry=resident,
        )
        keep, give, resident = fix_down(raw, band, resident)
        if row_size == 8:
            held, resident = small_call(
                join_kernel,
                shape(width, rows),
                one,
                more_y,
                two,
                more_x,
                name="merge_second",
                carry=resident,
            )
        other = flip(held, 1, row_size)
        quarter = shape(width, columns // 4)
        a, b, resident = small_call(
            halve_kernel,
            (quarter, quarter),
            keep,
            flip(give, 1, row_size),
            name="add_halves",
            carry=resident,
        )
        bits = []
        bit = 2
        while bit < row_size:
            bits.append(bit)
            bit *= 2
        for forward, backward in list(zip(bits, bits[::-1]))[:-1]:
            ra, rb = flip(a, forward, row_size), flip(b, backward, row_size)
            if bits[0] == forward:
                pieces = 1 if (rows // col_size) % 128 else col_size
                kct, *chunks, resident = product_across(held, other, band, resident, pieces)
            a, b, resident = small_call(
                pair_kernel, (quarter, quarter), a, ra, b, rb, name="add_chips", carry=resident
            )
        ra, rb = flip(a, bits[-1], row_size), flip(b, bits[0], row_size)
        st, resident = small_call(
            invert_kernel,
            small,
            head,
            band,
            band_inverse,
            name="invert",
            flops=50_000_000,
            carry=resident,
        )
        if pieces == 1:
            whole = [lax.psum(chunks[0], "col")]
        else:
            received = [shift(chunks[by], by, col_size) for by in range(1, col_size)]
            mine, resident = small_call(
                add_kernel,
                shape(width, rows // col_size),
                chunks[0],
                *received,
                name="add_line",
                carry=resident,
            )
            whole = [mine] + [shift(mine, by, col_size) for by in range(1, col_size)]
        summed, resident = small_call(
            join_kernel,
            shape(width, columns // 2),
            a,
            ra,
            b,
            rb,
            name="add_last",
            carry=resident,
        )
        xct, inner, resident = small_call(
            inner_kernel,
            (shape(width, columns), small),
            kct,
            summed,
            flip(summed, 1, row_size),
            name="inner",
            carry=resident,
        )
        bit = 1
        while bit < col_size // 2:
            inner, resident = small_call(
                add_kernel,
                small,
                inner,
                flip(inner, bit, col_size, "col"),
                name="add_inner",
                carry=resident,
            )
            bit *= 2
        more = flip(inner, bit, col_size, "col")
        cm, right, resident = small_call(
            right_kernel,
            (small, shape(4 * width, columns, dtype=bf16)),
            inner,
            more,
            st,
            xct,
            kct,
            name="right",
            mib=12,
            carry=resident,
        )
        left, _, resident = small_call(
            left_kernel,
            (shape(rows, 4 * width, dtype=bf16), shape(width, rows)),
            first,
            second,
            band,
            st,
            cm,
            *whole,
            name="left",
            mib=12,
            carry=resident,
        )
        return subtract(left, right, resident), band

    return body


def solution(mesh):
    return jax.shard_map(
        body_of(mesh.shape["row"], mesh.shape["col"]),
        mesh=mesh,
        in_specs=(P("row", "col"), P("row", None)),
        out_specs=(P("row", "col"), P()),
        check_vma=False,
    )
```

```python
import jax
import jax.numpy as jnp
from jax import lax
from jax.experimental import pallas as pl
from jax.experimental.pallas import tpu as pltpu
from jax.sharding import PartitionSpec as P


precise = lax.Precision.HIGHEST
f32 = jnp.float32
bf16 = jnp.bfloat16


def shape(*dims, dtype=f32):
    return jax.ShapeDtypeStruct(dims, dtype)


def params(mib):
    return pltpu.CompilerParams(vmem_limit_bytes=mib * 1024 * 1024)


def cost(flops, moved):
    return pl.CostEstimate(flops=flops, bytes_accessed=moved, transcendentals=0)


def dot(a, b):
    return jnp.dot(a, b, precision=precise, preferred_element_type=f32)


def fast(a, b):
    return jnp.dot(a, b, preferred_element_type=f32)


def split(value):
    high = value.astype(bf16)
    return high, (value - high.astype(f32)).astype(bf16)


def block_of(size, wanted):
    while size % wanted:
        wanted //= 2
    return wanted


def small_call(kernel, out, *operands, carry=None, flops=1_000_000, moved=1_000_000, mib=8):
    extra = {}
    body = kernel
    if carry is not None:
        outs = out if isinstance(out, tuple) else (out,)
        count = len(operands)
        anywhere = pl.BlockSpec(memory_space=pl.ANY)
        whole = pl.BlockSpec(memory_space=pltpu.VMEM)
        extra = dict(
            in_specs=[whole] * count + [anywhere],
            out_specs=(whole,) * len(outs) + (anywhere,),
            input_output_aliases={count: len(outs)},
        )
        operands = operands + (carry,)
        out = outs + (shape(*carry.shape),)

        def body(*refs):
            kernel(*refs[:count], *refs[count + 1 : -1])

    return pl.pallas_call(
        body, out_shape=out, compiler_params=params(mib), cost_estimate=cost(flops, moved), **extra
    )(*operands)


def open_kernel(turned_ref, first_ref, second_ref, packed_ref):
    width = turned_ref.shape[0]
    half = first_ref.shape[1]
    turned = turned_ref[...]
    first_ref[...] = turned[:, :half]
    second_ref[...] = turned[:, half:]
    gram = lax.dot_general(
        turned, turned, (((1,), (1,)), ((), ())), precision=precise, preferred_element_type=f32
    )
    head = jnp.where(lax.axis_index("row") == 0, turned[:, : 2 * width].T[:width], 0.0)
    packed_ref[...] = jnp.concatenate([gram, head], 1)


def add_kernel(*refs):
    total = refs[0][...]
    for ref in refs[1:-1]:
        total = total + ref[...]
    refs[-1][...] = total


def spread(tile, at):
    return jnp.broadcast_to(tile[at : at + 1, :], tile.shape)


def pick(tile, at):
    return jnp.broadcast_to(tile[:, at : at + 1], tile.shape)


def sweep(tiles, order, full):
    lane = lax.broadcasted_iota(jnp.int32, (8, order), 1)
    sub = lax.broadcasted_iota(jnp.int32, (8, order), 0)
    tiles = list(tiles)
    for at in range(order // 8):
        base = 8 * at
        inside = (lane >= base) & (lane < base + 8)
        tile = tiles[at]
        others = [t for t in range(order // 8) if (t != at if full else t > at)]
        picked = {t: [pick(tiles[t], base + q) for q in range(8)] for t in others}
        columns = [pick(tile, base + q) for q in range(8)]
        rows = jnp.where(inside, jnp.where(lane - base == sub, 1.0, 0.0), tile)
        lower, upper = rows, tile
        for q in range(8):
            here = sub == q
            inverse = 1.0 / spread(columns[q], q)
            scaled = spread(rows, q) * inverse
            if not full:
                lower = jnp.where(here, rows, lower)
                upper = jnp.where(
                    sub > q, upper - columns[q] * (spread(upper, q) * inverse), upper
                )
            rows = jnp.where(here, scaled, rows - columns[q] * scaled)
            for p in range(q + 1, 8):
                part = spread(columns[p], q) * inverse
                columns[p] = jnp.where(here, part, columns[p] - columns[q] * part)
        finals = [spread(rows, q) for q in range(8)]
        for t in others:
            value = jnp.where(inside, 0.0, tiles[t])
            for q in range(8):
                value = value - picked[t][q] * finals[q]
            tiles[t] = value
        tiles[at] = rows if full else jnp.where(inside & (lane - base >= sub), upper, lower)
    return tiles


def eliminate_kernel(a_ref, b_ref, c_ref, d_ref, band_ref, again_ref, inverse_ref, head_ref):
    order = band_ref.shape[0]
    lane = lax.broadcasted_iota(jnp.int32, (8, order), 1)
    sub = lax.broadcasted_iota(jnp.int32, (8, order), 0)
    total = (a_ref[...] + b_ref[...]) + (c_ref[...] + d_ref[...])
    head_ref[...] = total[:, order:]
    gram = total[:, :order]
    tiles = sweep([gram[8 * t : 8 * t + 8, :] for t in range(order // 8)], order, False)
    for t in range(order // 8):
        row_at = sub + 8 * t
        diagonal = jnp.sum(jnp.where(lane == row_at, tiles[t], 0.0), axis=1, keepdims=True)
        length = jnp.sqrt(diagonal)
        scaled = tiles[t] / length
        band = jnp.where(lane > row_at, -scaled, jnp.where(lane == row_at, -length, 0.0))
        band_ref[8 * t : 8 * t + 8, :] = band
        again_ref[8 * t : 8 * t + 8, :] = band
        inverse_ref[8 * t : 8 * t + 8, :] = jnp.where(
            lane < row_at, -scaled, jnp.where(lane == row_at, -1.0 / length, 0.0)
        )


def invert_kernel(head_ref, band_ref, inverse_ref, out_ref):
    order = head_ref.shape[0]
    tiles = [
        head_ref[8 * t : 8 * t + 8, :] - band_ref[8 * t : 8 * t + 8, :] for t in range(order // 8)
    ]
    tiles = sweep(tiles, order, True)
    out_ref[...] = -dot(jnp.concatenate(tiles, 0), inverse_ref[...])


def down_kernel(first_ref, second_ref, a_ref, out_ref, kept_ref, sems):
    width = first_ref.shape[0]
    columns = a_ref.shape[1]
    count = sems.shape[0]
    size = columns // count

    def load(i):
        part = pl.ds(pl.multiple_of(i * size, size), size)
        return pltpu.make_async_copy(a_ref.at[:, part], kept_ref.at[:, part], sems.at[i])

    for i in range(count):
        load(i).start()
    kh, kl = split(jnp.concatenate([first_ref[...], second_ref[...]], 1))
    left = jnp.concatenate([kh, kl], 0)

    @pl.loop(0, count)
    def _(i):
        load(i).wait()
        part = pl.ds(pl.multiple_of(i * size, size), size)
        ah, al = split(kept_ref[:, part])
        term = fast(left, ah) + fast(left, al)
        out_ref[:, part] = term[:width] + term[width:]


def product_down(first, second, a):
    rows, columns = a.shape
    width = first.shape[0]
    size = block_of(columns, 256)
    whole = pl.BlockSpec(memory_space=pltpu.VMEM)
    return pl.pallas_call(
        down_kernel,
        in_specs=[whole, whole, pl.BlockSpec(memory_space=pltpu.HBM)],
        out_specs=(whole, whole),
        out_shape=(shape(width, columns), shape(rows, columns)),
        scratch_shapes=[pltpu.SemaphoreType.DMA((columns // size,))],
        compiler_params=params(12),
        cost_estimate=cost(8 * rows * columns * width, 4 * rows * columns),
        name="product_down",
    )(first, second, pltpu.with_memory_space_constraint(a, pltpu.HBM))


def fix_kernel(raw_ref, band_ref, top_ref, keep_ref, give_ref, _):
    half = keep_ref.shape[1]
    row = lax.axis_index("row")
    core = lax.rem(row, 2)
    first, second = raw_ref[:, :half], raw_ref[:, half:]

    @pl.when(row == 0)
    def _():
        turned = band_ref[...].T
        keep_ref[...] = first - dot(turned, top_ref[:, :half])
        give_ref[...] = second - dot(turned, top_ref[:, half:])

    @pl.when((row != 0) & (core == 0))
    def _():
        keep_ref[...] = first
        give_ref[...] = second

    @pl.when(core == 1)
    def _():
        keep_ref[...] = second
        give_ref[...] = first


def fix_down(raw, band, a):
    width, columns = raw.shape
    half = shape(width, columns // 2)
    whole = pl.BlockSpec((width, columns), lambda i: (0, 0))
    halves = pl.BlockSpec((width, columns // 2), lambda i: (0, 0))
    return pl.pallas_call(
        fix_kernel,
        grid=(1,),
        in_specs=[whole, pl.BlockSpec((width, width), lambda i: (0, 0)), whole],
        out_specs=(halves, halves, pl.BlockSpec(memory_space=pl.ANY)),
        out_shape=(half, half, shape(*a.shape)),
        input_output_aliases={2: 2},
        compiler_params=params(12),
        cost_estimate=cost(12 * width * width * columns, 16 * width * columns),
        name="fix_down",
    )(raw, band, a)


def across_kernel(held_ref, other_ref, band_ref, a_ref, *refs):
    kct_ref, outs, right_ref = refs[0], refs[1:-2], refs[-1]
    width, half = held_ref.shape
    columns = a_ref.shape[1]
    step = pl.program_id(0)
    chunk = block_of(columns, 512)

    @pl.when(step == 0)
    def _():
        core = lax.rem(lax.axis_index("row"), 2)

        @pl.when(core == 0)
        def _():
            kct_ref[:, :half] = held_ref[...]
            kct_ref[:, half:] = other_ref[...]

        @pl.when(core == 1)
        def _():
            kct_ref[:, :half] = other_ref[...]
            kct_ref[:, half:] = held_ref[...]

        @pl.when(lax.axis_index("col") == 0)
        def _():
            kct_ref[:, :width] = kct_ref[:, :width] - band_ref[...].T

        for c in range(0, columns, chunk):
            right_ref[c : c + chunk, :] = jnp.concatenate(split(kct_ref[:, c : c + chunk].T), 1)

    total = None
    for c in range(0, columns, chunk):
        ah, al = split(a_ref[:, c : c + chunk])
        right = right_ref[c : c + chunk, :]
        term = fast(ah, right) + fast(al, right)
        total = term if total is None else total + term
    result = (total[:, :width] + total[:, width:]).T
    for at, out_ref in enumerate(outs):

        @pl.when(step == at)
        def _():
            out_ref[...] = result


def product_across(held, other, band, a, pieces):
    rows, columns = a.shape
    width, half = held.shape
    size = rows // pieces

    def turn(i):
        return (lax.rem(i + lax.axis_index("col"), pieces), 0)

    part = pl.BlockSpec((width, half), lambda i: (0, 0))
    one = pl.BlockSpec((width, size), lambda i: (0, 0))
    return pl.pallas_call(
        across_kernel,
        grid=(pieces,),
        in_specs=[
            part,
            part,
            pl.BlockSpec((width, width), lambda i: (0, 0)),
            pl.BlockSpec((size, columns), turn),
        ],
        out_specs=(pl.BlockSpec((width, columns), lambda i: (0, 0)),)
        + (one,) * pieces
        + (pl.BlockSpec(memory_space=pl.ANY),),
        out_shape=(shape(width, columns),)
        + (shape(width, size),) * pieces
        + (shape(rows, columns),),
        input_output_aliases={3: pieces + 1},
        scratch_shapes=[pltpu.VMEM((columns, 2 * width), bf16)],
        compiler_params=params(22),
        cost_estimate=cost(8 * rows * columns * width, 4 * rows * columns),
        name="product_across",
    )(held, other, band, a)


def merge_first_kernel(first_ref, second_ref, by_x_ref, by_y_ref, a_ref, b_ref):
    source = lax.div(lax.axis_index("row"), 2) == lax.axis_index("col")
    a_ref[...] = jnp.where(source, first_ref[...], by_x_ref[...])
    b_ref[...] = jnp.where(source, second_ref[...], by_y_ref[...])


def join_kernel(a_ref, b_ref, c_ref, d_ref, out_ref):
    half = a_ref.shape[1]
    out_ref[:, :half] = a_ref[...] + b_ref[...]
    out_ref[:, half:] = c_ref[...] + d_ref[...]


def halve_kernel(keep_ref, other_ref, a_ref, b_ref):
    half = a_ref.shape[1]
    a_ref[...] = keep_ref[:, :half] + other_ref[:, :half]
    b_ref[...] = keep_ref[:, half:] + other_ref[:, half:]


def pair_kernel(a_ref, b_ref, c_ref, d_ref, e_ref, f_ref):
    e_ref[...] = a_ref[...] + b_ref[...]
    f_ref[...] = c_ref[...] + d_ref[...]


def inner_kernel(kct_ref, held_ref, other_ref, xct_ref, inner_ref):
    half = held_ref.shape[1]
    core = lax.rem(lax.axis_index("row"), 2)

    @pl.when(core == 0)
    def _():
        xct_ref[:, :half] = held_ref[...]
        xct_ref[:, half:] = other_ref[...]

    @pl.when(core == 1)
    def _():
        xct_ref[:, :half] = other_ref[...]
        xct_ref[:, half:] = held_ref[...]

    inner_ref[...] = lax.dot_general(
        kct_ref[...],
        xct_ref[...],
        (((1,), (1,)), ((), ())),
        precision=precise,
        preferred_element_type=f32,
    )


def wide_kernel(st_ref, xct_ref, kct_ref, first_ref, second_ref, band_ref, x_ref, k_ref, rows_ref):
    width, columns = kct_ref.shape
    st = st_ref[...]
    chunk = block_of(columns, 512)
    for c in range(0, columns, chunk):
        for ref, value in (
            (x_ref, dot(st, xct_ref[:, c : c + chunk])),
            (k_ref, kct_ref[:, c : c + chunk]),
        ):
            ref[:, c : c + chunk] = jnp.concatenate(split(value), 0)
    half = first_ref.shape[1]
    rows_ref[:, :half] = first_ref[...]
    rows_ref[:, half:] = second_ref[...]

    @pl.when(lax.axis_index("row") == 0)
    def _():
        rows_ref[:, :width] = rows_ref[:, :width] - band_ref[...].T


def four_products(left, right_ref, start, size):
    width = left.shape[1] // 2
    high = right_ref[:width, pl.ds(start, size)]
    low = right_ref[width:, pl.ds(start, size)]
    return fast(
        jnp.concatenate([left, left], 1), jnp.concatenate([high, high, low, low], 0)
    )


def near_kernel(rows_ref, right_ref, a_ref, out_ref, left_ref):
    rows, columns = a_ref.shape
    deep = block_of(rows, 512)
    for r in range(0, rows, deep):
        left_ref[r : r + deep, :] = jnp.concatenate(split(rows_ref[:, r : r + deep].T), 1)
    chunk = block_of(columns, 512)

    @pl.loop(0, columns // chunk)
    def _(i):
        c = pl.multiple_of(i * chunk, chunk)
        for r in range(0, rows, deep):
            out_ref[r : r + deep, pl.ds(c, chunk)] = a_ref[r : r + deep, pl.ds(c, chunk)] - (
                four_products(left_ref[r : r + deep, :], right_ref, c, chunk)
            )


def subtract_near(krt, right, a):
    rows, columns = a.shape
    width = krt.shape[0]
    whole = pl.BlockSpec(memory_space=pltpu.VMEM)
    return pl.pallas_call(
        near_kernel,
        in_specs=[whole] * 3,
        out_specs=whole,
        out_shape=shape(rows, columns),
        input_output_aliases={2: 0},
        scratch_shapes=[pltpu.VMEM((rows, 2 * width), bf16)],
        compiler_params=params(12),
        cost_estimate=cost(8 * rows * columns * width, 8 * rows * columns),
        name="subtract_near",
    )(krt, right, a)


def core_kernel(part_ref, more_ref, st_ref, krt_ref, out_ref):
    st = st_ref[...]
    cm = dot(dot(st, part_ref[...] + more_ref[...]), st.T)
    out_ref[...] = dot(cm, krt_ref[...])


def left_kernel(st_ref, core_ref, *refs):
    chunks, left_ref = refs[:-1], refs[-1]
    pieces = len(chunks)
    size = chunks[0].shape[1]
    st = st_ref[...]
    col = lax.axis_index("col")
    for at, ref in enumerate(chunks):
        start = pl.multiple_of(lax.rem(col + pieces - at, pieces) * size, size)
        value = dot(st, ref[...]) - core_ref[:, pl.ds(start, size)]
        left_ref[pl.ds(start, size), :] = jnp.concatenate(split(value.T), 1)


def far_kernel(left_ref, right_ref, a_ref, out_ref):
    columns = a_ref.shape[1]
    chunk = block_of(columns, 512)
    left = left_ref[...]
    for c in range(0, columns, chunk):
        out_ref[:, c : c + chunk] = a_ref[:, c : c + chunk] - four_products(
            left, right_ref, c, chunk
        )


def subtract_far(left, right, a):
    rows, columns = a.shape
    deep = left.shape[1]
    br = block_of(rows, 256)
    return pl.pallas_call(
        far_kernel,
        grid=(rows // br,),
        in_specs=[
            pl.BlockSpec((br, deep), lambda i: (i, 0)),
            pl.BlockSpec((deep, columns), lambda i: (0, 0)),
            pl.BlockSpec((br, columns), lambda i: (i, 0)),
        ],
        out_specs=pl.BlockSpec((br, columns), lambda i: (i, 0)),
        out_shape=shape(rows, columns),
        compiler_params=params(22),
        cost_estimate=cost(4 * rows * columns * deep, 8 * rows * columns),
        name="subtract_far",
    )(left, right, a)


def flip(value, bit, size, axis="row"):
    return lax.ppermute(value, axis, [(i, i ^ bit) for i in range(size)])


def from_sources(piece, col_size, source_flips, bit):
    pairs = []
    for c in range(col_size):
        for source in source_flips:
            for core in range(2):
                at = (2 * c + core) ^ source
                pairs.append((at * col_size + c, (at ^ bit) * col_size + c))
    return lax.ppermute(piece, ("row", "col"), pairs)


def shift(piece, by, size):
    return lax.ppermute(piece, "col", [(i, (i + by) % size) for i in range(size)])


def body_of(row_size, col_size):
    assert row_size == 2 * col_size

    def body(matrix, panel):
        rows, width = panel.shape
        columns = matrix.shape[1]
        small = shape(width, width)
        packed = shape(width, 2 * width)
        half = shape(width, rows // 2)
        first, second, partial = small_call(
            open_kernel, (half, half, packed), panel.T, flops=100_000_000, mib=12
        )
        partial = small_call(add_kernel, packed, partial, flip(partial, 1, row_size))
        if row_size == 8:
            terms = [partial] + [flip(partial, bit, row_size) for bit in (2, 4, 6)]
        else:
            bit = 2
            total = partial
            while bit < row_size // 2:
                total = total + flip(total, bit, row_size)
                bit *= 2
            zero = jnp.zeros_like(total)
            terms = [total, flip(total, row_size // 2, row_size), zero, zero]
        first, second, partial = lax.optimization_barrier((first, second, partial))
        raw, resident = product_down(first, second, matrix)
        if row_size == 8:
            by_x = from_sources(first, col_size, [0], 2)
            by_y = from_sources(second, col_size, [0], 4)
            one, two, resident = small_call(
                merge_first_kernel, (half, half), first, second, by_x, by_y, carry=resident
            )
            more_x = from_sources(two, col_size, [0, 4], 2)
            more_y = from_sources(one, col_size, [0, 2], 4)
        else:
            relation = (lax.axis_index("row") // 2) ^ lax.axis_index("col")
            held = jnp.where(relation == 0, jnp.concatenate([first, second], 1), 0.0)
            reached = [0]
            bit = 2
            while bit < row_size:
                held = held + from_sources(held, col_size, reached, bit)
                reached = reached + [r ^ bit for r in reached]
                bit *= 2
        band, again, band_inverse, head, resident = small_call(
            eliminate_kernel, (small, small, small, small), *terms, flops=50_000_000, carry=resident
        )
        keep, give, resident = fix_down(raw, again, resident)
        if row_size == 8:
            held, resident = small_call(
                join_kernel, shape(width, rows), one, more_y, two, more_x, carry=resident
            )
        other = flip(held, 1, row_size)
        quarter = shape(width, columns // 4)
        a, b, resident = small_call(
            halve_kernel, (quarter, quarter), keep, flip(give, 1, row_size), carry=resident
        )
        bits = []
        bit = 2
        while bit < row_size:
            bits.append(bit)
            bit *= 2
        for forward, backward in list(zip(bits, bits[::-1]))[:-1]:
            ra = flip(a, forward, row_size)
            rb = flip(b, backward, row_size)
            if bits[0] == forward:
                pieces = 1 if (rows // col_size) % 128 else col_size
                kct, *chunks, resident = product_across(held, other, again, resident, pieces)
            a, b, resident = small_call(
                pair_kernel, (quarter, quarter), a, ra, b, rb, carry=resident
            )
        ra, rb = flip(a, bits[-1], row_size), flip(b, bits[0], row_size)
        st, resident = small_call(
            invert_kernel, small, head, again, band_inverse, flops=50_000_000, carry=resident
        )
        summed, resident = small_call(
            join_kernel, shape(width, columns // 2), a, ra, b, rb, carry=resident
        )
        xct, inner, resident = small_call(
            inner_kernel,
            (shape(width, columns), small),
            kct,
            summed,
            flip(summed, 1, row_size),
            carry=resident,
        )
        bit = 1
        others = []
        while bit < col_size // 2:
            others.append(bit)
            bit *= 2
        first_inner = flip(inner, 1, col_size, "col")
        if pieces == 1:
            whole = [lax.psum(chunks[0], "col")]
        else:
            received = [shift(chunks[by], by, col_size) for by in range(1, col_size)]
            mine, resident = small_call(
                add_kernel, shape(width, rows // col_size), chunks[0], *received, carry=resident
            )
            whole = [mine] + [shift(mine, by, col_size) for by in range(1, col_size)]
        for at in others:
            got = first_inner if at == 1 else flip(inner, at, col_size, "col")
            inner, resident = small_call(add_kernel, small, inner, got, carry=resident)
        more = flip(inner, bit, col_size, "col")
        xparts, kparts, krt, resident = small_call(
            wide_kernel,
            (
                shape(2 * width, columns, dtype=bf16),
                shape(2 * width, columns, dtype=bf16),
                shape(width, rows),
            ),
            st,
            xct,
            kct,
            first,
            second,
            again,
            mib=12,
            carry=resident,
        )
        resident = subtract_near(krt, xparts, resident)
        core, resident = small_call(
            core_kernel, shape(width, rows), inner, more, st, krt, carry=resident
        )
        left, resident = small_call(
            left_kernel,
            shape(rows, 2 * width, dtype=bf16),
            st,
            core,
            *whole,
            mib=12,
            carry=resident,
        )
        return subtract_far(left, kparts, resident), band

    return body


def solution(mesh):
    body = body_of(mesh.shape["row"], mesh.shape["col"])

    return jax.shard_map(
        body,
        mesh=mesh,
        in_specs=(P("row", "col"), P("row", None)),
        out_specs=(P("row", "col"), P()),
        check_vma=False,
    )
```

```python
import jax
import jax.numpy as jnp
from jax import lax
from jax.experimental import pallas as pl
from jax.experimental.pallas import tpu as pltpu
from jax.sharding import PartitionSpec as P


precise = lax.Precision.HIGHEST
f32 = jnp.float32
bf16 = jnp.bfloat16


def shape(*dims, dtype=f32):
    return jax.ShapeDtypeStruct(dims, dtype)


def params(mib):
    return pltpu.CompilerParams(vmem_limit_bytes=mib * 1024 * 1024)


def cost(flops, moved):
    return pl.CostEstimate(flops=flops, bytes_accessed=moved, transcendentals=0)


def dot(a, b):
    return jnp.dot(a, b, precision=precise, preferred_element_type=f32)


def fast(a, b):
    return jnp.dot(a, b, preferred_element_type=f32)


def split(value):
    high = value.astype(bf16)
    return high, (value - high.astype(f32)).astype(bf16)


def block_of(size, wanted):
    while size % wanted:
        wanted //= 2
    return wanted


def small_call(kernel, out, *operands, carry=None, flops=1_000_000, moved=1_000_000, mib=8):
    extra = {}
    body = kernel
    if carry is not None:
        outs = out if isinstance(out, tuple) else (out,)
        count = len(operands)
        anywhere = pl.BlockSpec(memory_space=pl.ANY)
        whole = pl.BlockSpec(memory_space=pltpu.VMEM)
        extra = dict(
            in_specs=[whole] * count + [anywhere],
            out_specs=(whole,) * len(outs) + (anywhere,),
            input_output_aliases={count: len(outs)},
        )
        operands = operands + (carry,)
        out = outs + (shape(*carry.shape),)

        def body(*refs):
            kernel(*refs[:count], *refs[count + 1 : -1])

    return pl.pallas_call(
        body, out_shape=out, compiler_params=params(mib), cost_estimate=cost(flops, moved), **extra
    )(*operands)


def open_kernel(turned_ref, first_ref, second_ref, packed_ref):
    width = turned_ref.shape[0]
    half = first_ref.shape[1]
    turned = turned_ref[...]
    first_ref[...] = turned[:, :half]
    second_ref[...] = turned[:, half:]
    gram = lax.dot_general(
        turned, turned, (((1,), (1,)), ((), ())), precision=precise, preferred_element_type=f32
    )
    head = jnp.where(lax.axis_index("row") == 0, turned[:, : 2 * width].T[:width], 0.0)
    packed_ref[...] = jnp.concatenate([gram, head], 1)


def add_cores_kernel(first_ref, second_ref, a_ref, b_ref, x_ref, y_ref, sum_ref):
    half = first_ref.shape[1]
    total = a_ref[...] + b_ref[...]
    sum_ref[...] = total
    for source, target in ((first_ref, x_ref), (second_ref, y_ref)):
        target[:, :half] = source[...]
        target[:, half:] = total


def add_kernel(*refs):
    total = refs[0][...]
    for ref in refs[1:-1]:
        total = total + ref[...]
    refs[-1][...] = total


def spread(tile, at):
    return jnp.broadcast_to(tile[at : at + 1, :], tile.shape)


def pick(tile, at):
    return jnp.broadcast_to(tile[:, at : at + 1], tile.shape)


def sweep(tiles, order, full):
    lane = lax.broadcasted_iota(jnp.int32, (8, order), 1)
    sub = lax.broadcasted_iota(jnp.int32, (8, order), 0)
    tiles = list(tiles)
    for at in range(order // 8):
        base = 8 * at
        inside = (lane >= base) & (lane < base + 8)
        tile = tiles[at]
        others = [t for t in range(order // 8) if (t != at if full else t > at)]
        picked = {t: [pick(tiles[t], base + q) for q in range(8)] for t in others}
        columns = [pick(tile, base + q) for q in range(8)]
        rows = jnp.where(inside, jnp.where(lane - base == sub, 1.0, 0.0), tile)
        lower, upper = rows, tile
        for q in range(8):
            here = sub == q
            inverse = 1.0 / spread(columns[q], q)
            scaled = spread(rows, q) * inverse
            if not full:
                lower = jnp.where(here, rows, lower)
                upper = jnp.where(
                    sub > q, upper - columns[q] * (spread(upper, q) * inverse), upper
                )
            rows = jnp.where(here, scaled, rows - columns[q] * scaled)
            for p in range(q + 1, 8):
                part = spread(columns[p], q) * inverse
                columns[p] = jnp.where(here, part, columns[p] - columns[q] * part)
        finals = [spread(rows, q) for q in range(8)]
        for t in others:
            value = jnp.where(inside, 0.0, tiles[t])
            for q in range(8):
                value = value - picked[t][q] * finals[q]
            tiles[t] = value
        tiles[at] = rows if full else jnp.where(inside & (lane - base >= sub), upper, lower)
    return tiles


def eliminate_kernel(a_ref, b_ref, c_ref, d_ref, band_ref, again_ref, inverse_ref, head_ref):
    order = band_ref.shape[0]
    lane = lax.broadcasted_iota(jnp.int32, (8, order), 1)
    sub = lax.broadcasted_iota(jnp.int32, (8, order), 0)
    skip = b_ref.shape[1] - a_ref.shape[1]
    total = (a_ref[...] + b_ref[:, skip:]) + (c_ref[:, skip:] + d_ref[...])
    head_ref[...] = total[:, order:]
    gram = total[:, :order]
    tiles = sweep([gram[8 * t : 8 * t + 8, :] for t in range(order // 8)], order, False)
    for t in range(order // 8):
        row_at = sub + 8 * t
        diagonal = jnp.sum(jnp.where(lane == row_at, tiles[t], 0.0), axis=1, keepdims=True)
        length = jnp.sqrt(diagonal)
        scaled = tiles[t] / length
        band = jnp.where(lane > row_at, -scaled, jnp.where(lane == row_at, -length, 0.0))
        band_ref[8 * t : 8 * t + 8, :] = band
        again_ref[8 * t : 8 * t + 8, :] = band
        inverse_ref[8 * t : 8 * t + 8, :] = jnp.where(
            lane < row_at, -scaled, jnp.where(lane == row_at, -1.0 / length, 0.0)
        )


def invert_kernel(head_ref, band_ref, inverse_ref, out_ref):
    order = head_ref.shape[0]
    tiles = [
        head_ref[8 * t : 8 * t + 8, :] - band_ref[8 * t : 8 * t + 8, :] for t in range(order // 8)
    ]
    tiles = sweep(tiles, order, True)
    out_ref[...] = -dot(jnp.concatenate(tiles, 0), inverse_ref[...])


def down_kernel(first_ref, second_ref, a_ref, out_ref, kept_ref, sems):
    width = first_ref.shape[0]
    columns = a_ref.shape[1]
    count = sems.shape[0]
    size = columns // count

    def load(i):
        part = pl.ds(pl.multiple_of(i * size, size), size)
        return pltpu.make_async_copy(a_ref.at[:, part], kept_ref.at[:, part], sems.at[i])

    for i in range(count):
        load(i).start()
    kh, kl = split(jnp.concatenate([first_ref[...], second_ref[...]], 1))
    left = jnp.concatenate([kh, kl], 0)

    @pl.loop(0, count)
    def _(i):
        load(i).wait()
        part = pl.ds(pl.multiple_of(i * size, size), size)
        ah, al = split(kept_ref[:, part])
        term = fast(left, ah) + fast(left, al)
        out_ref[:, part] = term[:width] + term[width:]


def product_down(first, second, a):
    rows, columns = a.shape
    width = first.shape[0]
    size = block_of(columns, 256)
    whole = pl.BlockSpec(memory_space=pltpu.VMEM)
    return pl.pallas_call(
        down_kernel,
        in_specs=[whole, whole, pl.BlockSpec(memory_space=pltpu.HBM)],
        out_specs=(whole, whole),
        out_shape=(shape(width, columns), shape(rows, columns)),
        scratch_shapes=[pltpu.SemaphoreType.DMA((columns // size,))],
        compiler_params=params(12),
        cost_estimate=cost(8 * rows * columns * width, 4 * rows * columns),
        name="product_down",
    )(first, second, pltpu.with_memory_space_constraint(a, pltpu.HBM))


def fix_kernel(raw_ref, band_ref, top_ref, keep_ref, give_ref, _):
    half = keep_ref.shape[1]
    row = lax.axis_index("row")
    core = lax.rem(row, 2)
    first, second = raw_ref[:, :half], raw_ref[:, half:]

    @pl.when(row == 0)
    def _():
        turned = band_ref[...].T
        keep_ref[...] = first - dot(turned, top_ref[:, :half])
        give_ref[...] = second - dot(turned, top_ref[:, half:])

    @pl.when((row != 0) & (core == 0))
    def _():
        keep_ref[...] = first
        give_ref[...] = second

    @pl.when(core == 1)
    def _():
        keep_ref[...] = second
        give_ref[...] = first


def fix_down(raw, band, a):
    width, columns = raw.shape
    half = shape(width, columns // 2)
    whole = pl.BlockSpec((width, columns), lambda i: (0, 0))
    halves = pl.BlockSpec((width, columns // 2), lambda i: (0, 0))
    return pl.pallas_call(
        fix_kernel,
        grid=(1,),
        in_specs=[whole, pl.BlockSpec((width, width), lambda i: (0, 0)), whole],
        out_specs=(halves, halves, pl.BlockSpec(memory_space=pl.ANY)),
        out_shape=(half, half, shape(*a.shape)),
        input_output_aliases={2: 2},
        compiler_params=params(12),
        cost_estimate=cost(12 * width * width * columns, 16 * width * columns),
        name="fix_down",
    )(raw, band, a)


def rows_product(right_ref, a_ref, outs):
    columns = a_ref.shape[1]
    width = right_ref.shape[1] // 2
    chunk = block_of(columns, 512)
    total = None
    for c in range(0, columns, chunk):
        ah, al = split(a_ref[:, c : c + chunk])
        right = right_ref[c : c + chunk, :]
        term = fast(ah, right) + fast(al, right)
        total = term if total is None else total + term
    result = (total[:, :width] + total[:, width:]).T
    for at, out_ref in enumerate(outs):

        @pl.when(pl.program_id(0) == at)
        def _():
            out_ref[...] = result


def across_kernel(held_ref, other_ref, band_ref, a_ref, kct_ref, right_ref, *refs):
    width, half = held_ref.shape
    columns = a_ref.shape[1]
    chunk = block_of(columns, 512)

    @pl.when(pl.program_id(0) == 0)
    def _():
        core = lax.rem(lax.axis_index("row"), 2)

        @pl.when(core == 0)
        def _():
            kct_ref[:, :half] = held_ref[...]
            kct_ref[:, half:] = other_ref[...]

        @pl.when(core == 1)
        def _():
            kct_ref[:, :half] = other_ref[...]
            kct_ref[:, half:] = held_ref[...]

        @pl.when(lax.axis_index("col") == 0)
        def _():
            kct_ref[:, :width] = kct_ref[:, :width] - band_ref[...].T

        for c in range(0, columns, chunk):
            right_ref[c : c + chunk, :] = jnp.concatenate(split(kct_ref[:, c : c + chunk].T), 1)

    rows_product(right_ref, a_ref, refs[:-1])


def more_kernel(right_ref, a_ref, *refs):
    rows_product(right_ref, a_ref, refs[:-1])


def across_call(kernel, operands, extra, a, pieces, start, count, width):
    rows, columns = a.shape
    size = rows // pieces

    def turn(i):
        return (lax.rem(i + start + lax.axis_index("col"), pieces), 0)

    def fixed(array):
        return pl.BlockSpec(array.shape, lambda i: (0, 0))

    one = shape(width, size)
    outs = tuple(extra) + (one,) * count
    return pl.pallas_call(
        kernel,
        grid=(count,),
        in_specs=[fixed(x) for x in operands] + [pl.BlockSpec((size, columns), turn)],
        out_specs=tuple(fixed(x) for x in outs) + (pl.BlockSpec(memory_space=pl.ANY),),
        out_shape=outs + (shape(rows, columns),),
        input_output_aliases={len(operands): len(outs)},
        compiler_params=params(22),
        cost_estimate=cost(8 * size * count * columns * width, 4 * size * count * columns),
    )(*operands, a)


def merge_first_kernel(first_ref, second_ref, by_x_ref, by_y_ref, a_ref, b_ref):
    half = a_ref.shape[1]
    relation = lax.div(lax.axis_index("row"), 2) ^ lax.axis_index("col")
    for at, own, got, out in (
        (1, first_ref, by_x_ref, a_ref),
        (2, second_ref, by_y_ref, b_ref),
    ):
        out[...] = jnp.where(
            relation == 0, own[...], jnp.where(relation == at, got[:, :half], 0.0)
        )


def join_kernel(a_ref, b_ref, c_ref, d_ref, out_ref):
    half = a_ref.shape[1]
    out_ref[:, :half] = a_ref[...] + b_ref[...]
    out_ref[:, half:] = c_ref[...] + d_ref[...]


def halve_kernel(keep_ref, other_ref, a_ref, b_ref):
    half = a_ref.shape[1]
    a_ref[...] = keep_ref[:, :half] + other_ref[:, :half]
    b_ref[...] = keep_ref[:, half:] + other_ref[:, half:]


def pair_kernel(a_ref, b_ref, c_ref, d_ref, e_ref, f_ref):
    e_ref[...] = a_ref[...] + b_ref[...]
    f_ref[...] = c_ref[...] + d_ref[...]


def inner_kernel(kct_ref, held_ref, other_ref, xct_ref, inner_ref):
    half = held_ref.shape[1]
    core = lax.rem(lax.axis_index("row"), 2)

    @pl.when(core == 0)
    def _():
        xct_ref[:, :half] = held_ref[...]
        xct_ref[:, half:] = other_ref[...]

    @pl.when(core == 1)
    def _():
        xct_ref[:, :half] = other_ref[...]
        xct_ref[:, half:] = held_ref[...]

    inner_ref[...] = lax.dot_general(
        kct_ref[...],
        xct_ref[...],
        (((1,), (1,)), ((), ())),
        precision=precise,
        preferred_element_type=f32,
    )


def wide_kernel(st_ref, xct_ref, kct_ref, first_ref, second_ref, band_ref, x_ref, k_ref, rows_ref):
    width, columns = kct_ref.shape
    st = st_ref[...]
    chunk = block_of(columns, 512)
    for c in range(0, columns, chunk):
        for ref, value in (
            (x_ref, dot(st, xct_ref[:, c : c + chunk])),
            (k_ref, kct_ref[:, c : c + chunk]),
        ):
            ref[:, c : c + chunk] = jnp.concatenate(split(value), 0)
    half = first_ref.shape[1]
    rows_ref[:, :half] = first_ref[...]
    rows_ref[:, half:] = second_ref[...]

    @pl.when(lax.axis_index("row") == 0)
    def _():
        rows_ref[:, :width] = rows_ref[:, :width] - band_ref[...].T


def four_products(left, right_ref, start, size):
    width = left.shape[1] // 2
    high = right_ref[:width, pl.ds(start, size)]
    low = right_ref[width:, pl.ds(start, size)]
    return fast(
        jnp.concatenate([left, left], 1), jnp.concatenate([high, high, low, low], 0)
    )


def near_kernel(rows_ref, right_ref, a_ref, out_ref, left_ref):
    rows, columns = a_ref.shape
    deep = block_of(rows, 512)
    for r in range(0, rows, deep):
        left_ref[r : r + deep, :] = jnp.concatenate(split(rows_ref[:, r : r + deep].T), 1)
    chunk = block_of(columns, 512)

    @pl.loop(0, columns // chunk)
    def _(i):
        c = pl.multiple_of(i * chunk, chunk)
        for r in range(0, rows, deep):
            out_ref[r : r + deep, pl.ds(c, chunk)] = a_ref[r : r + deep, pl.ds(c, chunk)] - (
                four_products(left_ref[r : r + deep, :], right_ref, c, chunk)
            )


def subtract_near(krt, right, a):
    rows, columns = a.shape
    width = krt.shape[0]
    whole = pl.BlockSpec(memory_space=pltpu.VMEM)
    return pl.pallas_call(
        near_kernel,
        in_specs=[whole] * 3,
        out_specs=whole,
        out_shape=shape(rows, columns),
        input_output_aliases={2: 0},
        scratch_shapes=[pltpu.VMEM((rows, 2 * width), bf16)],
        compiler_params=params(12),
        cost_estimate=cost(8 * rows * columns * width, 8 * rows * columns),
        name="subtract_near",
    )(krt, right, a)


def core_kernel(part_ref, more_ref, st_ref, krt_ref, out_ref):
    st = st_ref[...]
    cm = dot(dot(st, part_ref[...] + more_ref[...]), st.T)
    out_ref[...] = dot(cm, krt_ref[...])


def left_kernel(st_ref, core_ref, *refs):
    chunks, left_ref = refs[:-1], refs[-1]
    pieces = len(chunks)
    size = chunks[0].shape[1]
    st = st_ref[...]
    col = lax.axis_index("col")
    for at, ref in enumerate(chunks):
        start = pl.multiple_of(lax.rem(col + pieces - at, pieces) * size, size)
        value = dot(st, ref[...]) - core_ref[:, pl.ds(start, size)]
        left_ref[pl.ds(start, size), :] = jnp.concatenate(split(value.T), 1)


def far_kernel(left_ref, right_ref, a_ref, out_ref, buffer, sems):
    rows, columns = a_ref.shape
    slots, deep, wide = buffer.shape
    down, along = rows // deep, columns // wide
    count = down * along

    def place(i):
        return (
            pl.multiple_of(lax.rem(i, down) * deep, deep),
            pl.multiple_of(lax.div(i, down) * wide, wide),
        )

    def store(i, slot):
        r, c = place(i)
        return pltpu.make_async_copy(
            buffer.at[slot], out_ref.at[pl.ds(r, deep), pl.ds(c, wide)], sems.at[slot]
        )

    @pl.loop(0, count)
    def _(i):
        slot = lax.rem(i, slots)

        @pl.when(i >= slots)
        def _():
            store(i - slots, slot).wait()

        r, c = place(i)
        buffer[slot] = a_ref[pl.ds(r, deep), pl.ds(c, wide)] - four_products(
            left_ref[pl.ds(r, deep), :], right_ref, c, wide
        )
        store(i, slot).start()

    for back in range(slots, 0, -1):
        store(count - back, (count - back) % slots).wait()


def subtract_far(left, right, a):
    rows, columns = a.shape
    deep = left.shape[1]
    whole = pl.BlockSpec(memory_space=pltpu.VMEM)
    wide = columns if (columns // 4) % 128 else columns // 4
    piece = (block_of(rows, 512), wide)
    return pl.pallas_call(
        far_kernel,
        in_specs=[whole] * 3,
        out_specs=pl.BlockSpec(memory_space=pltpu.HBM),
        out_shape=shape(rows, columns),
        scratch_shapes=[pltpu.VMEM((3,) + piece, f32), pltpu.SemaphoreType.DMA((3,))],
        compiler_params=params(12),
        cost_estimate=cost(4 * rows * columns * deep, 8 * rows * columns),
        name="subtract_far",
    )(left, right, a)


def flip(value, bit, size, axis="row"):
    return lax.ppermute(value, axis, [(i, i ^ bit) for i in range(size)])


def from_sources(piece, col_size, source_flips, bit):
    pairs = []
    for c in range(col_size):
        for source in source_flips:
            for core in range(2):
                at = (2 * c + core) ^ source
                pairs.append((at * col_size + c, (at ^ bit) * col_size + c))
    return lax.ppermute(piece, ("row", "col"), pairs)


def shift(piece, by, size):
    return lax.ppermute(piece, "col", [(i, (i + by) % size) for i in range(size)])


def body_of(row_size, col_size):
    assert row_size == 2 * col_size

    def body(matrix, panel):
        rows, width = panel.shape
        columns = matrix.shape[1]
        small = shape(width, width)
        packed = shape(width, 2 * width)
        half = shape(width, rows // 2)
        first, second, partial = small_call(
            open_kernel, (half, half, packed), panel.T, flops=100_000_000, mib=12
        )
        apart = flip(partial, 1, row_size)
        if row_size == 8:
            wide_half = shape(width, rows // 2 + 2 * width)
            send_x, send_y, partial = small_call(
                add_cores_kernel, (wide_half, wide_half, packed), first, second, partial, apart
            )
            by_x = flip(send_x, 2, row_size)
            by_y = flip(send_y, 4, row_size)
            terms = [partial, by_x, by_y, flip(partial, 6, row_size)]
        else:
            partial = small_call(add_kernel, packed, partial, apart)
            bit = 2
            total = partial
            while bit < row_size // 2:
                total = total + flip(total, bit, row_size)
                bit *= 2
            zero = jnp.zeros_like(total)
            terms = [total, flip(total, row_size // 2, row_size), zero, zero]
        first, second, partial = lax.optimization_barrier((first, second, partial))
        raw, resident = product_down(first, second, matrix)
        if row_size == 8:
            one, two, resident = small_call(
                merge_first_kernel, (half, half), first, second, by_x, by_y, carry=resident
            )
            more_x = from_sources(two, col_size, [0, 4], 2)
            more_y = from_sources(one, col_size, [0, 2], 4)
        else:
            relation = (lax.axis_index("row") // 2) ^ lax.axis_index("col")
            held = jnp.where(relation == 0, jnp.concatenate([first, second], 1), 0.0)
            reached = [0]
            bit = 2
            while bit < row_size:
                held = held + from_sources(held, col_size, reached, bit)
                reached = reached + [r ^ bit for r in reached]
                bit *= 2
        band, again, band_inverse, head, resident = small_call(
            eliminate_kernel, (small, small, small, small), *terms, flops=50_000_000, carry=resident
        )
        keep, give, resident = fix_down(raw, again, resident)
        quarter = shape(width, columns // 4)
        a, b, resident = small_call(
            halve_kernel, (quarter, quarter), keep, flip(give, 1, row_size), carry=resident
        )
        if row_size == 8:
            held, resident = small_call(
                join_kernel, shape(width, rows), one, more_y, two, more_x, carry=resident
            )
        other = flip(held, 1, row_size)
        bits = []
        bit = 2
        while bit < row_size:
            bits.append(bit)
            bit *= 2
        pieces = 1 if (rows // col_size) % 128 else col_size
        late = pieces // 2
        for forward, backward in list(zip(bits, bits[::-1]))[:-1]:
            ra = flip(a, forward, row_size)
            rb = flip(b, backward, row_size)
            if bits[0] == forward:
                kct, right, *chunks, resident = across_call(
                    across_kernel,
                    (held, other, again),
                    (shape(width, columns), shape(columns, 2 * width, dtype=bf16)),
                    resident,
                    pieces,
                    late,
                    pieces - late,
                    width,
                )
            a, b, resident = small_call(
                pair_kernel, (quarter, quarter), a, ra, b, rb, carry=resident
            )
        ra = flip(a, bits[-1], row_size)
        rb = flip(b, bits[0], row_size)
        if late:
            received = [shift(chunks[at], late + at, col_size) for at in range(pieces - late)]
            *chunks, resident = across_call(
                more_kernel, (right,), (), resident, pieces, 0, late, width
            )
            received += [shift(chunks[by], by, col_size) for by in range(1, late)]
        summed, resident = small_call(
            join_kernel, shape(width, columns // 2), a, ra, b, rb, carry=resident
        )
        xct, inner, resident = small_call(
            inner_kernel,
            (shape(width, columns), small),
            kct,
            summed,
            flip(summed, 1, row_size),
            carry=resident,
        )
        bit = 1
        others = []
        while bit < col_size // 2:
            others.append(bit)
            bit *= 2
        first_inner = flip(inner, 1, col_size, "col")
        if pieces == 1:
            whole = [lax.psum(chunks[0], "col")]
        else:
            mine, resident = small_call(
                add_kernel, shape(width, rows // col_size), chunks[0], *received, carry=resident
            )
            whole = [mine] + [shift(mine, by, col_size) for by in range(1, col_size)]
        for at in others:
            got = first_inner if at == 1 else flip(inner, at, col_size, "col")
            inner, resident = small_call(add_kernel, small, inner, got, carry=resident)
        more = flip(inner, bit, col_size, "col")
        st, resident = small_call(
            invert_kernel, small, head, again, band_inverse, flops=50_000_000, carry=resident
        )
        xparts, kparts, krt, resident = small_call(
            wide_kernel,
            (
                shape(2 * width, columns, dtype=bf16),
                shape(2 * width, columns, dtype=bf16),
                shape(width, rows),
            ),
            st,
            xct,
            kct,
            first,
            second,
            again,
            mib=12,
            carry=resident,
        )
        resident = subtract_near(krt, xparts, resident)
        core, resident = small_call(
            core_kernel, shape(width, rows), inner, more, st, krt, carry=resident
        )
        left, resident = small_call(
            left_kernel,
            shape(rows, 2 * width, dtype=bf16),
            st,
            core,
            *whole,
            mib=12,
            carry=resident,
        )
        return subtract_far(left, kparts, resident), band

    return body


def solution(mesh):
    body = body_of(mesh.shape["row"], mesh.shape["col"])

    return jax.shard_map(
        body,
        mesh=mesh,
        in_specs=(P("row", "col"), P("row", None)),
        out_specs=(P("row", "col"), P()),
        check_vma=False,
    )
```

```python
import jax
import jax.numpy as jnp
from jax import lax
from jax.experimental import pallas as pl
from jax.experimental.pallas import tpu as pltpu
from jax.sharding import PartitionSpec as P


precise = lax.Precision.HIGHEST
f32 = jnp.float32
bf16 = jnp.bfloat16


def shape(*dims, dtype=f32):
    return jax.ShapeDtypeStruct(dims, dtype)


def params(mib):
    return pltpu.CompilerParams(vmem_limit_bytes=mib * 1024 * 1024)


def cost(flops, moved):
    return pl.CostEstimate(flops=flops, bytes_accessed=moved, transcendentals=0)


def dot(a, b):
    return jnp.dot(a, b, precision=precise, preferred_element_type=f32)


def fast(a, b):
    return jnp.dot(a, b, preferred_element_type=f32)


def split(value):
    high = value.astype(bf16)
    return high, (value - high.astype(f32)).astype(bf16)


def block_of(size, wanted):
    while size % wanted:
        wanted //= 2
    return wanted


def small_call(kernel, out, *operands, carry=(), flops=1_000_000, moved=1_000_000, mib=8):
    extra = {}
    body = kernel
    if carry:
        outs = out if isinstance(out, tuple) else (out,)
        count, more = len(operands), len(carry)
        anywhere = pl.BlockSpec(memory_space=pl.ANY)
        whole = pl.BlockSpec(memory_space=pltpu.VMEM)
        extra = dict(
            in_specs=[whole] * count + [anywhere] * more,
            out_specs=(whole,) * len(outs) + (anywhere,) * more,
            input_output_aliases={count + k: len(outs) + k for k in range(more)},
        )
        operands = operands + tuple(carry)
        out = outs + tuple(shape(*x.shape) for x in carry)

        def body(*refs):
            kernel(*refs[:count], *refs[count + more : -more])

    result = pl.pallas_call(
        body, out_shape=out, compiler_params=params(mib), cost_estimate=cost(flops, moved), **extra
    )(*operands)
    if carry:
        return tuple(result[: -len(carry)]) + (tuple(result[-len(carry) :]),)
    return result


def open_kernel(turned_ref, first_ref, second_ref, packed_ref):
    width = turned_ref.shape[0]
    half = first_ref.shape[1]
    turned = turned_ref[...]
    first_ref[...] = turned[:, :half]
    second_ref[...] = turned[:, half:]
    gram = lax.dot_general(
        turned, turned, (((1,), (1,)), ((), ())), precision=precise, preferred_element_type=f32
    )
    head = jnp.where(lax.axis_index("row") == 0, turned[:, : 2 * width].T[:width], 0.0)
    packed_ref[...] = jnp.concatenate([gram, head], 1)


def add_cores_kernel(first_ref, second_ref, a_ref, b_ref, x_ref, y_ref, sum_ref):
    half = first_ref.shape[1]
    total = a_ref[...] + b_ref[...]
    sum_ref[...] = total
    for source, target in ((first_ref, x_ref), (second_ref, y_ref)):
        target[:, :half] = source[...]
        target[:, half:] = total


def add_kernel(*refs):
    total = refs[0][...]
    for ref in refs[1:-1]:
        total = total + ref[...]
    refs[-1][...] = total


def spread(tile, at):
    return jnp.broadcast_to(tile[at : at + 1, :], tile.shape)


def pick(tile, at):
    return jnp.broadcast_to(tile[:, at : at + 1], tile.shape)


def sweep(tiles, order, full):
    lane = lax.broadcasted_iota(jnp.int32, (8, order), 1)
    sub = lax.broadcasted_iota(jnp.int32, (8, order), 0)
    tiles = list(tiles)
    for at in range(order // 8):
        base = 8 * at
        inside = (lane >= base) & (lane < base + 8)
        tile = tiles[at]
        others = [t for t in range(order // 8) if (t != at if full else t > at)]
        picked = {t: [pick(tiles[t], base + q) for q in range(8)] for t in others}
        columns = [pick(tile, base + q) for q in range(8)]
        rows = jnp.where(inside, jnp.where(lane - base == sub, 1.0, 0.0), tile)
        lower, upper = rows, tile
        for q in range(8):
            here = sub == q
            inverse = 1.0 / spread(columns[q], q)
            scaled = spread(rows, q) * inverse
            if not full:
                lower = jnp.where(here, rows, lower)
                upper = jnp.where(
                    sub > q, upper - columns[q] * (spread(upper, q) * inverse), upper
                )
            rows = jnp.where(here, scaled, rows - columns[q] * scaled)
            for p in range(q + 1, 8):
                part = spread(columns[p], q) * inverse
                columns[p] = jnp.where(here, part, columns[p] - columns[q] * part)
        finals = [spread(rows, q) for q in range(8)]
        for t in others:
            value = jnp.where(inside, 0.0, tiles[t])
            for q in range(8):
                value = value - picked[t][q] * finals[q]
            tiles[t] = value
        tiles[at] = rows if full else jnp.where(inside & (lane - base >= sub), upper, lower)
    return tiles


def eliminate_kernel(a_ref, b_ref, c_ref, d_ref, band_ref, again_ref, inverse_ref, head_ref):
    order = band_ref.shape[0]
    lane = lax.broadcasted_iota(jnp.int32, (8, order), 1)
    sub = lax.broadcasted_iota(jnp.int32, (8, order), 0)
    skip = b_ref.shape[1] - a_ref.shape[1]
    total = (a_ref[...] + b_ref[:, skip:]) + (c_ref[:, skip:] + d_ref[...])
    head_ref[...] = total[:, order:]
    gram = total[:, :order]
    tiles = sweep([gram[8 * t : 8 * t + 8, :] for t in range(order // 8)], order, False)
    for t in range(order // 8):
        row_at = sub + 8 * t
        diagonal = jnp.sum(jnp.where(lane == row_at, tiles[t], 0.0), axis=1, keepdims=True)
        length = jnp.sqrt(diagonal)
        scaled = tiles[t] / length
        band = jnp.where(lane > row_at, -scaled, jnp.where(lane == row_at, -length, 0.0))
        band_ref[8 * t : 8 * t + 8, :] = band
        again_ref[8 * t : 8 * t + 8, :] = band
        inverse_ref[8 * t : 8 * t + 8, :] = jnp.where(
            lane < row_at, -scaled, jnp.where(lane == row_at, -1.0 / length, 0.0)
        )


def invert_kernel(head_ref, band_ref, inverse_ref, out_ref):
    order = head_ref.shape[0]
    tiles = [
        head_ref[8 * t : 8 * t + 8, :] - band_ref[8 * t : 8 * t + 8, :] for t in range(order // 8)
    ]
    tiles = sweep(tiles, order, True)
    out_ref[...] = -dot(jnp.concatenate(tiles, 0), inverse_ref[...])


def down_kernel(base, first_ref, second_ref, a_ref, out_ref, kept_ref, sems):
    width = first_ref.shape[0]
    count = sems.shape[0]
    size = out_ref.shape[1] // count

    def load(i):
        start = pl.multiple_of(i * size, size)
        source = a_ref.at[:, pl.ds(pl.multiple_of(base + start, size), size)]
        return pltpu.make_async_copy(source, kept_ref.at[:, pl.ds(start, size)], sems.at[i])

    for i in range(count):
        load(i).start()
    kh, kl = split(jnp.concatenate([first_ref[...], second_ref[...]], 1))
    left = jnp.concatenate([kh, kl], 0)

    @pl.loop(0, count)
    def _(i):
        load(i).wait()
        part = pl.ds(pl.multiple_of(i * size, size), size)
        ah, al = split(kept_ref[:, part])
        term = fast(left, ah) + fast(left, al)
        out_ref[:, part] = term[:width] + term[width:]


def product_down(first, second, a, at, carry=()):
    rows, columns = a.shape
    width = first.shape[0]
    span = columns // 2
    size = block_of(span, 256)
    whole = pl.BlockSpec(memory_space=pltpu.VMEM)
    anywhere = pl.BlockSpec(memory_space=pl.ANY)
    more = len(carry)

    def kernel(first_ref, second_ref, a_ref, *refs):
        out_ref, kept_ref = refs[more : more + 2]
        down_kernel(at * span, first_ref, second_ref, a_ref, out_ref, kept_ref, refs[-1])

    out, kept, *carried = pl.pallas_call(
        kernel,
        in_specs=[whole, whole, pl.BlockSpec(memory_space=pltpu.HBM)] + [anywhere] * more,
        out_specs=(whole, whole) + (anywhere,) * more,
        out_shape=(shape(width, span), shape(rows, span)) + tuple(shape(*x.shape) for x in carry),
        input_output_aliases={3 + k: 2 + k for k in range(more)},
        scratch_shapes=[pltpu.SemaphoreType.DMA((span // size,))],
        compiler_params=params(12),
        cost_estimate=cost(8 * rows * span * width, 4 * rows * span),
    )(first, second, pltpu.with_memory_space_constraint(a, pltpu.HBM), *carry)
    return out, tuple(carried) + (kept,)


def fix_kernel(low_ref, high_ref, band_ref, top_ref, over_ref, keep_ref, give_ref, *_):
    row = lax.axis_index("row")
    core = lax.rem(row, 2)
    first, second = low_ref[...], high_ref[...]

    @pl.when(row == 0)
    def _():
        turned = band_ref[...].T
        keep_ref[...] = first - dot(turned, top_ref[...])
        give_ref[...] = second - dot(turned, over_ref[...])

    @pl.when((row != 0) & (core == 0))
    def _():
        keep_ref[...] = first
        give_ref[...] = second

    @pl.when(core == 1)
    def _():
        keep_ref[...] = second
        give_ref[...] = first


def fix_down(low, high, band, halves):
    width, span = low.shape
    part = pl.BlockSpec((width, span), lambda i: (0, 0))
    anywhere = pl.BlockSpec(memory_space=pl.ANY)
    keep, give, *halves = pl.pallas_call(
        fix_kernel,
        grid=(1,),
        in_specs=[part, part, pl.BlockSpec((width, width), lambda i: (0, 0)), part, part],
        out_specs=(part, part, anywhere, anywhere),
        out_shape=(shape(width, span),) * 2 + tuple(shape(*x.shape) for x in halves),
        input_output_aliases={3: 2, 4: 3},
        compiler_params=params(12),
        cost_estimate=cost(24 * width * width * span, 32 * width * span),
        name="fix_down",
    )(low, high, band, *halves)
    return keep, give, tuple(halves)


def rows_product(right_ref, halves, outs):
    span = halves[0].shape[1]
    width = right_ref.shape[1] // 2
    chunk = block_of(span, 512)
    total = None
    for at, a_ref in enumerate(halves):
        for c in range(0, span, chunk):
            ah, al = split(a_ref[:, c : c + chunk])
            right = right_ref[at * span + c : at * span + c + chunk, :]
            term = fast(ah, right) + fast(al, right)
            total = term if total is None else total + term
    result = (total[:, :width] + total[:, width:]).T
    for at, out_ref in enumerate(outs):

        @pl.when(pl.program_id(0) == at)
        def _():
            out_ref[...] = result


def across_kernel(held_ref, other_ref, band_ref, low_ref, high_ref, kct_ref, right_ref, *refs):
    width, half = held_ref.shape
    columns = 2 * half
    chunk = block_of(columns, 512)

    @pl.when(pl.program_id(0) == 0)
    def _():
        core = lax.rem(lax.axis_index("row"), 2)

        @pl.when(core == 0)
        def _():
            kct_ref[:, :half] = held_ref[...]
            kct_ref[:, half:] = other_ref[...]

        @pl.when(core == 1)
        def _():
            kct_ref[:, :half] = other_ref[...]
            kct_ref[:, half:] = held_ref[...]

        @pl.when(lax.axis_index("col") == 0)
        def _():
            kct_ref[:, :width] = kct_ref[:, :width] - band_ref[...].T

        for c in range(0, columns, chunk):
            right_ref[c : c + chunk, :] = jnp.concatenate(split(kct_ref[:, c : c + chunk].T), 1)

    rows_product(right_ref, (low_ref, high_ref), refs[:-2])


def more_kernel(right_ref, low_ref, high_ref, *refs):
    rows_product(right_ref, (low_ref, high_ref), refs[:-2])


def across_call(kernel, operands, extra, halves, pieces, start, count, width):
    rows, span = halves[0].shape
    size = rows // pieces

    def turn(i):
        return (lax.rem(i + start + lax.axis_index("col"), pieces), 0)

    def fixed(array):
        return pl.BlockSpec(array.shape, lambda i: (0, 0))

    outs = tuple(extra) + (shape(width, size),) * count
    at, to = len(operands), len(outs)
    *results, low, high = pl.pallas_call(
        kernel,
        grid=(count,),
        in_specs=[fixed(x) for x in operands] + [pl.BlockSpec((size, span), turn)] * 2,
        out_specs=tuple(fixed(x) for x in outs) + (pl.BlockSpec(memory_space=pl.ANY),) * 2,
        out_shape=outs + (shape(rows, span),) * 2,
        input_output_aliases={at: to, at + 1: to + 1},
        compiler_params=params(22),
        cost_estimate=cost(16 * size * count * span * width, 8 * size * count * span),
    )(*operands, *halves)
    return (*results, (low, high))


def merge_first_kernel(first_ref, second_ref, by_x_ref, by_y_ref, a_ref, b_ref):
    half = a_ref.shape[1]
    relation = lax.div(lax.axis_index("row"), 2) ^ lax.axis_index("col")
    for at, own, got, out in (
        (1, first_ref, by_x_ref, a_ref),
        (2, second_ref, by_y_ref, b_ref),
    ):
        out[...] = jnp.where(
            relation == 0, own[...], jnp.where(relation == at, got[:, :half], 0.0)
        )


def join_kernel(a_ref, b_ref, c_ref, d_ref, out_ref):
    half = a_ref.shape[1]
    out_ref[:, :half] = a_ref[...] + b_ref[...]
    out_ref[:, half:] = c_ref[...] + d_ref[...]


def halve_kernel(keep_ref, other_ref, a_ref, b_ref):
    half = a_ref.shape[1]
    a_ref[...] = keep_ref[:, :half] + other_ref[:, :half]
    b_ref[...] = keep_ref[:, half:] + other_ref[:, half:]


def pair_kernel(a_ref, b_ref, c_ref, d_ref, e_ref, f_ref):
    e_ref[...] = a_ref[...] + b_ref[...]
    f_ref[...] = c_ref[...] + d_ref[...]


def inner_kernel(kct_ref, held_ref, other_ref, xct_ref, inner_ref):
    half = held_ref.shape[1]
    core = lax.rem(lax.axis_index("row"), 2)

    @pl.when(core == 0)
    def _():
        xct_ref[:, :half] = held_ref[...]
        xct_ref[:, half:] = other_ref[...]

    @pl.when(core == 1)
    def _():
        xct_ref[:, :half] = other_ref[...]
        xct_ref[:, half:] = held_ref[...]

    inner_ref[...] = lax.dot_general(
        kct_ref[...],
        xct_ref[...],
        (((1,), (1,)), ((), ())),
        precision=precise,
        preferred_element_type=f32,
    )


def wide_kernel(
    st_ref, xct_ref, kct_ref, first_ref, second_ref, band_ref, x_ref, k_ref, rows_ref, left_ref
):
    width, columns = kct_ref.shape
    st = st_ref[...]
    chunk = block_of(columns, 512)
    for c in range(0, columns, chunk):
        for ref, value in (
            (x_ref, dot(st, xct_ref[:, c : c + chunk])),
            (k_ref, kct_ref[:, c : c + chunk]),
        ):
            ref[:, c : c + chunk] = jnp.concatenate(split(value), 0)
    half = first_ref.shape[1]
    rows_ref[:, :half] = first_ref[...]
    rows_ref[:, half:] = second_ref[...]

    @pl.when(lax.axis_index("row") == 0)
    def _():
        rows_ref[:, :width] = rows_ref[:, :width] - band_ref[...].T

    rows = rows_ref.shape[1]
    deep = block_of(rows, 512)
    for r in range(0, rows, deep):
        left_ref[r : r + deep, :] = jnp.concatenate(split(rows_ref[:, r : r + deep].T), 1)


def both_parts(left):
    return jnp.concatenate([left, left], 1)


def four_parts(right_ref, start, size):
    width = right_ref.shape[0] // 2
    high = right_ref[:width, pl.ds(start, size)]
    low = right_ref[width:, pl.ds(start, size)]
    return jnp.concatenate([high, high, low, low], 0)


def near_kernel(left_ref, right_ref, a_ref, _, out_ref, __):
    rows, span = a_ref.shape
    deep = block_of(rows, 512)
    chunk = block_of(span, 512)

    @pl.loop(0, span // chunk)
    def _(i):
        c = pl.multiple_of(i * chunk, chunk)
        right = four_parts(right_ref, c, chunk)
        for r in range(0, rows, deep):
            out_ref[r : r + deep, pl.ds(c, chunk)] = a_ref[r : r + deep, pl.ds(c, chunk)] - fast(
                both_parts(left_ref[r : r + deep, :]), right
            )


def subtract_near(left, right, low, high):
    rows, span = low.shape
    deep = left.shape[1]
    whole = pl.BlockSpec(memory_space=pltpu.VMEM)
    anywhere = pl.BlockSpec(memory_space=pl.ANY)
    return tuple(
        pl.pallas_call(
            near_kernel,
            in_specs=[whole] * 3 + [anywhere],
            out_specs=(whole, anywhere),
            out_shape=(shape(rows, span),) * 2,
            input_output_aliases={2: 0, 3: 1},
            compiler_params=params(12),
            cost_estimate=cost(4 * rows * span * deep, 8 * rows * span),
            name="subtract_near",
        )(left, right, low, high)
    )


def core_kernel(part_ref, more_ref, st_ref, krt_ref, out_ref):
    st = st_ref[...]
    cm = dot(dot(st, part_ref[...] + more_ref[...]), st.T)
    out_ref[...] = dot(cm, krt_ref[...])


def left_kernel(st_ref, core_ref, *refs):
    chunks, left_ref = refs[:-1], refs[-1]
    pieces = len(chunks)
    size = chunks[0].shape[1]
    st = st_ref[...]
    col = lax.axis_index("col")
    for at, ref in enumerate(chunks):
        start = pl.multiple_of(lax.rem(col + pieces - at, pieces) * size, size)
        value = dot(st, ref[...]) - core_ref[:, pl.ds(start, size)]
        left_ref[pl.ds(start, size), :] = jnp.concatenate(split(value.T), 1)


def far_kernel(
    left_ref, right_ref, near_left_ref, near_right_ref, low_ref, high_ref, out_ref, buffer, sems
):
    rows, span = low_ref.shape
    slots, deep, wide = buffer.shape
    down = rows // deep
    pairs = down * (span // wide)

    def store(i, slot):
        turn, pair = lax.rem(i, 2), lax.div(i, 2)
        r = pl.multiple_of(lax.rem(pair, down) * deep, deep)
        c = pl.multiple_of(turn * span + lax.div(pair, down) * wide, wide)
        return pltpu.make_async_copy(
            buffer.at[slot], out_ref.at[pl.ds(r, deep), pl.ds(c, wide)], sems.at[slot]
        )

    @pl.loop(0, pairs)
    def _(pair):
        r = pl.multiple_of(lax.rem(pair, down) * deep, deep)
        local = pl.multiple_of(lax.div(pair, down) * wide, wide)
        for turn, a_ref in enumerate((low_ref, high_ref)):
            i = pair * 2 + turn
            slot = lax.rem(i, slots)

            @pl.when(i >= slots)
            def _():
                store(i - slots, slot).wait()

            c = pl.multiple_of(turn * span + local, wide)
            left = both_parts(left_ref[pl.ds(r, deep), :])
            right = four_parts(right_ref, c, wide)
            if turn:
                left = jnp.concatenate([left, both_parts(near_left_ref[pl.ds(r, deep), :])], 1)
                right = jnp.concatenate([right, four_parts(near_right_ref, c, wide)], 0)
            buffer[slot] = a_ref[pl.ds(r, deep), pl.ds(local, wide)] - fast(left, right)
            store(i, slot).start()

    for back in range(slots, 0, -1):
        store(2 * pairs - back, (2 * pairs - back) % slots).wait()


def subtract_far(left, right, near_left, near_right, low, high):
    rows, span = low.shape
    deep = left.shape[1]
    whole = pl.BlockSpec(memory_space=pltpu.VMEM)
    wide = span if (span // 2) % 128 else span // 2
    piece = (block_of(rows, 512), wide)
    return pl.pallas_call(
        far_kernel,
        in_specs=[whole] * 6,
        out_specs=pl.BlockSpec(memory_space=pltpu.HBM),
        out_shape=shape(rows, 2 * span),
        scratch_shapes=[pltpu.VMEM((3,) + piece, f32), pltpu.SemaphoreType.DMA((3,))],
        compiler_params=params(12),
        cost_estimate=cost(12 * rows * span * deep, 16 * rows * span),
        name="subtract_far",
    )(left, right, near_left, near_right, low, high)


def flip(value, bit, size, axis="row"):
    return lax.ppermute(value, axis, [(i, i ^ bit) for i in range(size)])


def from_sources(piece, col_size, source_flips, bit):
    pairs = []
    for c in range(col_size):
        for source in source_flips:
            for core in range(2):
                at = (2 * c + core) ^ source
                pairs.append((at * col_size + c, (at ^ bit) * col_size + c))
    return lax.ppermute(piece, ("row", "col"), pairs)


def shift(piece, by, size):
    return lax.ppermute(piece, "col", [(i, (i + by) % size) for i in range(size)])


def body_of(row_size, col_size):
    assert row_size == 2 * col_size

    def body(matrix, panel):
        rows, width = panel.shape
        columns = matrix.shape[1]
        small = shape(width, width)
        packed = shape(width, 2 * width)
        half = shape(width, rows // 2)
        first, second, partial = small_call(
            open_kernel, (half, half, packed), panel.T, flops=100_000_000, mib=12
        )
        apart = flip(partial, 1, row_size)
        if row_size == 8:
            wide_half = shape(width, rows // 2 + 2 * width)
            send_x, send_y, partial = small_call(
                add_cores_kernel, (wide_half, wide_half, packed), first, second, partial, apart
            )
            by_x = flip(send_x, 2, row_size)
            by_y = flip(send_y, 4, row_size)
            terms = [partial, by_x, by_y, flip(partial, 6, row_size)]
        else:
            partial = small_call(add_kernel, packed, partial, apart)
            bit = 2
            total = partial
            while bit < row_size // 2:
                total = total + flip(total, bit, row_size)
                bit *= 2
            zero = jnp.zeros_like(total)
            terms = [total, flip(total, row_size // 2, row_size), zero, zero]
        first, second, partial = lax.optimization_barrier((first, second, partial))
        low, resident = product_down(first, second, matrix, 0)
        if row_size == 8:
            one, two, resident = small_call(
                merge_first_kernel, (half, half), first, second, by_x, by_y, carry=resident
            )
            more_x = from_sources(two, col_size, [0, 4], 2)
            more_y = from_sources(one, col_size, [0, 2], 4)
        else:
            relation = (lax.axis_index("row") // 2) ^ lax.axis_index("col")
            held = jnp.where(relation == 0, jnp.concatenate([first, second], 1), 0.0)
            reached = [0]
            bit = 2
            while bit < row_size:
                held = held + from_sources(held, col_size, reached, bit)
                reached = reached + [r ^ bit for r in reached]
                bit *= 2
        high, resident = product_down(first, second, matrix, 1, resident)
        band, again, band_inverse, head, resident = small_call(
            eliminate_kernel, (small, small, small, small), *terms, flops=50_000_000, carry=resident
        )
        keep, give, resident = fix_down(low, high, again, resident)
        if row_size == 8:
            held, resident = small_call(
                join_kernel, shape(width, rows), one, more_y, two, more_x, carry=resident
            )
        other = flip(held, 1, row_size)
        quarter = shape(width, columns // 4)
        a, b, resident = small_call(
            halve_kernel, (quarter, quarter), keep, flip(give, 1, row_size), carry=resident
        )
        bits = []
        bit = 2
        while bit < row_size:
            bits.append(bit)
            bit *= 2
        pieces = 1 if (rows // col_size) % 128 else col_size
        late = pieces // 2
        for forward, backward in list(zip(bits, bits[::-1]))[:-1]:
            ra = flip(a, forward, row_size)
            rb = flip(b, backward, row_size)
            if bits[0] == forward:
                kct, right, *chunks, resident = across_call(
                    across_kernel,
                    (held, other, again),
                    (shape(width, columns), shape(columns, 2 * width, dtype=bf16)),
                    resident,
                    pieces,
                    late,
                    pieces - late,
                    width,
                )
            a, b, resident = small_call(
                pair_kernel, (quarter, quarter), a, ra, b, rb, carry=resident
            )
        ra = flip(a, bits[-1], row_size)
        rb = flip(b, bits[0], row_size)
        if late:
            received = [shift(chunks[at], late + at, col_size) for at in range(pieces - late)]
            *chunks, resident = across_call(
                more_kernel, (right,), (), resident, pieces, 0, late, width
            )
            received += [shift(chunks[by], by, col_size) for by in range(1, late)]
        summed, resident = small_call(
            join_kernel, shape(width, columns // 2), a, ra, b, rb, carry=resident
        )
        xct, inner, resident = small_call(
            inner_kernel,
            (shape(width, columns), small),
            kct,
            summed,
            flip(summed, 1, row_size),
            carry=resident,
        )
        bit = 1
        others = []
        while bit < col_size // 2:
            others.append(bit)
            bit *= 2
        first_inner = flip(inner, 1, col_size, "col")
        if pieces == 1:
            whole = [lax.psum(chunks[0], "col")]
        else:
            mine, resident = small_call(
                add_kernel, shape(width, rows // col_size), chunks[0], *received, carry=resident
            )
            whole = [mine] + [shift(mine, by, col_size) for by in range(1, col_size)]
        for at in others:
            got = first_inner if at == 1 else flip(inner, at, col_size, "col")
            inner, resident = small_call(add_kernel, small, inner, got, carry=resident)
        more = flip(inner, bit, col_size, "col")
        st, resident = small_call(
            invert_kernel, small, head, again, band_inverse, flops=50_000_000, carry=resident
        )
        xparts, kparts, krt, near_left, resident = small_call(
            wide_kernel,
            (
                shape(2 * width, columns, dtype=bf16),
                shape(2 * width, columns, dtype=bf16),
                shape(width, rows),
                shape(rows, 2 * width, dtype=bf16),
            ),
            st,
            xct,
            kct,
            first,
            second,
            again,
            mib=12,
            carry=resident,
        )
        resident = subtract_near(near_left, xparts, *resident)
        core, resident = small_call(
            core_kernel, shape(width, rows), inner, more, st, krt, carry=resident
        )
        left, resident = small_call(
            left_kernel,
            shape(rows, 2 * width, dtype=bf16),
            st,
            core,
            *whole,
            mib=12,
            carry=resident,
        )
        return subtract_far(left, kparts, near_left, xparts, *resident), band

    return body


def solution(mesh):
    body = body_of(mesh.shape["row"], mesh.shape["col"])

    return jax.shard_map(
        body,
        mesh=mesh,
        in_specs=(P("row", "col"), P("row", None)),
        out_specs=(P("row", "col"), P()),
        check_vma=False,
    )
```

```python
import jax
import jax.numpy as jnp
from jax import lax
from jax.experimental import pallas as pl
from jax.experimental.pallas import tpu as pltpu
from jax.sharding import PartitionSpec as P


precise = lax.Precision.HIGHEST
f32 = jnp.float32
bf16 = jnp.bfloat16


def shape(*dims, dtype=f32):
    return jax.ShapeDtypeStruct(dims, dtype)


def params(mib):
    return pltpu.CompilerParams(vmem_limit_bytes=mib * 1024 * 1024)


def cost(flops, moved):
    return pl.CostEstimate(flops=flops, bytes_accessed=moved, transcendentals=0)


def dot(a, b):
    return jnp.dot(a, b, precision=precise, preferred_element_type=f32)


def fast(a, b):
    return jnp.dot(a, b, preferred_element_type=f32)


def split(value):
    high = value.astype(bf16)
    return high, (value - high.astype(f32)).astype(bf16)


def block_of(size, wanted):
    while size % wanted:
        wanted //= 2
    return wanted


def small_call(kernel, out, *operands, carry=(), flops=1_000_000, moved=1_000_000, mib=8):
    extra = {}
    body = kernel
    if carry:
        outs = out if isinstance(out, tuple) else (out,)
        count, more = len(operands), len(carry)
        anywhere = pl.BlockSpec(memory_space=pl.ANY)
        whole = pl.BlockSpec(memory_space=pltpu.VMEM)
        extra = dict(
            in_specs=[whole] * count + [anywhere] * more,
            out_specs=(whole,) * len(outs) + (anywhere,) * more,
            input_output_aliases={count + k: len(outs) + k for k in range(more)},
        )
        operands = operands + tuple(carry)
        out = outs + tuple(shape(*x.shape) for x in carry)

        def body(*refs):
            kernel(*refs[:count], *refs[count + more : -more])

    result = pl.pallas_call(
        body, out_shape=out, compiler_params=params(mib), cost_estimate=cost(flops, moved), **extra
    )(*operands)
    if carry:
        return tuple(result[: -len(carry)]) + (tuple(result[-len(carry) :]),)
    return result


def open_kernel(turned_ref, first_ref, second_ref, packed_ref):
    width = turned_ref.shape[0]
    half = first_ref.shape[1]
    turned = turned_ref[...]
    first_ref[...] = turned[:, :half]
    second_ref[...] = turned[:, half:]
    gram = lax.dot_general(
        turned, turned, (((1,), (1,)), ((), ())), precision=precise, preferred_element_type=f32
    )
    head = jnp.where(lax.axis_index("row") == 0, turned[:, : 2 * width].T[:width], 0.0)
    packed_ref[...] = jnp.concatenate([gram, head], 1)


def add_cores_kernel(first_ref, second_ref, a_ref, b_ref, x_ref, y_ref, sum_ref):
    half = first_ref.shape[1]
    total = a_ref[...] + b_ref[...]
    sum_ref[...] = total
    for source, target in ((first_ref, x_ref), (second_ref, y_ref)):
        target[:, :half] = source[...]
        target[:, half:] = total


def add_kernel(*refs):
    total = refs[0][...]
    for ref in refs[1:-1]:
        total = total + ref[...]
    refs[-1][...] = total


def spread(tile, at):
    return jnp.broadcast_to(tile[at : at + 1, :], tile.shape)


def pick(tile, at):
    return jnp.broadcast_to(tile[:, at : at + 1], tile.shape)


def sweep(tiles, order, full):
    lane = lax.broadcasted_iota(jnp.int32, (8, order), 1)
    sub = lax.broadcasted_iota(jnp.int32, (8, order), 0)
    tiles = list(tiles)
    for at in range(order // 8):
        base = 8 * at
        inside = (lane >= base) & (lane < base + 8)
        tile = tiles[at]
        others = [t for t in range(order // 8) if (t != at if full else t > at)]
        picked = {t: [pick(tiles[t], base + q) for q in range(8)] for t in others}
        columns = [pick(tile, base + q) for q in range(8)]
        rows = jnp.where(inside, jnp.where(lane - base == sub, 1.0, 0.0), tile)
        lower, upper = rows, tile
        for q in range(8):
            here = sub == q
            inverse = 1.0 / spread(columns[q], q)
            scaled = spread(rows, q) * inverse
            if not full:
                lower = jnp.where(here, rows, lower)
                upper = jnp.where(
                    sub > q, upper - columns[q] * (spread(upper, q) * inverse), upper
                )
            rows = jnp.where(here, scaled, rows - columns[q] * scaled)
            for p in range(q + 1, 8):
                part = spread(columns[p], q) * inverse
                columns[p] = jnp.where(here, part, columns[p] - columns[q] * part)
        finals = [spread(rows, q) for q in range(8)]
        for t in others:
            value = jnp.where(inside, 0.0, tiles[t])
            for q in range(8):
                value = value - picked[t][q] * finals[q]
            tiles[t] = value
        tiles[at] = rows if full else jnp.where(inside & (lane - base >= sub), upper, lower)
    return tiles


def eliminate_kernel(a_ref, b_ref, c_ref, d_ref, band_ref, again_ref, inverse_ref, head_ref):
    order = band_ref.shape[0]
    lane = lax.broadcasted_iota(jnp.int32, (8, order), 1)
    sub = lax.broadcasted_iota(jnp.int32, (8, order), 0)
    skip = b_ref.shape[1] - a_ref.shape[1]
    total = (a_ref[...] + b_ref[:, skip:]) + (c_ref[:, skip:] + d_ref[...])
    head_ref[...] = total[:, order:]
    gram = total[:, :order]
    tiles = sweep([gram[8 * t : 8 * t + 8, :] for t in range(order // 8)], order, False)
    for t in range(order // 8):
        row_at = sub + 8 * t
        diagonal = jnp.sum(jnp.where(lane == row_at, tiles[t], 0.0), axis=1, keepdims=True)
        length = jnp.sqrt(diagonal)
        scaled = tiles[t] / length
        band = jnp.where(lane > row_at, -scaled, jnp.where(lane == row_at, -length, 0.0))
        band_ref[8 * t : 8 * t + 8, :] = band
        again_ref[8 * t : 8 * t + 8, :] = band
        inverse_ref[8 * t : 8 * t + 8, :] = jnp.where(
            lane < row_at, -scaled, jnp.where(lane == row_at, -1.0 / length, 0.0)
        )


def invert_kernel(head_ref, band_ref, inverse_ref, out_ref):
    order = head_ref.shape[0]
    tiles = [
        head_ref[8 * t : 8 * t + 8, :] - band_ref[8 * t : 8 * t + 8, :] for t in range(order // 8)
    ]
    tiles = sweep(tiles, order, True)
    out_ref[...] = -dot(jnp.concatenate(tiles, 0), inverse_ref[...])


def down_kernel(first_ref, second_ref, a_ref, low_ref, high_ref, kept_ref, over_ref, sems):
    width, span = low_ref.shape
    count = sems.shape[0] // 2
    size = span // count
    halves = ((0, low_ref, kept_ref), (1, high_ref, over_ref))

    def load(at, ref, i):
        start = pl.multiple_of(i * size, size)
        source = a_ref.at[:, pl.ds(pl.multiple_of(at * span + start, size), size)]
        return pltpu.make_async_copy(
            source, ref.at[:, pl.ds(start, size)], sems.at[at * count + i]
        )

    for at, _, kept in halves:
        for i in range(count):
            load(at, kept, i).start()
    kh, kl = split(jnp.concatenate([first_ref[...], second_ref[...]], 1))
    left = jnp.concatenate([kh, kl], 0)
    for at, out, kept in halves:

        @pl.loop(0, count)
        def _(i):
            load(at, kept, i).wait()
            part = pl.ds(pl.multiple_of(i * size, size), size)
            ah, al = split(kept[:, part])
            term = fast(left, ah) + fast(left, al)
            out[:, part] = term[:width] + term[width:]


def product_down(first, second, a):
    rows, columns = a.shape
    width = first.shape[0]
    span = columns // 2
    size = block_of(span, 256)
    whole = pl.BlockSpec(memory_space=pltpu.VMEM)
    low, high, *halves = pl.pallas_call(
        down_kernel,
        in_specs=[whole, whole, pl.BlockSpec(memory_space=pltpu.HBM)],
        out_specs=(whole,) * 4,
        out_shape=(shape(width, span),) * 2 + (shape(rows, span),) * 2,
        scratch_shapes=[pltpu.SemaphoreType.DMA((columns // size,))],
        compiler_params=params(12),
        cost_estimate=cost(8 * rows * columns * width, 4 * rows * columns),
        name="product_down",
    )(first, second, pltpu.with_memory_space_constraint(a, pltpu.HBM))
    return low, high, tuple(halves)


def fix_kernel(low_ref, high_ref, band_ref, top_ref, over_ref, keep_ref, give_ref, *_):
    row = lax.axis_index("row")
    core = lax.rem(row, 2)
    first, second = low_ref[...], high_ref[...]

    @pl.when(row == 0)
    def _():
        rh, rl = split(band_ref[...].T)
        left = jnp.concatenate([rh, rl, rh, rl], 1)
        for value, top, out in ((first, top_ref, keep_ref), (second, over_ref, give_ref)):
            ah, al = split(top[...])
            out[...] = value - fast(left, jnp.concatenate([ah, ah, al, al], 0))

    @pl.when((row != 0) & (core == 0))
    def _():
        keep_ref[...] = first
        give_ref[...] = second

    @pl.when(core == 1)
    def _():
        keep_ref[...] = second
        give_ref[...] = first


def fix_down(low, high, band, halves):
    width, span = low.shape
    part = pl.BlockSpec((width, span), lambda i: (0, 0))
    anywhere = pl.BlockSpec(memory_space=pl.ANY)
    keep, give, *halves = pl.pallas_call(
        fix_kernel,
        grid=(1,),
        in_specs=[part, part, pl.BlockSpec((width, width), lambda i: (0, 0)), part, part],
        out_specs=(part, part, anywhere, anywhere),
        out_shape=(shape(width, span),) * 2 + tuple(shape(*x.shape) for x in halves),
        input_output_aliases={3: 2, 4: 3},
        compiler_params=params(12),
        cost_estimate=cost(24 * width * width * span, 32 * width * span),
        name="fix_down",
    )(low, high, band, *halves)
    return keep, give, tuple(halves)


def rows_product(right_ref, halves, outs):
    span = halves[0].shape[1]
    width = right_ref.shape[1] // 2
    chunk = block_of(span, 512)
    total = None
    for at, a_ref in enumerate(halves):
        for c in range(0, span, chunk):
            ah, al = split(a_ref[:, c : c + chunk])
            right = right_ref[at * span + c : at * span + c + chunk, :]
            term = fast(ah, right) + fast(al, right)
            total = term if total is None else total + term
    result = (total[:, :width] + total[:, width:]).T
    for at, out_ref in enumerate(outs):

        @pl.when(pl.program_id(0) == at)
        def _():
            out_ref[...] = result


def across_kernel(held_ref, other_ref, band_ref, low_ref, high_ref, kct_ref, right_ref, *refs):
    width, half = held_ref.shape
    columns = 2 * half
    chunk = block_of(columns, 512)

    @pl.when(pl.program_id(0) == 0)
    def _():
        core = lax.rem(lax.axis_index("row"), 2)

        @pl.when(core == 0)
        def _():
            kct_ref[:, :half] = held_ref[...]
            kct_ref[:, half:] = other_ref[...]

        @pl.when(core == 1)
        def _():
            kct_ref[:, :half] = other_ref[...]
            kct_ref[:, half:] = held_ref[...]

        @pl.when(lax.axis_index("col") == 0)
        def _():
            kct_ref[:, :width] = kct_ref[:, :width] - band_ref[...].T

        for c in range(0, columns, chunk):
            right_ref[c : c + chunk, :] = jnp.concatenate(split(kct_ref[:, c : c + chunk].T), 1)

    rows_product(right_ref, (low_ref, high_ref), refs[:-2])


def more_kernel(right_ref, low_ref, high_ref, *refs):
    rows_product(right_ref, (low_ref, high_ref), refs[:-2])


def across_call(kernel, operands, extra, halves, pieces, start, count, width):
    rows, span = halves[0].shape
    size = rows // pieces

    def turn(i):
        return (lax.rem(i + start + lax.axis_index("col"), pieces), 0)

    def fixed(array):
        return pl.BlockSpec(array.shape, lambda i: (0, 0))

    outs = tuple(extra) + (shape(width, size),) * count
    at, to = len(operands), len(outs)
    *results, low, high = pl.pallas_call(
        kernel,
        grid=(count,),
        in_specs=[fixed(x) for x in operands] + [pl.BlockSpec((size, span), turn)] * 2,
        out_specs=tuple(fixed(x) for x in outs) + (pl.BlockSpec(memory_space=pl.ANY),) * 2,
        out_shape=outs + (shape(rows, span),) * 2,
        input_output_aliases={at: to, at + 1: to + 1},
        compiler_params=params(22),
        cost_estimate=cost(16 * size * count * span * width, 8 * size * count * span),
    )(*operands, *halves)
    return (*results, (low, high))


def merge_first_kernel(first_ref, second_ref, by_x_ref, by_y_ref, a_ref, b_ref):
    half = a_ref.shape[1]
    relation = lax.div(lax.axis_index("row"), 2) ^ lax.axis_index("col")
    for at, own, got, out in (
        (1, first_ref, by_x_ref, a_ref),
        (2, second_ref, by_y_ref, b_ref),
    ):
        out[...] = jnp.where(
            relation == 0, own[...], jnp.where(relation == at, got[:, :half], 0.0)
        )


def join_kernel(a_ref, b_ref, c_ref, d_ref, out_ref):
    half = a_ref.shape[1]
    out_ref[:, :half] = a_ref[...] + b_ref[...]
    out_ref[:, half:] = c_ref[...] + d_ref[...]


def halve_kernel(keep_ref, other_ref, a_ref, b_ref):
    half = a_ref.shape[1]
    a_ref[...] = keep_ref[:, :half] + other_ref[:, :half]
    b_ref[...] = keep_ref[:, half:] + other_ref[:, half:]


def pair_kernel(a_ref, b_ref, c_ref, d_ref, e_ref, f_ref):
    e_ref[...] = a_ref[...] + b_ref[...]
    f_ref[...] = c_ref[...] + d_ref[...]


def inner_kernel(kct_ref, held_ref, other_ref, xct_ref, inner_ref):
    half = held_ref.shape[1]
    core = lax.rem(lax.axis_index("row"), 2)

    @pl.when(core == 0)
    def _():
        xct_ref[:, :half] = held_ref[...]
        xct_ref[:, half:] = other_ref[...]

    @pl.when(core == 1)
    def _():
        xct_ref[:, :half] = other_ref[...]
        xct_ref[:, half:] = held_ref[...]

    inner_ref[...] = lax.dot_general(
        kct_ref[...],
        xct_ref[...],
        (((1,), (1,)), ((), ())),
        precision=precise,
        preferred_element_type=f32,
    )


def wide_kernel(
    st_ref, xct_ref, kct_ref, first_ref, second_ref, band_ref, x_ref, k_ref, rows_ref, left_ref
):
    width, columns = kct_ref.shape
    st = st_ref[...]
    chunk = block_of(columns, 512)
    for c in range(0, columns, chunk):
        for ref, value in (
            (x_ref, dot(st, xct_ref[:, c : c + chunk])),
            (k_ref, kct_ref[:, c : c + chunk]),
        ):
            ref[:, c : c + chunk] = jnp.concatenate(split(value), 0)
    half = first_ref.shape[1]
    rows_ref[:, :half] = first_ref[...]
    rows_ref[:, half:] = second_ref[...]

    @pl.when(lax.axis_index("row") == 0)
    def _():
        rows_ref[:, :width] = rows_ref[:, :width] - band_ref[...].T

    rows = rows_ref.shape[1]
    deep = block_of(rows, 512)
    for r in range(0, rows, deep):
        left_ref[r : r + deep, :] = jnp.concatenate(split(rows_ref[:, r : r + deep].T), 1)


def both_parts(left):
    return jnp.concatenate([left, left], 1)


def four_parts(right_ref, start, size):
    width = right_ref.shape[0] // 2
    high = right_ref[:width, pl.ds(start, size)]
    low = right_ref[width:, pl.ds(start, size)]
    return jnp.concatenate([high, high, low, low], 0)


def near_kernel(left_ref, right_ref, a_ref, _, out_ref, __):
    rows, span = a_ref.shape
    deep = block_of(rows, 512)
    chunk = block_of(span, 512)

    @pl.loop(0, span // chunk)
    def _(i):
        c = pl.multiple_of(i * chunk, chunk)
        right = four_parts(right_ref, c, chunk)
        for r in range(0, rows, deep):
            out_ref[r : r + deep, pl.ds(c, chunk)] = a_ref[r : r + deep, pl.ds(c, chunk)] - fast(
                both_parts(left_ref[r : r + deep, :]), right
            )


def subtract_near(left, right, low, high):
    rows, span = low.shape
    deep = left.shape[1]
    whole = pl.BlockSpec(memory_space=pltpu.VMEM)
    anywhere = pl.BlockSpec(memory_space=pl.ANY)
    return tuple(
        pl.pallas_call(
            near_kernel,
            in_specs=[whole] * 3 + [anywhere],
            out_specs=(whole, anywhere),
            out_shape=(shape(rows, span),) * 2,
            input_output_aliases={2: 0, 3: 1},
            compiler_params=params(12),
            cost_estimate=cost(4 * rows * span * deep, 8 * rows * span),
            name="subtract_near",
        )(left, right, low, high)
    )


def packing(width, size):
    beside = 1
    while 2 * beside <= min(size // width, 8):
        beside *= 2
    return beside, width // beside


def line_kernel(*refs):
    *chunks, inner_ref, out_ref = refs
    width, size = chunks[0].shape
    beside, tall = packing(width, size)
    total = chunks[0][...]
    for ref in chunks[1:]:
        total = total + ref[...]
    out_ref[:width, :] = total
    out_ref[width:, :] = jnp.zeros((tall, size), f32)
    for k in range(beside):
        out_ref[width:, k * width : (k + 1) * width] = inner_ref[k * tall : (k + 1) * tall, :]


def core_kernel(st_ref, krt_ref, *refs):
    chunks, out_ref = refs[:-1], refs[-1]
    width = st_ref.shape[0]
    beside, _ = packing(width, chunks[0].shape[1])
    packed = chunks[0][width:, :]
    for ref in chunks[1:]:
        packed = packed + ref[width:, :]
    inner = jnp.concatenate([packed[:, k * width : (k + 1) * width] for k in range(beside)], 0)
    st = st_ref[...]
    cm = dot(dot(st, inner), st.T)
    out_ref[...] = dot(cm, krt_ref[...])


def left_kernel(st_ref, core_ref, *refs):
    chunks, left_ref = refs[:-1], refs[-1]
    pieces = len(chunks)
    size = chunks[0].shape[1]
    st = st_ref[...]
    col = lax.axis_index("col")
    for at, ref in enumerate(chunks):
        start = pl.multiple_of(lax.rem(col + pieces - at, pieces) * size, size)
        value = dot(st, ref[: st.shape[0], :]) - core_ref[:, pl.ds(start, size)]
        left_ref[pl.ds(start, size), :] = jnp.concatenate(split(value.T), 1)


def far_kernel(
    left_ref, right_ref, near_left_ref, near_right_ref, low_ref, high_ref, out_ref, buffer, sems
):
    rows, span = low_ref.shape
    slots, deep, wide = buffer.shape
    down = rows // deep
    pairs = down * (span // wide)

    def store(i, slot):
        turn, pair = lax.rem(i, 2), lax.div(i, 2)
        r = pl.multiple_of(lax.rem(pair, down) * deep, deep)
        c = pl.multiple_of(turn * span + lax.div(pair, down) * wide, wide)
        return pltpu.make_async_copy(
            buffer.at[slot], out_ref.at[pl.ds(r, deep), pl.ds(c, wide)], sems.at[slot]
        )

    @pl.loop(0, pairs)
    def _(pair):
        r = pl.multiple_of(lax.rem(pair, down) * deep, deep)
        local = pl.multiple_of(lax.div(pair, down) * wide, wide)
        for turn, a_ref in enumerate((low_ref, high_ref)):
            i = pair * 2 + turn
            slot = lax.rem(i, slots)

            @pl.when(i >= slots)
            def _():
                store(i - slots, slot).wait()

            c = pl.multiple_of(turn * span + local, wide)
            left = both_parts(left_ref[pl.ds(r, deep), :])
            right = four_parts(right_ref, c, wide)
            if turn:
                left = jnp.concatenate([left, both_parts(near_left_ref[pl.ds(r, deep), :])], 1)
                right = jnp.concatenate([right, four_parts(near_right_ref, c, wide)], 0)
            buffer[slot] = a_ref[pl.ds(r, deep), pl.ds(local, wide)] - fast(left, right)
            store(i, slot).start()

    for back in range(slots, 0, -1):
        store(2 * pairs - back, (2 * pairs - back) % slots).wait()


def subtract_far(left, right, near_left, near_right, low, high):
    rows, span = low.shape
    deep = left.shape[1]
    whole = pl.BlockSpec(memory_space=pltpu.VMEM)
    wide = span if (span // 2) % 128 else span // 2
    piece = (block_of(rows, 512), wide)
    return pl.pallas_call(
        far_kernel,
        in_specs=[whole] * 6,
        out_specs=pl.BlockSpec(memory_space=pltpu.HBM),
        out_shape=shape(rows, 2 * span),
        scratch_shapes=[pltpu.VMEM((3,) + piece, f32), pltpu.SemaphoreType.DMA((3,))],
        compiler_params=params(12),
        cost_estimate=cost(12 * rows * span * deep, 16 * rows * span),
        name="subtract_far",
    )(left, right, near_left, near_right, low, high)


def flip(value, bit, size, axis="row"):
    return lax.ppermute(value, axis, [(i, i ^ bit) for i in range(size)])


def from_sources(piece, col_size, source_flips, bit):
    pairs = []
    for c in range(col_size):
        for source in source_flips:
            for core in range(2):
                at = (2 * c + core) ^ source
                pairs.append((at * col_size + c, (at ^ bit) * col_size + c))
    return lax.ppermute(piece, ("row", "col"), pairs)


def shift(piece, by, size):
    return lax.ppermute(piece, "col", [(i, (i + by) % size) for i in range(size)])


def body_of(row_size, col_size):
    assert row_size == 2 * col_size

    def body(matrix, panel):
        rows, width = panel.shape
        columns = matrix.shape[1]
        small = shape(width, width)
        packed = shape(width, 2 * width)
        half = shape(width, rows // 2)
        first, second, partial = small_call(
            open_kernel, (half, half, packed), panel.T, flops=100_000_000, mib=12
        )
        apart = flip(partial, 1, row_size)
        if row_size == 8:
            wide_half = shape(width, rows // 2 + 2 * width)
            send_x, send_y, partial = small_call(
                add_cores_kernel, (wide_half, wide_half, packed), first, second, partial, apart
            )
            by_x = flip(send_x, 2, row_size)
            by_y = flip(send_y, 4, row_size)
            terms = [partial, by_x, by_y, flip(partial, 6, row_size)]
        else:
            partial = small_call(add_kernel, packed, partial, apart)
            bit = 2
            total = partial
            while bit < row_size // 2:
                total = total + flip(total, bit, row_size)
                bit *= 2
            zero = jnp.zeros_like(total)
            terms = [total, flip(total, row_size // 2, row_size), zero, zero]
        first, second, partial = lax.optimization_barrier((first, second, partial))
        low, high, resident = product_down(first, second, matrix)
        if row_size == 8:
            one, two, resident = small_call(
                merge_first_kernel, (half, half), first, second, by_x, by_y, carry=resident
            )
            more_x = flip(two, 2, row_size)
            more_y = flip(one, 4, row_size)
        else:
            relation = (lax.axis_index("row") // 2) ^ lax.axis_index("col")
            held = jnp.where(relation == 0, jnp.concatenate([first, second], 1), 0.0)
            reached = [0]
            bit = 2
            while bit < row_size:
                held = held + from_sources(held, col_size, reached, bit)
                reached = reached + [r ^ bit for r in reached]
                bit *= 2
        band, again, band_inverse, head, resident = small_call(
            eliminate_kernel, (small, small, small, small), *terms, flops=50_000_000, carry=resident
        )
        keep, give, resident = fix_down(low, high, again, resident)
        quarter = shape(width, columns // 4)
        a, b, resident = small_call(
            halve_kernel, (quarter, quarter), keep, flip(give, 1, row_size), carry=resident
        )
        if row_size == 8:
            held, resident = small_call(
                join_kernel, shape(width, rows), one, more_y, two, more_x, carry=resident
            )
        other = flip(held, 1, row_size)
        bits = []
        bit = 2
        while bit < row_size:
            bits.append(bit)
            bit *= 2
        pieces = 1 if (rows // col_size) % 128 else col_size
        late = pieces // 2
        for forward, backward in list(zip(bits, bits[::-1]))[:-1]:
            ra = flip(a, forward, row_size)
            rb = flip(b, backward, row_size)
            if bits[0] == forward:
                kct, right, *chunks, resident = across_call(
                    across_kernel,
                    (held, other, again),
                    (shape(width, columns), shape(columns, 2 * width, dtype=bf16)),
                    resident,
                    pieces,
                    late,
                    pieces - late,
                    width,
                )
            a, b, resident = small_call(
                pair_kernel, (quarter, quarter), a, ra, b, rb, carry=resident
            )
        ra = flip(a, bits[-1], row_size)
        rb = flip(b, bits[0], row_size)
        received = []
        if late:
            received = [shift(chunks[at], late + at, col_size) for at in range(pieces - late)]
            *chunks, resident = across_call(
                more_kernel, (right,), (), resident, pieces, 0, late, width
            )
            received += [shift(chunks[by], by, col_size) for by in range(1, late)]
        summed, resident = small_call(
            join_kernel, shape(width, columns // 2), a, ra, b, rb, carry=resident
        )
        xct, inner, resident = small_call(
            inner_kernel,
            (shape(width, columns), small),
            kct,
            summed,
            flip(summed, 1, row_size),
            carry=resident,
        )
        tall = packing(width, rows // pieces)[1]
        mine, resident = small_call(
            line_kernel,
            shape(width + tall, rows // pieces),
            chunks[0],
            *received,
            inner,
            carry=resident,
        )
        if pieces == 1:
            whole = [lax.psum(mine, "col")]
        else:
            whole = [mine] + [shift(mine, by, col_size) for by in range(1, col_size)]
        st, resident = small_call(
            invert_kernel, small, head, again, band_inverse, flops=50_000_000, carry=resident
        )
        xparts, kparts, krt, near_left, resident = small_call(
            wide_kernel,
            (
                shape(2 * width, columns, dtype=bf16),
                shape(2 * width, columns, dtype=bf16),
                shape(width, rows),
                shape(rows, 2 * width, dtype=bf16),
            ),
            st,
            xct,
            kct,
            first,
            second,
            again,
            mib=12,
            carry=resident,
        )
        resident = subtract_near(near_left, xparts, *resident)
        core, resident = small_call(
            core_kernel, shape(width, rows), st, krt, *whole, carry=resident
        )
        left, resident = small_call(
            left_kernel,
            shape(rows, 2 * width, dtype=bf16),
            st,
            core,
            *whole,
            mib=12,
            carry=resident,
        )
        return subtract_far(left, kparts, near_left, xparts, *resident), band

    return body


def solution(mesh):
    body = body_of(mesh.shape["row"], mesh.shape["col"])

    return jax.shard_map(
        body,
        mesh=mesh,
        in_specs=(P("row", "col"), P("row", None)),
        out_specs=(P("row", "col"), P()),
        check_vma=False,
    )
```

```python
import jax
import jax.numpy as jnp
from jax import lax
from jax.experimental import pallas as pl
from jax.experimental.pallas import tpu as pltpu
from jax.sharding import PartitionSpec as P


precise = lax.Precision.HIGHEST
f32 = jnp.float32
bf16 = jnp.bfloat16


def shape(*dims, dtype=f32):
    return jax.ShapeDtypeStruct(dims, dtype)


def params(mib):
    return pltpu.CompilerParams(vmem_limit_bytes=mib * 1024 * 1024)


def cost(flops, moved):
    return pl.CostEstimate(flops=flops, bytes_accessed=moved, transcendentals=0)


def dot(a, b):
    return jnp.dot(a, b, precision=precise, preferred_element_type=f32)


def fast(a, b):
    return jnp.dot(a, b, preferred_element_type=f32)


def split(value):
    high = value.astype(bf16)
    return high, (value - high.astype(f32)).astype(bf16)


def block_of(size, wanted):
    while size % wanted:
        wanted //= 2
    return wanted


def small_call(kernel, out, *operands, carry=(), flops=1_000_000, moved=1_000_000, mib=8):
    extra = {}
    body = kernel
    if carry:
        outs = out if isinstance(out, tuple) else (out,)
        count, more = len(operands), len(carry)
        anywhere = pl.BlockSpec(memory_space=pl.ANY)
        whole = pl.BlockSpec(memory_space=pltpu.VMEM)
        extra = dict(
            in_specs=[whole] * count + [anywhere] * more,
            out_specs=(whole,) * len(outs) + (anywhere,) * more,
            input_output_aliases={count + k: len(outs) + k for k in range(more)},
        )
        operands = operands + tuple(carry)
        out = outs + tuple(shape(*x.shape) for x in carry)

        def body(*refs):
            kernel(*refs[:count], *refs[count + more : -more])

    result = pl.pallas_call(
        body, out_shape=out, compiler_params=params(mib), cost_estimate=cost(flops, moved), **extra
    )(*operands)
    if carry:
        return tuple(result[: -len(carry)]) + (tuple(result[-len(carry) :]),)
    return result


def open_kernel(turned_ref, first_ref, second_ref, packed_ref):
    width = turned_ref.shape[0]
    half = first_ref.shape[1]
    turned = turned_ref[...]
    first_ref[...] = turned[:, :half]
    second_ref[...] = turned[:, half:]
    gram = lax.dot_general(
        turned, turned, (((1,), (1,)), ((), ())), precision=precise, preferred_element_type=f32
    )
    head = jnp.where(lax.axis_index("row") == 0, turned[:, : 2 * width].T[:width], 0.0)
    packed_ref[...] = jnp.concatenate([gram, head], 1)


def add_cores_kernel(first_ref, second_ref, a_ref, b_ref, x_ref, y_ref, sum_ref):
    half = first_ref.shape[1]
    total = a_ref[...] + b_ref[...]
    sum_ref[...] = total
    for source, target in ((first_ref, x_ref), (second_ref, y_ref)):
        target[:, :half] = source[...]
        target[:, half:] = total


def add_kernel(*refs):
    total = refs[0][...]
    for ref in refs[1:-1]:
        total = total + ref[...]
    refs[-1][...] = total


def spread(tile, at):
    return jnp.broadcast_to(tile[at : at + 1, :], tile.shape)


def pick(tile, at):
    return jnp.broadcast_to(tile[:, at : at + 1], tile.shape)


def sweep(tiles, order, full):
    lane = lax.broadcasted_iota(jnp.int32, (8, order), 1)
    sub = lax.broadcasted_iota(jnp.int32, (8, order), 0)
    tiles = list(tiles)
    for at in range(order // 8):
        base = 8 * at
        inside = (lane >= base) & (lane < base + 8)
        tile = tiles[at]
        others = [t for t in range(order // 8) if (t != at if full else t > at)]
        picked = {t: [pick(tiles[t], base + q) for q in range(8)] for t in others}
        columns = [pick(tile, base + q) for q in range(8)]
        rows = jnp.where(inside, jnp.where(lane - base == sub, 1.0, 0.0), tile)
        lower, upper = rows, tile
        for q in range(8):
            here = sub == q
            inverse = 1.0 / spread(columns[q], q)
            scaled = spread(rows, q) * inverse
            if not full:
                lower = jnp.where(here, rows, lower)
                upper = jnp.where(
                    sub > q, upper - columns[q] * (spread(upper, q) * inverse), upper
                )
            rows = jnp.where(here, scaled, rows - columns[q] * scaled)
            for p in range(q + 1, 8):
                part = spread(columns[p], q) * inverse
                columns[p] = jnp.where(here, part, columns[p] - columns[q] * part)
        finals = [spread(rows, q) for q in range(8)]
        for t in others:
            value = jnp.where(inside, 0.0, tiles[t])
            for q in range(8):
                value = value - picked[t][q] * finals[q]
            tiles[t] = value
        tiles[at] = rows if full else jnp.where(inside & (lane - base >= sub), upper, lower)
    return tiles


def eliminate_kernel(a_ref, b_ref, c_ref, d_ref, band_ref, again_ref, inverse_ref, head_ref):
    order = band_ref.shape[0]
    lane = lax.broadcasted_iota(jnp.int32, (8, order), 1)
    sub = lax.broadcasted_iota(jnp.int32, (8, order), 0)
    skip = b_ref.shape[1] - a_ref.shape[1]
    total = (a_ref[...] + b_ref[:, skip:]) + (c_ref[:, skip:] + d_ref[...])
    head_ref[...] = total[:, order:]
    gram = total[:, :order]
    tiles = sweep([gram[8 * t : 8 * t + 8, :] for t in range(order // 8)], order, False)
    for t in range(order // 8):
        row_at = sub + 8 * t
        diagonal = jnp.sum(jnp.where(lane == row_at, tiles[t], 0.0), axis=1, keepdims=True)
        length = jnp.sqrt(diagonal)
        scaled = tiles[t] / length
        band = jnp.where(lane > row_at, -scaled, jnp.where(lane == row_at, -length, 0.0))
        band_ref[8 * t : 8 * t + 8, :] = band
        again_ref[8 * t : 8 * t + 8, :] = band
        inverse_ref[8 * t : 8 * t + 8, :] = jnp.where(
            lane < row_at, -scaled, jnp.where(lane == row_at, -1.0 / length, 0.0)
        )


def invert_kernel(head_ref, band_ref, inverse_ref, out_ref):
    order = head_ref.shape[0]
    tiles = [
        head_ref[8 * t : 8 * t + 8, :] - band_ref[8 * t : 8 * t + 8, :] for t in range(order // 8)
    ]
    tiles = sweep(tiles, order, True)
    out_ref[...] = -dot(jnp.concatenate(tiles, 0), inverse_ref[...])


def parts_of(columns):
    return 2 if columns % 512 else 4


def down_kernel(first_ref, second_ref, a_ref, low_ref, high_ref, *refs):
    kept, sems = refs[:-1], refs[-1]
    width = low_ref.shape[0]
    span = kept[0].shape[1]
    count = sems.shape[0] // len(kept)
    size = span // count

    def load(at, i):
        start = pl.multiple_of(i * size, size)
        source = a_ref.at[:, pl.ds(pl.multiple_of(at * span + start, size), size)]
        target = kept[at].at[:, pl.ds(start, size)]
        return pltpu.make_async_copy(source, target, sems.at[at * count + i])

    for at in range(len(kept)):
        for i in range(count):
            load(at, i).start()
    kh, kl = split(jnp.concatenate([first_ref[...], second_ref[...]], 1))
    left = jnp.concatenate([kh, kl], 0)
    for at, ref in enumerate(kept):
        half, place = divmod(at, len(kept) // 2)
        out = (low_ref, high_ref)[half]

        @pl.loop(0, count)
        def _(i):
            load(at, i).wait()
            start = pl.multiple_of(i * size, size)
            ah, al = split(ref[:, pl.ds(start, size)])
            term = fast(left, ah) + fast(left, al)
            into = pl.ds(pl.multiple_of(place * span + start, size), size)
            out[:, into] = term[:width] + term[width:]


def product_down(first, second, a):
    rows, columns = a.shape
    width = first.shape[0]
    parts = parts_of(columns)
    span = columns // parts
    size = block_of(span, 256)
    whole = pl.BlockSpec(memory_space=pltpu.VMEM)
    low, high, *kept = pl.pallas_call(
        down_kernel,
        in_specs=[whole, whole, pl.BlockSpec(memory_space=pltpu.HBM)],
        out_specs=(whole,) * (2 + parts),
        out_shape=(shape(width, columns // 2),) * 2 + (shape(rows, span),) * parts,
        scratch_shapes=[pltpu.SemaphoreType.DMA((columns // size,))],
        compiler_params=params(12),
        cost_estimate=cost(8 * rows * columns * width, 4 * rows * columns),
        name="product_down",
    )(first, second, pltpu.with_memory_space_constraint(a, pltpu.HBM))
    return low, high, tuple(kept)


def fix_kernel(parts, low_ref, high_ref, band_ref, *refs):
    tops, keep_ref, give_ref = refs[:parts], refs[parts], refs[parts + 1]
    row = lax.axis_index("row")
    core = lax.rem(row, 2)
    first, second = low_ref[...], high_ref[...]
    span = tops[0].shape[1]

    @pl.when(row == 0)
    def _():
        rh, rl = split(band_ref[...].T)
        left = jnp.concatenate([rh, rl, rh, rl], 1)
        for at, top in enumerate(tops):
            half, place = divmod(at, parts // 2)
            ah, al = split(top[...])
            value = (first, second)[half][:, place * span : (place + 1) * span]
            (keep_ref, give_ref)[half][:, place * span : (place + 1) * span] = value - fast(
                left, jnp.concatenate([ah, ah, al, al], 0)
            )

    @pl.when((row != 0) & (core == 0))
    def _():
        keep_ref[...] = first
        give_ref[...] = second

    @pl.when(core == 1)
    def _():
        keep_ref[...] = second
        give_ref[...] = first


def fix_down(low, high, band, kept):
    width, half = low.shape
    parts = len(kept)
    side = pl.BlockSpec((width, half), lambda i: (0, 0))
    top = pl.BlockSpec((width, kept[0].shape[1]), lambda i: (0, 0))
    anywhere = pl.BlockSpec(memory_space=pl.ANY)

    def kernel(*refs):
        fix_kernel(parts, *refs)

    keep, give, *kept = pl.pallas_call(
        kernel,
        grid=(1,),
        in_specs=[side, side, pl.BlockSpec((width, width), lambda i: (0, 0))] + [top] * parts,
        out_specs=(side, side) + (anywhere,) * parts,
        out_shape=(shape(width, half),) * 2 + tuple(shape(*x.shape) for x in kept),
        input_output_aliases={3 + k: 2 + k for k in range(parts)},
        compiler_params=params(12),
        cost_estimate=cost(24 * width * width * half, 32 * width * half),
        name="fix_down",
    )(low, high, band, *kept)
    return keep, give, tuple(kept)


def rows_product(right_ref, halves, outs):
    span = halves[0].shape[1]
    width = right_ref.shape[1] // 2
    chunk = block_of(span, 512)
    total = None
    for at, a_ref in enumerate(halves):
        for c in range(0, span, chunk):
            ah, al = split(a_ref[:, c : c + chunk])
            right = right_ref[at * span + c : at * span + c + chunk, :]
            term = fast(ah, right) + fast(al, right)
            total = term if total is None else total + term
    result = (total[:, :width] + total[:, width:]).T
    for at, out_ref in enumerate(outs):

        @pl.when(pl.program_id(0) == at)
        def _():
            out_ref[...] = result


def across_kernel(parts, held_ref, other_ref, band_ref, *refs):
    kct_ref, right_ref = refs[parts : parts + 2]
    width, half = held_ref.shape
    columns = 2 * half
    chunk = block_of(columns, 512)

    @pl.when(pl.program_id(0) == 0)
    def _():
        core = lax.rem(lax.axis_index("row"), 2)

        @pl.when(core == 0)
        def _():
            kct_ref[:, :half] = held_ref[...]
            kct_ref[:, half:] = other_ref[...]

        @pl.when(core == 1)
        def _():
            kct_ref[:, :half] = other_ref[...]
            kct_ref[:, half:] = held_ref[...]

        @pl.when(lax.axis_index("col") == 0)
        def _():
            kct_ref[:, :width] = kct_ref[:, :width] - band_ref[...].T

        for c in range(0, columns, chunk):
            right_ref[c : c + chunk, :] = jnp.concatenate(split(kct_ref[:, c : c + chunk].T), 1)

    rows_product(right_ref, refs[:parts], refs[parts + 2 : -parts])


def more_kernel(parts, right_ref, *refs):
    rows_product(right_ref, refs[:parts], refs[parts:-parts])


def across_call(kernel, operands, extra, kept, pieces, start, count, width):
    rows, span = kept[0].shape
    parts = len(kept)
    size = rows // pieces

    def turn(i):
        return (lax.rem(i + start + lax.axis_index("col"), pieces), 0)

    def fixed(array):
        return pl.BlockSpec(array.shape, lambda i: (0, 0))

    def body(*refs):
        kernel(parts, *refs)

    outs = tuple(extra) + (shape(width, size),) * count
    at, to = len(operands), len(outs)
    results = pl.pallas_call(
        body,
        grid=(count,),
        in_specs=[fixed(x) for x in operands] + [pl.BlockSpec((size, span), turn)] * parts,
        out_specs=tuple(fixed(x) for x in outs) + (pl.BlockSpec(memory_space=pl.ANY),) * parts,
        out_shape=outs + (shape(rows, span),) * parts,
        input_output_aliases={at + k: to + k for k in range(parts)},
        compiler_params=params(22),
        cost_estimate=cost(8 * size * count * span * parts * width, 4 * size * count * span * parts),
    )(*operands, *kept)
    return (*results[:to], tuple(results[to:]))


def merge_first_kernel(first_ref, second_ref, by_x_ref, by_y_ref, a_ref, b_ref):
    half = a_ref.shape[1]
    relation = lax.div(lax.axis_index("row"), 2) ^ lax.axis_index("col")
    for at, own, got, out in (
        (1, first_ref, by_x_ref, a_ref),
        (2, second_ref, by_y_ref, b_ref),
    ):
        out[...] = jnp.where(
            relation == 0, own[...], jnp.where(relation == at, got[:, :half], 0.0)
        )


def join_kernel(a_ref, b_ref, c_ref, d_ref, out_ref):
    half = a_ref.shape[1]
    out_ref[:, :half] = a_ref[...] + b_ref[...]
    out_ref[:, half:] = c_ref[...] + d_ref[...]


def halve_kernel(keep_ref, other_ref, a_ref, b_ref):
    half = a_ref.shape[1]
    a_ref[...] = keep_ref[:, :half] + other_ref[:, :half]
    b_ref[...] = keep_ref[:, half:] + other_ref[:, half:]


def pair_kernel(a_ref, b_ref, c_ref, d_ref, e_ref, f_ref):
    e_ref[...] = a_ref[...] + b_ref[...]
    f_ref[...] = c_ref[...] + d_ref[...]


def inner_kernel(kct_ref, held_ref, other_ref, xct_ref, inner_ref):
    half = held_ref.shape[1]
    core = lax.rem(lax.axis_index("row"), 2)

    @pl.when(core == 0)
    def _():
        xct_ref[:, :half] = held_ref[...]
        xct_ref[:, half:] = other_ref[...]

    @pl.when(core == 1)
    def _():
        xct_ref[:, :half] = other_ref[...]
        xct_ref[:, half:] = held_ref[...]

    inner_ref[...] = lax.dot_general(
        kct_ref[...],
        xct_ref[...],
        (((1,), (1,)), ((), ())),
        precision=precise,
        preferred_element_type=f32,
    )


def wide_kernel(
    st_ref, xct_ref, kct_ref, first_ref, second_ref, band_ref, x_ref, k_ref, rows_ref, left_ref
):
    width, columns = kct_ref.shape
    st = st_ref[...]
    chunk = block_of(columns, 512)
    for c in range(0, columns, chunk):
        for ref, value in (
            (x_ref, dot(st, xct_ref[:, c : c + chunk])),
            (k_ref, kct_ref[:, c : c + chunk]),
        ):
            ref[:, c : c + chunk] = jnp.concatenate(split(value), 0)
    half = first_ref.shape[1]
    rows_ref[:, :half] = first_ref[...]
    rows_ref[:, half:] = second_ref[...]

    @pl.when(lax.axis_index("row") == 0)
    def _():
        rows_ref[:, :width] = rows_ref[:, :width] - band_ref[...].T

    rows = rows_ref.shape[1]
    deep = block_of(rows, 512)
    for r in range(0, rows, deep):
        left_ref[r : r + deep, :] = jnp.concatenate(split(rows_ref[:, r : r + deep].T), 1)


def both_parts(left):
    return jnp.concatenate([left, left], 1)


def four_parts(right_ref, start, size):
    width = right_ref.shape[0] // 2
    high = right_ref[:width, pl.ds(start, size)]
    low = right_ref[width:, pl.ds(start, size)]
    return jnp.concatenate([high, high, low, low], 0)


def near_kernel(count, left_ref, right_ref, *refs):
    total = (len(refs)) // 2
    rows, span = refs[0].shape
    deep = block_of(rows, 512)
    chunk = block_of(span, 512)
    if (span // 2) % 128 == 0:
        chunk = span // 2
    for at in range(count):
        a_ref, out_ref = refs[at], refs[total + at]

        @pl.loop(0, span // chunk)
        def _(i):
            c = pl.multiple_of(i * chunk, chunk)
            right = four_parts(right_ref, pl.multiple_of(at * span + c, 128), chunk)
            for r in range(0, rows, deep):
                out_ref[r : r + deep, pl.ds(c, chunk)] = a_ref[
                    r : r + deep, pl.ds(c, chunk)
                ] - fast(both_parts(left_ref[r : r + deep, :]), right)


def near_count(parts):
    return parts - max(1, parts // 4)


def subtract_near(left, right, kept):
    rows, span = kept[0].shape
    parts = len(kept)
    count = near_count(parts)
    deep = left.shape[1]
    whole = pl.BlockSpec(memory_space=pltpu.VMEM)
    places = [whole] * count + [pl.BlockSpec(memory_space=pl.ANY)] * (parts - count)

    def kernel(*refs):
        near_kernel(count, *refs)

    return tuple(
        pl.pallas_call(
            kernel,
            in_specs=[whole] * 2 + places,
            out_specs=tuple(places),
            out_shape=(shape(rows, span),) * parts,
            input_output_aliases={2 + k: k for k in range(parts)},
            compiler_params=params(12),
            cost_estimate=cost(4 * rows * span * count * deep, 8 * rows * span * count),
            name="subtract_near",
        )(left, right, *kept)
    )


def core_blocks(width):
    half = width // 2
    return [(0, 0), (0, half), (half, half)], half


def packing(width, size):
    half = width // 2
    beside = 1
    while 6 * beside * half <= size and 2 * beside <= half // 8:
        beside *= 2
    return beside, half // beside


def line_kernel(*refs):
    *chunks, inner_ref, out_ref = refs
    width, size = chunks[0].shape
    beside, tall = packing(width, size)
    blocks, half = core_blocks(width)
    total = chunks[0][...]
    for ref in chunks[1:]:
        total = total + ref[...]
    out_ref[:width, :] = total
    below = [
        inner_ref[r + k * tall : r + (k + 1) * tall, c : c + half]
        for r, c in blocks
        for k in range(beside)
    ]
    spare = size - half * len(below)
    if spare:
        below.append(jnp.zeros((tall, spare), f32))
    out_ref[width:, :] = jnp.concatenate(below, 1)


def core_kernel(st_ref, krt_ref, *refs):
    chunks, out_ref = refs[:-1], refs[-1]
    width = st_ref.shape[0]
    beside, _ = packing(width, chunks[0].shape[1])
    half = core_blocks(width)[1]
    packed = chunks[0][width:, :]
    for ref in chunks[1:]:
        packed = packed + ref[width:, :]
    near, cross, far = (
        jnp.concatenate(
            [packed[:, (b * beside + k) * half : (b * beside + k + 1) * half] for k in range(beside)],
            0,
        )
        for b in range(3)
    )
    inner = jnp.concatenate(
        [jnp.concatenate([near, cross], 1), jnp.concatenate([cross.T, far], 1)], 0
    )
    st = st_ref[...]
    cm = dot(dot(st, inner), st.T)
    out_ref[...] = dot(cm, krt_ref[...])


def left_kernel(st_ref, core_ref, *refs):
    chunks, left_ref = refs[:-1], refs[-1]
    pieces = len(chunks)
    size = chunks[0].shape[1]
    st = st_ref[...]
    col = lax.axis_index("col")
    for at, ref in enumerate(chunks):
        start = pl.multiple_of(lax.rem(col + pieces - at, pieces) * size, size)
        value = dot(st, ref[: st.shape[0], :]) - core_ref[:, pl.ds(start, size)]
        left_ref[pl.ds(start, size), :] = jnp.concatenate(split(value.T), 1)


def far_kernel(count, left_ref, right_ref, near_left_ref, near_right_ref, *refs):
    *kept, out_ref, buffer, sems = refs
    rows, span = kept[0].shape
    slots, deep, _ = buffer.shape
    turns = len(kept)
    down = rows // deep

    def store(i, slot):
        turn, pair = lax.rem(i, turns), lax.div(i, turns)
        r = pl.multiple_of(pair * deep, deep)
        c = pl.multiple_of(turn * span, span)
        return pltpu.make_async_copy(
            buffer.at[slot], out_ref.at[pl.ds(r, deep), pl.ds(c, span)], sems.at[slot]
        )

    @pl.loop(0, down)
    def _(pair):
        r = pl.multiple_of(pair * deep, deep)
        for turn, a_ref in enumerate(kept):
            i = pair * turns + turn
            slot = lax.rem(i, slots)

            @pl.when(i >= slots)
            def _():
                store(i - slots, slot).wait()

            left = both_parts(left_ref[pl.ds(r, deep), :])
            right = four_parts(right_ref, turn * span, span)
            if turn >= count:
                left = jnp.concatenate([left, both_parts(near_left_ref[pl.ds(r, deep), :])], 1)
                right = jnp.concatenate([right, four_parts(near_right_ref, turn * span, span)], 0)
            buffer[slot] = a_ref[pl.ds(r, deep), :] - fast(left, right)
            store(i, slot).start()

    for back in range(slots, 0, -1):
        store(down * turns - back, (down * turns - back) % slots).wait()


def subtract_far(left, right, near_left, near_right, kept):
    rows, span = kept[0].shape
    parts = len(kept)
    deep = left.shape[1]
    whole = pl.BlockSpec(memory_space=pltpu.VMEM)

    def kernel(*refs):
        far_kernel(near_count(parts), *refs)

    return pl.pallas_call(
        kernel,
        in_specs=[whole] * (4 + parts),
        out_specs=pl.BlockSpec(memory_space=pltpu.HBM),
        out_shape=shape(rows, parts * span),
        scratch_shapes=[
            pltpu.VMEM((3, block_of(rows, 512), span), f32),
            pltpu.SemaphoreType.DMA((3,)),
        ],
        compiler_params=params(12),
        cost_estimate=cost(5 * rows * span * parts * deep, 8 * rows * span * parts),
        name="subtract_far",
    )(left, right, near_left, near_right, *kept)


def flip(value, bit, size, axis="row"):
    return lax.ppermute(value, axis, [(i, i ^ bit) for i in range(size)])


def from_sources(piece, col_size, source_flips, bit):
    pairs = []
    for c in range(col_size):
        for source in source_flips:
            for core in range(2):
                at = (2 * c + core) ^ source
                pairs.append((at * col_size + c, (at ^ bit) * col_size + c))
    return lax.ppermute(piece, ("row", "col"), pairs)


def shift(piece, by, size):
    return lax.ppermute(piece, "col", [(i, (i + by) % size) for i in range(size)])


def body_of(row_size, col_size):
    assert row_size == 2 * col_size

    def body(matrix, panel):
        rows, width = panel.shape
        columns = matrix.shape[1]
        small = shape(width, width)
        packed = shape(width, 2 * width)
        half = shape(width, rows // 2)
        first, second, partial = small_call(
            open_kernel, (half, half, packed), panel.T, flops=100_000_000, mib=12
        )
        apart = flip(partial, 1, row_size)
        if row_size == 8:
            wide_half = shape(width, rows // 2 + 2 * width)
            send_x, send_y, partial = small_call(
                add_cores_kernel, (wide_half, wide_half, packed), first, second, partial, apart
            )
            by_x = flip(send_x, 2, row_size)
            by_y = flip(send_y, 4, row_size)
            terms = [partial, by_x, by_y, flip(partial, 6, row_size)]
        else:
            partial = small_call(add_kernel, packed, partial, apart)
            bit = 2
            total = partial
            while bit < row_size // 2:
                total = total + flip(total, bit, row_size)
                bit *= 2
            zero = jnp.zeros_like(total)
            terms = [total, flip(total, row_size // 2, row_size), zero, zero]
        first, second, partial = lax.optimization_barrier((first, second, partial))
        low, high, resident = product_down(first, second, matrix)
        if row_size == 8:
            one, two, resident = small_call(
                merge_first_kernel, (half, half), first, second, by_x, by_y, carry=resident
            )
            more_x = flip(two, 2, row_size)
            more_y = flip(one, 4, row_size)
        else:
            relation = (lax.axis_index("row") // 2) ^ lax.axis_index("col")
            held = jnp.where(relation == 0, jnp.concatenate([first, second], 1), 0.0)
            reached = [0]
            bit = 2
            while bit < row_size:
                held = held + from_sources(held, col_size, reached, bit)
                reached = reached + [r ^ bit for r in reached]
                bit *= 2
        band, again, band_inverse, head, resident = small_call(
            eliminate_kernel, (small, small, small, small), *terms, flops=50_000_000, carry=resident
        )
        keep, give, resident = fix_down(low, high, again, resident)
        if row_size == 8:
            held, resident = small_call(
                join_kernel, shape(width, rows), one, more_y, two, more_x, carry=resident
            )
        other = flip(held, 1, row_size)
        quarter = shape(width, columns // 4)
        a, b, resident = small_call(
            halve_kernel, (quarter, quarter), keep, flip(give, 1, row_size), carry=resident
        )
        bits = []
        bit = 2
        while bit < row_size:
            bits.append(bit)
            bit *= 2
        pieces = 1 if (rows // col_size) % 128 else col_size
        late = pieces // 2
        for forward, backward in list(zip(bits, bits[::-1]))[:-1]:
            ra = flip(a, forward, row_size)
            rb = flip(b, backward, row_size)
            if bits[0] == forward:
                kct, right, *chunks, resident = across_call(
                    across_kernel,
                    (held, other, again),
                    (shape(width, columns), shape(columns, 2 * width, dtype=bf16)),
                    resident,
                    pieces,
                    late,
                    pieces - late,
                    width,
                )
            a, b, resident = small_call(
                pair_kernel, (quarter, quarter), a, ra, b, rb, carry=resident
            )
        ra = flip(a, bits[-1], row_size)
        rb = flip(b, bits[0], row_size)
        received = []
        if late:
            received = [shift(chunks[at], late + at, col_size) for at in range(pieces - late)]
            *chunks, resident = across_call(
                more_kernel, (right,), (), resident, pieces, 0, late, width
            )
            received += [shift(chunks[by], by, col_size) for by in range(1, late)]
        summed, resident = small_call(
            join_kernel, shape(width, columns // 2), a, ra, b, rb, carry=resident
        )
        xct, inner, resident = small_call(
            inner_kernel,
            (shape(width, columns), small),
            kct,
            summed,
            flip(summed, 1, row_size),
            carry=resident,
        )
        tall = packing(width, rows // pieces)[1]
        mine, resident = small_call(
            line_kernel,
            shape(width + tall, rows // pieces),
            chunks[0],
            *received,
            inner,
            carry=resident,
        )
        if pieces == 1:
            whole = [lax.psum(mine, "col")]
        else:
            whole = [mine] + [shift(mine, by, col_size) for by in range(1, col_size)]
        st, resident = small_call(
            invert_kernel, small, head, again, band_inverse, flops=50_000_000, carry=resident
        )
        xparts, kparts, krt, near_left, resident = small_call(
            wide_kernel,
            (
                shape(2 * width, columns, dtype=bf16),
                shape(2 * width, columns, dtype=bf16),
                shape(width, rows),
                shape(rows, 2 * width, dtype=bf16),
            ),
            st,
            xct,
            kct,
            first,
            second,
            again,
            mib=12,
            carry=resident,
        )
        resident = subtract_near(near_left, xparts, resident)
        core, resident = small_call(
            core_kernel, shape(width, rows), st, krt, *whole, carry=resident
        )
        left, resident = small_call(
            left_kernel,
            shape(rows, 2 * width, dtype=bf16),
            st,
            core,
            *whole,
            mib=12,
            carry=resident,
        )
        return subtract_far(left, kparts, near_left, xparts, resident), band

    return body


def solution(mesh):
    body = body_of(mesh.shape["row"], mesh.shape["col"])

    return jax.shard_map(
        body,
        mesh=mesh,
        in_specs=(P("row", "col"), P("row", None)),
        out_specs=(P("row", "col"), P()),
        check_vma=False,
    )
```

```python
import jax
import jax.numpy as jnp
from jax import lax
from jax.experimental import pallas as pl
from jax.experimental.pallas import tpu as pltpu
from jax.sharding import PartitionSpec as P


precise = lax.Precision.HIGHEST
f32 = jnp.float32
bf16 = jnp.bfloat16


def shape(*dims, dtype=f32):
    return jax.ShapeDtypeStruct(dims, dtype)


def params(mib):
    return pltpu.CompilerParams(vmem_limit_bytes=mib * 1024 * 1024)


def cost(flops, moved):
    return pl.CostEstimate(flops=flops, bytes_accessed=moved, transcendentals=0)


def dot(a, b):
    return jnp.dot(a, b, precision=precise, preferred_element_type=f32)


def fast(a, b):
    return jnp.dot(a, b, preferred_element_type=f32)


def split(value):
    high = value.astype(bf16)
    return high, (value - high.astype(f32)).astype(bf16)


def block_of(size, wanted):
    while size % wanted:
        wanted //= 2
    return wanted


def small_call(kernel, out, *operands, carry=(), flops=1_000_000, moved=1_000_000, mib=8):
    extra = {}
    body = kernel
    if carry:
        outs = out if isinstance(out, tuple) else (out,)
        count, more = len(operands), len(carry)
        anywhere = pl.BlockSpec(memory_space=pl.ANY)
        whole = pl.BlockSpec(memory_space=pltpu.VMEM)
        extra = dict(
            in_specs=[whole] * count + [anywhere] * more,
            out_specs=(whole,) * len(outs) + (anywhere,) * more,
            input_output_aliases={count + k: len(outs) + k for k in range(more)},
        )
        operands = operands + tuple(carry)
        out = outs + tuple(shape(*x.shape) for x in carry)

        def body(*refs):
            kernel(*refs[:count], *refs[count + more : -more])

    result = pl.pallas_call(
        body, out_shape=out, compiler_params=params(mib), cost_estimate=cost(flops, moved), **extra
    )(*operands)
    if carry:
        return tuple(result[: -len(carry)]) + (tuple(result[-len(carry) :]),)
    return result


def open_kernel(turned_ref, first_ref, second_ref, packed_ref):
    width = turned_ref.shape[0]
    half = first_ref.shape[1]
    turned = turned_ref[...]
    first_ref[...] = turned[:, :half]
    second_ref[...] = turned[:, half:]
    gram = lax.dot_general(
        turned, turned, (((1,), (1,)), ((), ())), precision=precise, preferred_element_type=f32
    )
    head = jnp.where(lax.axis_index("row") == 0, turned[:, : 2 * width].T[:width], 0.0)
    packed_ref[...] = jnp.concatenate([gram, head], 1)


def add_cores_kernel(first_ref, second_ref, a_ref, b_ref, x_ref, y_ref, sum_ref):
    half = first_ref.shape[1]
    total = a_ref[...] + b_ref[...]
    sum_ref[...] = total
    for source, target in ((first_ref, x_ref), (second_ref, y_ref)):
        target[:, :half] = source[...]
        target[:, half:] = total


def add_kernel(*refs):
    total = refs[0][...]
    for ref in refs[1:-1]:
        total = total + ref[...]
    refs[-1][...] = total


def spread(tile, at):
    return jnp.broadcast_to(tile[at : at + 1, :], tile.shape)


def pick(tile, at):
    return jnp.broadcast_to(tile[:, at : at + 1], tile.shape)


def sweep(tiles, order, full):
    lane = lax.broadcasted_iota(jnp.int32, (8, order), 1)
    sub = lax.broadcasted_iota(jnp.int32, (8, order), 0)
    tiles = list(tiles)
    for at in range(order // 8):
        base = 8 * at
        inside = (lane >= base) & (lane < base + 8)
        tile = tiles[at]
        others = [t for t in range(order // 8) if (t != at if full else t > at)]
        picked = {t: [pick(tiles[t], base + q) for q in range(8)] for t in others}
        columns = [pick(tile, base + q) for q in range(8)]
        rows = jnp.where(inside, jnp.where(lane - base == sub, 1.0, 0.0), tile)
        lower, upper = rows, tile
        for q in range(8):
            here = sub == q
            inverse = 1.0 / spread(columns[q], q)
            scaled = spread(rows, q) * inverse
            if not full:
                lower = jnp.where(here, rows, lower)
                upper = jnp.where(
                    sub > q, upper - columns[q] * (spread(upper, q) * inverse), upper
                )
            rows = jnp.where(here, scaled, rows - columns[q] * scaled)
            for p in range(q + 1, 8):
                part = spread(columns[p], q) * inverse
                columns[p] = jnp.where(here, part, columns[p] - columns[q] * part)
        finals = [spread(rows, q) for q in range(8)]
        for t in others:
            value = jnp.where(inside, 0.0, tiles[t])
            for q in range(8):
                value = value - picked[t][q] * finals[q]
            tiles[t] = value
        tiles[at] = rows if full else jnp.where(inside & (lane - base >= sub), upper, lower)
    return tiles


def eliminate_kernel(a_ref, b_ref, c_ref, d_ref, band_ref, again_ref, inverse_ref, head_ref):
    order = band_ref.shape[0]
    lane = lax.broadcasted_iota(jnp.int32, (8, order), 1)
    sub = lax.broadcasted_iota(jnp.int32, (8, order), 0)
    skip = b_ref.shape[1] - a_ref.shape[1]
    total = (a_ref[...] + b_ref[:, skip:]) + (c_ref[:, skip:] + d_ref[...])
    head_ref[...] = total[:, order:]
    gram = total[:, :order]
    tiles = sweep([gram[8 * t : 8 * t + 8, :] for t in range(order // 8)], order, False)
    for t in range(order // 8):
        row_at = sub + 8 * t
        diagonal = jnp.sum(jnp.where(lane == row_at, tiles[t], 0.0), axis=1, keepdims=True)
        length = jnp.sqrt(diagonal)
        scaled = tiles[t] / length
        band = jnp.where(lane > row_at, -scaled, jnp.where(lane == row_at, -length, 0.0))
        band_ref[8 * t : 8 * t + 8, :] = band
        again_ref[8 * t : 8 * t + 8, :] = band
        inverse_ref[8 * t : 8 * t + 8, :] = jnp.where(
            lane < row_at, -scaled, jnp.where(lane == row_at, -1.0 / length, 0.0)
        )


def invert_kernel(head_ref, band_ref, inverse_ref, out_ref):
    order = head_ref.shape[0]
    tiles = [
        head_ref[8 * t : 8 * t + 8, :] - band_ref[8 * t : 8 * t + 8, :] for t in range(order // 8)
    ]
    tiles = sweep(tiles, order, True)
    out_ref[...] = -dot(jnp.concatenate(tiles, 0), inverse_ref[...])


def parts_of(columns):
    return 2 if columns % 512 else 4


def down_kernel(first_ref, second_ref, a_ref, low_ref, high_ref, *refs):
    kept, sems = refs[:-1], refs[-1]
    width = low_ref.shape[0]
    span = kept[0].shape[1]
    count = sems.shape[0] // len(kept)
    size = span // count

    def load(at, i):
        start = pl.multiple_of(i * size, size)
        source = a_ref.at[:, pl.ds(pl.multiple_of(at * span + start, size), size)]
        target = kept[at].at[:, pl.ds(start, size)]
        return pltpu.make_async_copy(source, target, sems.at[at * count + i])

    for at in range(len(kept)):
        for i in range(count):
            load(at, i).start()
    kh, kl = split(jnp.concatenate([first_ref[...], second_ref[...]], 1))
    left = jnp.concatenate([kh, kl], 0)
    for at, ref in enumerate(kept):
        half, place = divmod(at, len(kept) // 2)
        out = (low_ref, high_ref)[half]

        @pl.loop(0, count)
        def _(i):
            load(at, i).wait()
            start = pl.multiple_of(i * size, size)
            ah, al = split(ref[:, pl.ds(start, size)])
            term = fast(left, ah) + fast(left, al)
            into = pl.ds(pl.multiple_of(place * span + start, size), size)
            out[:, into] = term[:width] + term[width:]


def product_down(first, second, a):
    rows, columns = a.shape
    width = first.shape[0]
    parts = parts_of(columns)
    span = columns // parts
    size = block_of(span, 256)
    whole = pl.BlockSpec(memory_space=pltpu.VMEM)
    low, high, *kept = pl.pallas_call(
        down_kernel,
        in_specs=[whole, whole, pl.BlockSpec(memory_space=pltpu.HBM)],
        out_specs=(whole,) * (2 + parts),
        out_shape=(shape(width, columns // 2),) * 2 + (shape(rows, span),) * parts,
        scratch_shapes=[pltpu.SemaphoreType.DMA((columns // size,))],
        compiler_params=params(12),
        cost_estimate=cost(8 * rows * columns * width, 4 * rows * columns),
        name="product_down",
    )(first, second, pltpu.with_memory_space_constraint(a, pltpu.HBM))
    return low, high, tuple(kept)


def fix_kernel(parts, low_ref, high_ref, band_ref, *refs):
    tops, keep_ref, give_ref = refs[:parts], refs[parts], refs[parts + 1]
    row = lax.axis_index("row")
    core = lax.rem(row, 2)
    first, second = low_ref[...], high_ref[...]
    span = tops[0].shape[1]

    @pl.when(row == 0)
    def _():
        rh, rl = split(band_ref[...].T)
        left = jnp.concatenate([rh, rl, rh, rl], 1)
        for at, top in enumerate(tops):
            half, place = divmod(at, parts // 2)
            ah, al = split(top[...])
            value = (first, second)[half][:, place * span : (place + 1) * span]
            (keep_ref, give_ref)[half][:, place * span : (place + 1) * span] = value - fast(
                left, jnp.concatenate([ah, ah, al, al], 0)
            )

    @pl.when((row != 0) & (core == 0))
    def _():
        keep_ref[...] = first
        give_ref[...] = second

    @pl.when(core == 1)
    def _():
        keep_ref[...] = second
        give_ref[...] = first


def fix_down(low, high, band, kept):
    width, half = low.shape
    parts = len(kept)
    side = pl.BlockSpec((width, half), lambda i: (0, 0))
    top = pl.BlockSpec((width, kept[0].shape[1]), lambda i: (0, 0))
    anywhere = pl.BlockSpec(memory_space=pl.ANY)

    def kernel(*refs):
        fix_kernel(parts, *refs)

    keep, give, *kept = pl.pallas_call(
        kernel,
        grid=(1,),
        in_specs=[side, side, pl.BlockSpec((width, width), lambda i: (0, 0))] + [top] * parts,
        out_specs=(side, side) + (anywhere,) * parts,
        out_shape=(shape(width, half),) * 2 + tuple(shape(*x.shape) for x in kept),
        input_output_aliases={3 + k: 2 + k for k in range(parts)},
        compiler_params=params(12),
        cost_estimate=cost(24 * width * width * half, 32 * width * half),
        name="fix_down",
    )(low, high, band, *kept)
    return keep, give, tuple(kept)


def rows_product(right_ref, halves, outs):
    span = halves[0].shape[1]
    width = right_ref.shape[1] // 2
    chunk = block_of(span, 512)
    total = None
    for at, a_ref in enumerate(halves):
        for c in range(0, span, chunk):
            ah, al = split(a_ref[:, c : c + chunk])
            right = right_ref[at * span + c : at * span + c + chunk, :]
            term = fast(ah, right) + fast(al, right)
            total = term if total is None else total + term
    result = (total[:, :width] + total[:, width:]).T
    for at, out_ref in enumerate(outs):

        @pl.when(pl.program_id(0) == at)
        def _():
            out_ref[...] = result


def across_kernel(parts, held_ref, other_ref, band_ref, *refs):
    kct_ref, right_ref = refs[parts : parts + 2]
    width, half = held_ref.shape
    columns = 2 * half
    chunk = block_of(columns, 512)

    @pl.when(pl.program_id(0) == 0)
    def _():
        core = lax.rem(lax.axis_index("row"), 2)

        @pl.when(core == 0)
        def _():
            kct_ref[:, :half] = held_ref[...]
            kct_ref[:, half:] = other_ref[...]

        @pl.when(core == 1)
        def _():
            kct_ref[:, :half] = other_ref[...]
            kct_ref[:, half:] = held_ref[...]

        @pl.when(lax.axis_index("col") == 0)
        def _():
            kct_ref[:, :width] = kct_ref[:, :width] - band_ref[...].T

        for c in range(0, columns, chunk):
            right_ref[c : c + chunk, :] = jnp.concatenate(split(kct_ref[:, c : c + chunk].T), 1)

    rows_product(right_ref, refs[:parts], refs[parts + 2 : -parts])


def more_kernel(parts, right_ref, *refs):
    rows_product(right_ref, refs[:parts], refs[parts:-parts])


def across_call(kernel, operands, extra, kept, pieces, start, count, width):
    rows, span = kept[0].shape
    parts = len(kept)
    size = rows // pieces

    def turn(i):
        return (lax.rem(i + start + lax.axis_index("col"), pieces), 0)

    def fixed(array):
        return pl.BlockSpec(array.shape, lambda i: (0, 0))

    def body(*refs):
        kernel(parts, *refs)

    outs = tuple(extra) + (shape(width, size),) * count
    at, to = len(operands), len(outs)
    results = pl.pallas_call(
        body,
        grid=(count,),
        in_specs=[fixed(x) for x in operands] + [pl.BlockSpec((size, span), turn)] * parts,
        out_specs=tuple(fixed(x) for x in outs) + (pl.BlockSpec(memory_space=pl.ANY),) * parts,
        out_shape=outs + (shape(rows, span),) * parts,
        input_output_aliases={at + k: to + k for k in range(parts)},
        compiler_params=params(22),
        cost_estimate=cost(8 * size * count * span * parts * width, 4 * size * count * span * parts),
    )(*operands, *kept)
    return (*results[:to], tuple(results[to:]))


def merge_first_kernel(first_ref, second_ref, by_x_ref, by_y_ref, a_ref, b_ref):
    half = a_ref.shape[1]
    relation = lax.div(lax.axis_index("row"), 2) ^ lax.axis_index("col")
    for at, own, got, out in (
        (1, first_ref, by_x_ref, a_ref),
        (2, second_ref, by_y_ref, b_ref),
    ):
        out[...] = jnp.where(
            relation == 0, own[...], jnp.where(relation == at, got[:, :half], 0.0)
        )


def join_kernel(a_ref, b_ref, c_ref, d_ref, out_ref):
    half = a_ref.shape[1]
    out_ref[:, :half] = a_ref[...] + b_ref[...]
    out_ref[:, half:] = c_ref[...] + d_ref[...]


def halve_kernel(keep_ref, other_ref, a_ref, b_ref):
    half = a_ref.shape[1]
    a_ref[...] = keep_ref[:, :half] + other_ref[:, :half]
    b_ref[...] = keep_ref[:, half:] + other_ref[:, half:]


def pair_kernel(a_ref, b_ref, c_ref, d_ref, e_ref, f_ref):
    e_ref[...] = a_ref[...] + b_ref[...]
    f_ref[...] = c_ref[...] + d_ref[...]


def half_product(kct_ref, x_ref, core):
    half = x_ref.shape[1]
    start = pl.multiple_of(core * half, half)
    return lax.dot_general(
        kct_ref[:, pl.ds(start, half)],
        x_ref[...],
        (((1,), (1,)), ((), ())),
        precision=precise,
        preferred_element_type=f32,
    )


def inner_own_kernel(kct_ref, held_ref, inner_ref):
    inner_ref[...] = half_product(kct_ref, held_ref, lax.rem(lax.axis_index("row"), 2))


def inner_kernel(kct_ref, held_ref, other_ref, own_ref, xct_ref, inner_ref):
    half = held_ref.shape[1]
    core = lax.rem(lax.axis_index("row"), 2)

    @pl.when(core == 0)
    def _():
        xct_ref[:, :half] = held_ref[...]
        xct_ref[:, half:] = other_ref[...]

    @pl.when(core == 1)
    def _():
        xct_ref[:, :half] = other_ref[...]
        xct_ref[:, half:] = held_ref[...]

    inner_ref[...] = own_ref[...] + half_product(kct_ref, other_ref, 1 - core)


def wide_kernel(
    st_ref, xct_ref, kct_ref, first_ref, second_ref, band_ref, x_ref, k_ref, rows_ref, left_ref
):
    width, columns = kct_ref.shape
    st = st_ref[...]
    chunk = block_of(columns, 512)
    for c in range(0, columns, chunk):
        for ref, value in (
            (x_ref, dot(st, xct_ref[:, c : c + chunk])),
            (k_ref, kct_ref[:, c : c + chunk]),
        ):
            ref[:, c : c + chunk] = jnp.concatenate(split(value), 0)
    half = first_ref.shape[1]
    rows_ref[:, :half] = first_ref[...]
    rows_ref[:, half:] = second_ref[...]

    @pl.when(lax.axis_index("row") == 0)
    def _():
        rows_ref[:, :width] = rows_ref[:, :width] - band_ref[...].T

    rows = rows_ref.shape[1]
    deep = block_of(rows, 512)
    for r in range(0, rows, deep):
        left_ref[r : r + deep, :] = jnp.concatenate(split(rows_ref[:, r : r + deep].T), 1)


def both_parts(left):
    return jnp.concatenate([left, left], 1)


def four_parts(right_ref, start, size):
    width = right_ref.shape[0] // 2
    high = right_ref[:width, pl.ds(start, size)]
    low = right_ref[width:, pl.ds(start, size)]
    return jnp.concatenate([high, high, low, low], 0)


def near_kernel(count, left_ref, right_ref, *refs):
    total = (len(refs)) // 2
    rows, span = refs[0].shape
    deep = block_of(rows, 512)
    chunk = block_of(span, 512)
    if span % 256 == 0 and span <= 1024:
        chunk = span
    for at in range(count):
        a_ref, out_ref = refs[at], refs[total + at]

        @pl.loop(0, span // chunk)
        def _(i):
            c = pl.multiple_of(i * chunk, chunk)
            right = four_parts(right_ref, pl.multiple_of(at * span + c, 128), chunk)
            for r in range(0, rows, deep):
                out_ref[r : r + deep, pl.ds(c, chunk)] = a_ref[
                    r : r + deep, pl.ds(c, chunk)
                ] - fast(both_parts(left_ref[r : r + deep, :]), right)


def subtract_near(left, right, kept):
    rows, span = kept[0].shape
    parts = len(kept)
    count = parts
    deep = left.shape[1]
    whole = pl.BlockSpec(memory_space=pltpu.VMEM)
    places = [whole] * count + [pl.BlockSpec(memory_space=pl.ANY)] * (parts - count)

    def kernel(*refs):
        near_kernel(count, *refs)

    return tuple(
        pl.pallas_call(
            kernel,
            in_specs=[whole] * 2 + places,
            out_specs=tuple(places),
            out_shape=(shape(rows, span),) * parts,
            input_output_aliases={2 + k: k for k in range(parts)},
            compiler_params=params(12),
            cost_estimate=cost(4 * rows * span * count * deep, 8 * rows * span * count),
            name="subtract_near",
        )(left, right, *kept)
    )


def core_blocks(width):
    half = width // 2
    return [(0, 0), (0, half), (half, half)], half


def packing(width, size):
    half = width // 2
    beside = 1
    while 6 * beside * half <= size and 2 * beside <= half // 8:
        beside *= 2
    return beside, half // beside


def line_kernel(*refs):
    *chunks, inner_ref, out_ref = refs
    width, size = chunks[0].shape
    beside, tall = packing(width, size)
    blocks, half = core_blocks(width)
    total = chunks[0][...]
    for ref in chunks[1:]:
        total = total + ref[...]
    out_ref[:width, :] = total
    below = [
        inner_ref[r + k * tall : r + (k + 1) * tall, c : c + half]
        for r, c in blocks
        for k in range(beside)
    ]
    spare = size - half * len(below)
    if spare:
        below.append(jnp.zeros((tall, spare), f32))
    out_ref[width:, :] = jnp.concatenate(below, 1)


def left_kernel(st_ref, krt_ref, *refs):
    chunks, left_ref = refs[:-1], refs[-1]
    pieces = len(chunks)
    width, size = st_ref.shape[0], chunks[0].shape[1]
    beside, _ = packing(width, size)
    half = core_blocks(width)[1]
    packed = chunks[0][width:, :]
    for ref in chunks[1:]:
        packed = packed + ref[width:, :]
    near, cross, far = (
        jnp.concatenate(
            [packed[:, (b * beside + k) * half : (b * beside + k + 1) * half] for k in range(beside)],
            0,
        )
        for b in range(3)
    )
    inner = jnp.concatenate(
        [jnp.concatenate([near, cross], 1), jnp.concatenate([cross.T, far], 1)], 0
    )
    st = st_ref[...]
    scaled = [dot(st, ref[:width, :]) for ref in chunks]
    cm = dot(dot(st, inner), st.T)
    col = lax.axis_index("col")
    for at in range(pieces):
        start = pl.multiple_of(lax.rem(col + pieces - at, pieces) * size, size)
        value = scaled[at] - dot(cm, krt_ref[:, pl.ds(start, size)])
        left_ref[pl.ds(start, size), :] = jnp.concatenate(split(value.T), 1)


def far_kernel(count, left_ref, right_ref, near_left_ref, near_right_ref, *refs):
    *kept, out_ref, buffer, sems = refs
    rows, span = kept[0].shape
    slots, deep, _ = buffer.shape
    turns = len(kept)
    down = rows // deep

    def store(i, slot):
        turn, pair = lax.rem(i, turns), lax.div(i, turns)
        r = pl.multiple_of(pair * deep, deep)
        c = pl.multiple_of(turn * span, span)
        return pltpu.make_async_copy(
            buffer.at[slot], out_ref.at[pl.ds(r, deep), pl.ds(c, span)], sems.at[slot]
        )

    @pl.loop(0, down)
    def _(pair):
        r = pl.multiple_of(pair * deep, deep)
        for turn, a_ref in enumerate(kept):
            i = pair * turns + turn
            slot = lax.rem(i, slots)

            @pl.when(i >= slots)
            def _():
                store(i - slots, slot).wait()

            left = both_parts(left_ref[pl.ds(r, deep), :])
            right = four_parts(right_ref, turn * span, span)
            if turn >= count:
                left = jnp.concatenate([left, both_parts(near_left_ref[pl.ds(r, deep), :])], 1)
                right = jnp.concatenate([right, four_parts(near_right_ref, turn * span, span)], 0)
            buffer[slot] = a_ref[pl.ds(r, deep), :] - fast(left, right)
            store(i, slot).start()

    for back in range(slots, 0, -1):
        store(down * turns - back, (down * turns - back) % slots).wait()


def subtract_far(left, right, near_left, near_right, kept):
    rows, span = kept[0].shape
    parts = len(kept)
    deep = left.shape[1]
    whole = pl.BlockSpec(memory_space=pltpu.VMEM)

    def kernel(*refs):
        far_kernel(parts, *refs)

    return pl.pallas_call(
        kernel,
        in_specs=[whole] * (4 + parts),
        out_specs=pl.BlockSpec(memory_space=pltpu.HBM),
        out_shape=shape(rows, parts * span),
        scratch_shapes=[
            pltpu.VMEM((3, block_of(rows, 512), span), f32),
            pltpu.SemaphoreType.DMA((3,)),
        ],
        compiler_params=params(12),
        cost_estimate=cost(5 * rows * span * parts * deep, 8 * rows * span * parts),
        name="subtract_far",
    )(left, right, near_left, near_right, *kept)


def flip(value, bit, size, axis="row"):
    return lax.ppermute(value, axis, [(i, i ^ bit) for i in range(size)])


def from_sources(piece, col_size, source_flips, bit):
    pairs = []
    for c in range(col_size):
        for source in source_flips:
            for core in range(2):
                at = (2 * c + core) ^ source
                pairs.append((at * col_size + c, (at ^ bit) * col_size + c))
    return lax.ppermute(piece, ("row", "col"), pairs)


def shift(piece, by, size):
    return lax.ppermute(piece, "col", [(i, (i + by) % size) for i in range(size)])


def body_of(row_size, col_size):
    assert row_size == 2 * col_size

    def body(matrix, panel):
        rows, width = panel.shape
        columns = matrix.shape[1]
        small = shape(width, width)
        packed = shape(width, 2 * width)
        half = shape(width, rows // 2)
        first, second, partial = small_call(
            open_kernel, (half, half, packed), panel.T, flops=100_000_000, mib=12
        )
        apart = flip(partial, 1, row_size)
        if row_size == 8:
            wide_half = shape(width, rows // 2 + 2 * width)
            send_x, send_y, partial = small_call(
                add_cores_kernel, (wide_half, wide_half, packed), first, second, partial, apart
            )
            by_x = flip(send_x, 2, row_size)
            by_y = flip(send_y, 4, row_size)
            terms = [partial, by_x, by_y, flip(partial, 6, row_size)]
        else:
            partial = small_call(add_kernel, packed, partial, apart)
            bit = 2
            total = partial
            while bit < row_size // 2:
                total = total + flip(total, bit, row_size)
                bit *= 2
            zero = jnp.zeros_like(total)
            terms = [total, flip(total, row_size // 2, row_size), zero, zero]
        first, second, partial = lax.optimization_barrier((first, second, partial))
        low, high, resident = product_down(first, second, matrix)
        if row_size == 8:
            one, two, resident = small_call(
                merge_first_kernel, (half, half), first, second, by_x, by_y, carry=resident
            )
            more_x = flip(two, 2, row_size)
            more_y = flip(one, 4, row_size)
        else:
            relation = (lax.axis_index("row") // 2) ^ lax.axis_index("col")
            held = jnp.where(relation == 0, jnp.concatenate([first, second], 1), 0.0)
            reached = [0]
            bit = 2
            while bit < row_size:
                held = held + from_sources(held, col_size, reached, bit)
                reached = reached + [r ^ bit for r in reached]
                bit *= 2
        band, again, band_inverse, head, resident = small_call(
            eliminate_kernel, (small, small, small, small), *terms, flops=50_000_000, carry=resident
        )
        keep, give, resident = fix_down(low, high, again, resident)
        if row_size == 8:
            held, resident = small_call(
                join_kernel, shape(width, rows), one, more_y, two, more_x, carry=resident
            )
        other = flip(held, 1, row_size)
        quarter = shape(width, columns // 4)
        a, b, resident = small_call(
            halve_kernel, (quarter, quarter), keep, flip(give, 1, row_size), carry=resident
        )
        bits = []
        bit = 2
        while bit < row_size:
            bits.append(bit)
            bit *= 2
        pieces = 1 if (rows // col_size) % 128 else col_size
        late = pieces // 2
        for forward, backward in list(zip(bits, bits[::-1]))[:-1]:
            ra = flip(a, forward, row_size)
            rb = flip(b, backward, row_size)
            if bits[0] == forward:
                kct, right, *chunks, resident = across_call(
                    across_kernel,
                    (held, other, again),
                    (shape(width, columns), shape(columns, 2 * width, dtype=bf16)),
                    resident,
                    pieces,
                    late,
                    pieces - late,
                    width,
                )
            a, b, resident = small_call(
                pair_kernel, (quarter, quarter), a, ra, b, rb, carry=resident
            )
        ra = flip(a, bits[-1], row_size)
        rb = flip(b, bits[0], row_size)
        received = []
        if late:
            received = [shift(chunks[at], late + at, col_size) for at in range(pieces - late)]
            chunks = []
            for at in range(late - 1, -1, -1):
                piece, resident = across_call(
                    more_kernel, (right,), (), resident, pieces, at, 1, width
                )
                chunks = [piece] + chunks
                if at:
                    received += [shift(piece, at, col_size)]
        summed, resident = small_call(
            join_kernel, shape(width, columns // 2), a, ra, b, rb, carry=resident
        )
        exchanged = flip(summed, 1, row_size)
        own, resident = small_call(inner_own_kernel, small, kct, summed, carry=resident)
        xct, inner, resident = small_call(
            inner_kernel,
            (shape(width, columns), small),
            kct,
            summed,
            exchanged,
            own,
            carry=resident,
        )
        tall = packing(width, rows // pieces)[1]
        mine, resident = small_call(
            line_kernel,
            shape(width + tall, rows // pieces),
            chunks[0],
            *received,
            inner,
            carry=resident,
        )
        if pieces == 1:
            whole = [lax.psum(mine, "col")]
        else:
            whole = [mine] + [shift(mine, by, col_size) for by in range(1, col_size)]
        st, resident = small_call(
            invert_kernel, small, head, again, band_inverse, flops=50_000_000, carry=resident
        )
        xparts, kparts, krt, near_left, resident = small_call(
            wide_kernel,
            (
                shape(2 * width, columns, dtype=bf16),
                shape(2 * width, columns, dtype=bf16),
                shape(width, rows),
                shape(rows, 2 * width, dtype=bf16),
            ),
            st,
            xct,
            kct,
            first,
            second,
            again,
            mib=12,
            carry=resident,
        )
        resident = subtract_near(near_left, xparts, resident)
        left, resident = small_call(
            left_kernel, shape(rows, 2 * width, dtype=bf16), st, krt, *whole, mib=12, carry=resident
        )
        return subtract_far(left, kparts, near_left, xparts, resident), band

    return body


def solution(mesh):
    body = body_of(mesh.shape["row"], mesh.shape["col"])

    return jax.shard_map(
        body,
        mesh=mesh,
        in_specs=(P("row", "col"), P("row", None)),
        out_specs=(P("row", "col"), P()),
        check_vma=False,
    )
```

```python
import jax
import jax.numpy as jnp
from jax import lax
from jax.experimental import pallas as pl
from jax.experimental.pallas import tpu as pltpu
from jax.sharding import PartitionSpec as P


precise = lax.Precision.HIGHEST
f32 = jnp.float32
bf16 = jnp.bfloat16


def shape(*dims, dtype=f32):
    return jax.ShapeDtypeStruct(dims, dtype)


def params(mib):
    return pltpu.CompilerParams(vmem_limit_bytes=mib * 1024 * 1024)


def cost(flops, moved):
    return pl.CostEstimate(flops=flops, bytes_accessed=moved, transcendentals=0)


def dot(a, b):
    return jnp.dot(a, b, precision=precise, preferred_element_type=f32)


def fast(a, b):
    return jnp.dot(a, b, preferred_element_type=f32)


def split(value):
    high = value.astype(bf16)
    return high, (value - high.astype(f32)).astype(bf16)


def block_of(size, wanted):
    while size % wanted:
        wanted //= 2
    return wanted


def parts_of(columns):
    return 2 if columns % 512 else 4


def small_call(kernel, out, *operands, carry=(), flops=1_000_000, moved=1_000_000, mib=8):
    extra = {}
    body = kernel
    if carry:
        outs = out if isinstance(out, tuple) else (out,)
        count, more = len(operands), len(carry)
        anywhere = pl.BlockSpec(memory_space=pl.ANY)
        whole = pl.BlockSpec(memory_space=pltpu.VMEM)
        extra = dict(
            in_specs=[whole] * count + [anywhere] * more,
            out_specs=(whole,) * len(outs) + (anywhere,) * more,
            input_output_aliases={count + k: len(outs) + k for k in range(more)},
        )
        operands = operands + tuple(carry)
        out = outs + tuple(shape(*x.shape) for x in carry)

        def body(*refs):
            kernel(*refs[:count], *refs[count + more : -more])

    result = pl.pallas_call(
        body, out_shape=out, compiler_params=params(mib), cost_estimate=cost(flops, moved), **extra
    )(*operands)
    if carry:
        return tuple(result[: -len(carry)]) + (tuple(result[-len(carry) :]),)
    return result


def open_kernel(
    panel_ref, a_ref, first_ref, second_ref, packed_ref, part_ref, turned_ref, sems
):
    width = turned_ref.shape[0]
    half = first_ref.shape[1]
    span = part_ref.shape[1]
    panel_copy = pltpu.make_async_copy(panel_ref, turned_ref, sems.at[0])
    part_copy = pltpu.make_async_copy(a_ref.at[:, pl.ds(0, span)], part_ref, sems.at[1])
    panel_copy.start()
    part_copy.start()
    panel_copy.wait()
    turned = turned_ref[...]
    first_ref[...] = turned[:, :half]
    second_ref[...] = turned[:, half:]
    gram = lax.dot_general(
        turned, turned, (((1,), (1,)), ((), ())), precision=precise, preferred_element_type=f32
    )
    head = jnp.where(lax.axis_index("row") == 0, turned[:, : 2 * width].T[:width], 0.0)
    packed_ref[...] = jnp.concatenate([gram, head], 1)
    part_copy.wait()


def open_panel(turned, a):
    width, rows = turned.shape
    whole = pl.BlockSpec(memory_space=pltpu.VMEM)
    remote = pl.BlockSpec(memory_space=pltpu.HBM)
    span = a.shape[1] // parts_of(a.shape[1])
    half = shape(width, rows // 2)
    return pl.pallas_call(
        open_kernel,
        in_specs=[remote, remote],
        out_specs=(whole,) * 4,
        out_shape=(half, half, shape(width, 2 * width), shape(rows, span)),
        scratch_shapes=[pltpu.VMEM((width, rows), f32), pltpu.SemaphoreType.DMA((2,))],
        compiler_params=params(12),
        cost_estimate=cost(100_000_000, 4 * rows * span),
        name="open",
    )(
        pltpu.with_memory_space_constraint(turned, pltpu.HBM),
        pltpu.with_memory_space_constraint(a, pltpu.HBM),
    )


def add_cores_kernel(first_ref, second_ref, a_ref, b_ref, x_ref, y_ref, sum_ref):
    half = first_ref.shape[1]
    total = a_ref[...] + b_ref[...]
    sum_ref[...] = total
    for source, target in ((first_ref, x_ref), (second_ref, y_ref)):
        target[:, :half] = source[...]
        target[:, half:] = total


def add_kernel(*refs):
    total = refs[0][...]
    for ref in refs[1:-1]:
        total = total + ref[...]
    refs[-1][...] = total


def spread(tile, at):
    return jnp.broadcast_to(tile[at : at + 1, :], tile.shape)


def pick(tile, at):
    return jnp.broadcast_to(tile[:, at : at + 1], tile.shape)


def sweep(tiles, order, full):
    lane = lax.broadcasted_iota(jnp.int32, (8, order), 1)
    sub = lax.broadcasted_iota(jnp.int32, (8, order), 0)
    tiles = list(tiles)
    for at in range(order // 8):
        base = 8 * at
        inside = (lane >= base) & (lane < base + 8)
        tile = tiles[at]
        others = [t for t in range(order // 8) if (t != at if full else t > at)]
        picked = {t: [pick(tiles[t], base + q) for q in range(8)] for t in others}
        columns = [pick(tile, base + q) for q in range(8)]
        rows = jnp.where(inside, jnp.where(lane - base == sub, 1.0, 0.0), tile)
        lower, upper = rows, tile
        for q in range(8):
            here = sub == q
            inverse = 1.0 / spread(columns[q], q)
            scaled = spread(rows, q) * inverse
            if not full:
                lower = jnp.where(here, rows, lower)
                upper = jnp.where(
                    sub > q, upper - columns[q] * (spread(upper, q) * inverse), upper
                )
            rows = jnp.where(here, scaled, rows - columns[q] * scaled)
            for p in range(q + 1, 8):
                part = spread(columns[p], q) * inverse
                columns[p] = jnp.where(here, part, columns[p] - columns[q] * part)
        finals = [spread(rows, q) for q in range(8)]
        for t in others:
            value = jnp.where(inside, 0.0, tiles[t])
            for q in range(8):
                value = value - picked[t][q] * finals[q]
            tiles[t] = value
        tiles[at] = rows if full else jnp.where(inside & (lane - base >= sub), upper, lower)
    return tiles


def eliminate_kernel(a_ref, b_ref, c_ref, d_ref, band_ref, again_ref, inverse_ref, head_ref):
    order = band_ref.shape[0]
    lane = lax.broadcasted_iota(jnp.int32, (8, order), 1)
    sub = lax.broadcasted_iota(jnp.int32, (8, order), 0)
    skip = b_ref.shape[1] - a_ref.shape[1]
    total = (a_ref[...] + b_ref[:, skip:]) + (c_ref[:, skip:] + d_ref[...])
    head_ref[...] = total[:, order:]
    gram = total[:, :order]
    tiles = sweep([gram[8 * t : 8 * t + 8, :] for t in range(order // 8)], order, False)
    for t in range(order // 8):
        row_at = sub + 8 * t
        diagonal = jnp.sum(jnp.where(lane == row_at, tiles[t], 0.0), axis=1, keepdims=True)
        length = jnp.sqrt(diagonal)
        scaled = tiles[t] / length
        band = jnp.where(lane > row_at, -scaled, jnp.where(lane == row_at, -length, 0.0))
        band_ref[8 * t : 8 * t + 8, :] = band
        again_ref[8 * t : 8 * t + 8, :] = band
        inverse_ref[8 * t : 8 * t + 8, :] = jnp.where(
            lane < row_at, -scaled, jnp.where(lane == row_at, -1.0 / length, 0.0)
        )


def invert_kernel(head_ref, band_ref, inverse_ref, out_ref):
    order = head_ref.shape[0]
    tiles = [
        head_ref[8 * t : 8 * t + 8, :] - band_ref[8 * t : 8 * t + 8, :] for t in range(order // 8)
    ]
    tiles = sweep(tiles, order, True)
    out_ref[...] = -dot(jnp.concatenate(tiles, 0), inverse_ref[...])


def down_kernel(begin, first_ref, second_ref, a_ref, given, out_ref, kept, sems):
    width = out_ref.shape[0]
    refs = list(given) + list(kept)
    span = refs[0].shape[1]
    size = block_of(span, 256)
    count = span // size

    def load(at, i):
        start = pl.multiple_of(i * size, size)
        place = (begin + len(given) + at) * span
        source = a_ref.at[:, pl.ds(pl.multiple_of(place + start, size), size)]
        target = kept[at].at[:, pl.ds(start, size)]
        return pltpu.make_async_copy(source, target, sems.at[at * count + i])

    for at in range(len(kept)):
        for i in range(count):
            load(at, i).start()
    kh, kl = split(jnp.concatenate([first_ref[...], second_ref[...]], 1))
    left = jnp.concatenate([kh, kl], 0)
    for at, ref in enumerate(refs):

        @pl.loop(0, count)
        def _(i):
            if at >= len(given):
                load(at - len(given), i).wait()
            start = pl.multiple_of(i * size, size)
            ah, al = split(ref[:, pl.ds(start, size)])
            term = fast(left, ah) + fast(left, al)
            into = pl.ds(pl.multiple_of(at * span + start, size), size)
            out_ref[:, into] = term[:width] + term[width:]


def product_down(first, second, a, given, begin, end, carry=()):
    rows, columns = a.shape
    width = first.shape[0]
    span = columns // parts_of(columns)
    ready, fresh, more = len(given), end - begin - len(given), len(carry)
    whole = pl.BlockSpec(memory_space=pltpu.VMEM)
    anywhere = pl.BlockSpec(memory_space=pl.ANY)
    copies = max(1, fresh * (span // block_of(span, 256)))

    def kernel(first_ref, second_ref, a_ref, *refs):
        outs = refs[ready + more : -1]
        down_kernel(
            begin,
            first_ref,
            second_ref,
            a_ref,
            refs[:ready],
            outs[0],
            outs[1 : 1 + fresh],
            refs[-1],
        )

    out, *kept = pl.pallas_call(
        kernel,
        in_specs=[whole, whole, pl.BlockSpec(memory_space=pltpu.HBM)]
        + [whole] * ready
        + [anywhere] * more,
        out_specs=(whole,) * (1 + fresh) + (anywhere,) * more,
        out_shape=(shape(width, span * (end - begin)),)
        + (shape(rows, span),) * fresh
        + tuple(shape(*x.shape) for x in carry),
        input_output_aliases={3 + ready + k: 1 + fresh + k for k in range(more)},
        scratch_shapes=[pltpu.SemaphoreType.DMA((copies,))],
        compiler_params=params(12),
        cost_estimate=cost(
            8 * rows * span * (end - begin) * width, 4 * rows * span * (end - begin)
        ),
    )(first, second, pltpu.with_memory_space_constraint(a, pltpu.HBM), *given, *carry)
    return out, tuple(kept[fresh:]) + tuple(given) + tuple(kept[:fresh])


def fix_kernel(parts, low_ref, high_ref, band_ref, *refs):
    tops, keep_ref, give_ref = refs[:parts], refs[parts], refs[parts + 1]
    row = lax.axis_index("row")
    core = lax.rem(row, 2)
    first, second = low_ref[...], high_ref[...]
    span = tops[0].shape[1]

    @pl.when(row == 0)
    def _():
        rh, rl = split(band_ref[...].T)
        left = jnp.concatenate([rh, rl, rh, rl], 1)
        for at, top in enumerate(tops):
            half, place = divmod(at, parts // 2)
            ah, al = split(top[...])
            value = (first, second)[half][:, place * span : (place + 1) * span]
            (keep_ref, give_ref)[half][:, place * span : (place + 1) * span] = value - fast(
                left, jnp.concatenate([ah, ah, al, al], 0)
            )

    @pl.when((row != 0) & (core == 0))
    def _():
        keep_ref[...] = first
        give_ref[...] = second

    @pl.when(core == 1)
    def _():
        keep_ref[...] = second
        give_ref[...] = first


def fix_down(low, high, band, kept):
    width, half = low.shape
    parts = len(kept)
    side = pl.BlockSpec((width, half), lambda i: (0, 0))
    top = pl.BlockSpec((width, kept[0].shape[1]), lambda i: (0, 0))
    anywhere = pl.BlockSpec(memory_space=pl.ANY)

    def kernel(*refs):
        fix_kernel(parts, *refs)

    keep, give, *kept = pl.pallas_call(
        kernel,
        grid=(1,),
        in_specs=[side, side, pl.BlockSpec((width, width), lambda i: (0, 0))] + [top] * parts,
        out_specs=(side, side) + (anywhere,) * parts,
        out_shape=(shape(width, half),) * 2 + tuple(shape(*x.shape) for x in kept),
        input_output_aliases={3 + k: 2 + k for k in range(parts)},
        compiler_params=params(12),
        cost_estimate=cost(24 * width * width * half, 32 * width * half),
        name="fix_down",
    )(low, high, band, *kept)
    return keep, give, tuple(kept)


def rows_product(right_ref, halves, outs):
    span = halves[0].shape[1]
    width = right_ref.shape[1] // 2
    chunk = block_of(span, 512)
    total = None
    for at, a_ref in enumerate(halves):
        for c in range(0, span, chunk):
            ah, al = split(a_ref[:, c : c + chunk])
            right = right_ref[at * span + c : at * span + c + chunk, :]
            term = fast(ah, right) + fast(al, right)
            total = term if total is None else total + term
    result = (total[:, :width] + total[:, width:]).T
    for at, out_ref in enumerate(outs):

        @pl.when(pl.program_id(0) == at)
        def _():
            out_ref[...] = result


def across_kernel(parts, held_ref, other_ref, band_ref, *refs):
    kct_ref, right_ref = refs[parts : parts + 2]
    width, half = held_ref.shape
    columns = 2 * half
    chunk = block_of(columns, 512)

    @pl.when(pl.program_id(0) == 0)
    def _():
        core = lax.rem(lax.axis_index("row"), 2)

        @pl.when(core == 0)
        def _():
            kct_ref[:, :half] = held_ref[...]
            kct_ref[:, half:] = other_ref[...]

        @pl.when(core == 1)
        def _():
            kct_ref[:, :half] = other_ref[...]
            kct_ref[:, half:] = held_ref[...]

        @pl.when(lax.axis_index("col") == 0)
        def _():
            kct_ref[:, :width] = kct_ref[:, :width] - band_ref[...].T

        for c in range(0, columns, chunk):
            right_ref[c : c + chunk, :] = jnp.concatenate(split(kct_ref[:, c : c + chunk].T), 1)

    rows_product(right_ref, refs[:parts], refs[parts + 2 : -parts])


def more_kernel(parts, right_ref, *refs):
    rows_product(right_ref, refs[:parts], refs[parts:-parts])


def across_call(kernel, operands, extra, kept, pieces, start, count, width):
    rows, span = kept[0].shape
    parts = len(kept)
    size = rows // pieces

    def turn(i):
        return (lax.rem(i + start + lax.axis_index("col"), pieces), 0)

    def fixed(array):
        return pl.BlockSpec(array.shape, lambda i: (0, 0))

    def body(*refs):
        kernel(parts, *refs)

    outs = tuple(extra) + (shape(width, size),) * count
    at, to = len(operands), len(outs)
    results = pl.pallas_call(
        body,
        grid=(count,),
        in_specs=[fixed(x) for x in operands] + [pl.BlockSpec((size, span), turn)] * parts,
        out_specs=tuple(fixed(x) for x in outs) + (pl.BlockSpec(memory_space=pl.ANY),) * parts,
        out_shape=outs + (shape(rows, span),) * parts,
        input_output_aliases={at + k: to + k for k in range(parts)},
        compiler_params=params(22),
        cost_estimate=cost(8 * size * count * span * parts * width, 4 * size * count * span * parts),
    )(*operands, *kept)
    return (*results[:to], tuple(results[to:]))


def merge_first_kernel(first_ref, second_ref, by_x_ref, by_y_ref, a_ref, b_ref):
    half = a_ref.shape[1]
    relation = lax.div(lax.axis_index("row"), 2) ^ lax.axis_index("col")
    for at, own, got, out in (
        (1, first_ref, by_x_ref, a_ref),
        (2, second_ref, by_y_ref, b_ref),
    ):
        out[...] = jnp.where(
            relation == 0, own[...], jnp.where(relation == at, got[:, :half], 0.0)
        )


def join_kernel(a_ref, b_ref, c_ref, d_ref, out_ref):
    half = a_ref.shape[1]
    out_ref[:, :half] = a_ref[...] + b_ref[...]
    out_ref[:, half:] = c_ref[...] + d_ref[...]


def halve_kernel(keep_ref, other_ref, a_ref, b_ref):
    half = a_ref.shape[1]
    a_ref[...] = keep_ref[:, :half] + other_ref[:, :half]
    b_ref[...] = keep_ref[:, half:] + other_ref[:, half:]


def pair_kernel(a_ref, b_ref, c_ref, d_ref, e_ref, f_ref):
    e_ref[...] = a_ref[...] + b_ref[...]
    f_ref[...] = c_ref[...] + d_ref[...]


def half_product(kct_ref, x_ref, core):
    half = x_ref.shape[1]
    start = pl.multiple_of(core * half, half)
    return lax.dot_general(
        kct_ref[:, pl.ds(start, half)],
        x_ref[...],
        (((1,), (1,)), ((), ())),
        precision=precise,
        preferred_element_type=f32,
    )


def inner_own_kernel(kct_ref, held_ref, inner_ref):
    inner_ref[...] = half_product(kct_ref, held_ref, lax.rem(lax.axis_index("row"), 2))


def inner_kernel(kct_ref, held_ref, other_ref, own_ref, xct_ref, inner_ref):
    half = held_ref.shape[1]
    core = lax.rem(lax.axis_index("row"), 2)

    @pl.when(core == 0)
    def _():
        xct_ref[:, :half] = held_ref[...]
        xct_ref[:, half:] = other_ref[...]

    @pl.when(core == 1)
    def _():
        xct_ref[:, :half] = other_ref[...]
        xct_ref[:, half:] = held_ref[...]

    inner_ref[...] = own_ref[...] + half_product(kct_ref, other_ref, 1 - core)


def wide_kernel(
    st_ref, xct_ref, kct_ref, first_ref, second_ref, band_ref, x_ref, k_ref, rows_ref, left_ref
):
    width, columns = kct_ref.shape
    st = st_ref[...]
    chunk = block_of(columns, 512)
    for c in range(0, columns, chunk):
        for ref, value in (
            (x_ref, dot(st, xct_ref[:, c : c + chunk])),
            (k_ref, kct_ref[:, c : c + chunk]),
        ):
            ref[:, c : c + chunk] = jnp.concatenate(split(value), 0)
    half = first_ref.shape[1]
    rows_ref[:, :half] = first_ref[...]
    rows_ref[:, half:] = second_ref[...]

    @pl.when(lax.axis_index("row") == 0)
    def _():
        rows_ref[:, :width] = rows_ref[:, :width] - band_ref[...].T

    rows = rows_ref.shape[1]
    deep = block_of(rows, 512)
    for r in range(0, rows, deep):
        left_ref[r : r + deep, :] = jnp.concatenate(split(rows_ref[:, r : r + deep].T), 1)


def both_parts(left):
    return jnp.concatenate([left, left], 1)


def four_parts(right_ref, start, size):
    width = right_ref.shape[0] // 2
    high = right_ref[:width, pl.ds(start, size)]
    low = right_ref[width:, pl.ds(start, size)]
    return jnp.concatenate([high, high, low, low], 0)


def near_kernel(count, left_ref, right_ref, *refs):
    total = (len(refs)) // 2
    rows, span = refs[0].shape
    deep = block_of(rows, 512)
    chunk = block_of(span, 512)
    if span % 256 == 0 and span <= 1024:
        chunk = span
    for at in range(count):
        a_ref, out_ref = refs[at], refs[total + at]

        @pl.loop(0, span // chunk)
        def _(i):
            c = pl.multiple_of(i * chunk, chunk)
            right = four_parts(right_ref, pl.multiple_of(at * span + c, 128), chunk)
            for r in range(0, rows, deep):
                out_ref[r : r + deep, pl.ds(c, chunk)] = a_ref[
                    r : r + deep, pl.ds(c, chunk)
                ] - fast(both_parts(left_ref[r : r + deep, :]), right)


def subtract_near(left, right, kept):
    rows, span = kept[0].shape
    parts = len(kept)
    count = parts
    deep = left.shape[1]
    whole = pl.BlockSpec(memory_space=pltpu.VMEM)
    places = [whole] * count + [pl.BlockSpec(memory_space=pl.ANY)] * (parts - count)

    def kernel(*refs):
        near_kernel(count, *refs)

    return tuple(
        pl.pallas_call(
            kernel,
            in_specs=[whole] * 2 + places,
            out_specs=tuple(places),
            out_shape=(shape(rows, span),) * parts,
            input_output_aliases={2 + k: k for k in range(parts)},
            compiler_params=params(12),
            cost_estimate=cost(4 * rows * span * count * deep, 8 * rows * span * count),
            name="subtract_near",
        )(left, right, *kept)
    )


def core_blocks(width):
    half = width // 2
    return [(0, 0), (0, half), (half, half)], half


def packing(width, size):
    half = width // 2
    beside = 1
    while 6 * beside * half <= size and 2 * beside <= half // 8:
        beside *= 2
    return beside, half // beside


def line_kernel(*refs):
    *chunks, inner_ref, out_ref = refs
    width, size = chunks[0].shape
    beside, tall = packing(width, size)
    blocks, half = core_blocks(width)
    total = chunks[0][...]
    for ref in chunks[1:]:
        total = total + ref[...]
    out_ref[:width, :] = total
    below = [
        inner_ref[r + k * tall : r + (k + 1) * tall, c : c + half]
        for r, c in blocks
        for k in range(beside)
    ]
    spare = size - half * len(below)
    if spare:
        below.append(jnp.zeros((tall, spare), f32))
    out_ref[width:, :] = jnp.concatenate(below, 1)


def left_kernel(st_ref, krt_ref, *refs):
    chunks, left_ref = refs[:-1], refs[-1]
    pieces = len(chunks)
    width, size = st_ref.shape[0], chunks[0].shape[1]
    beside, _ = packing(width, size)
    half = core_blocks(width)[1]
    packed = chunks[0][width:, :]
    for ref in chunks[1:]:
        packed = packed + ref[width:, :]
    near, cross, far = (
        jnp.concatenate(
            [packed[:, (b * beside + k) * half : (b * beside + k + 1) * half] for k in range(beside)],
            0,
        )
        for b in range(3)
    )
    inner = jnp.concatenate(
        [jnp.concatenate([near, cross], 1), jnp.concatenate([cross.T, far], 1)], 0
    )
    st = st_ref[...]
    scaled = [dot(st, ref[:width, :]) for ref in chunks]
    cm = dot(dot(st, inner), st.T)
    col = lax.axis_index("col")
    for at in range(pieces):
        start = pl.multiple_of(lax.rem(col + pieces - at, pieces) * size, size)
        value = scaled[at] - dot(cm, krt_ref[:, pl.ds(start, size)])
        left_ref[pl.ds(start, size), :] = jnp.concatenate(split(value.T), 1)


def far_kernel(count, left_ref, right_ref, near_left_ref, near_right_ref, *refs):
    *kept, out_ref, buffer, sems = refs
    rows, span = kept[0].shape
    slots, deep, _ = buffer.shape
    turns = len(kept)
    down = rows // deep

    def store(i, slot):
        turn, pair = lax.rem(i, turns), lax.div(i, turns)
        r = pl.multiple_of(pair * deep, deep)
        c = pl.multiple_of(turn * span, span)
        return pltpu.make_async_copy(
            buffer.at[slot], out_ref.at[pl.ds(r, deep), pl.ds(c, span)], sems.at[slot]
        )

    @pl.loop(0, down)
    def _(pair):
        r = pl.multiple_of(pair * deep, deep)
        for turn, a_ref in enumerate(kept):
            i = pair * turns + turn
            slot = lax.rem(i, slots)

            @pl.when(i >= slots)
            def _():
                store(i - slots, slot).wait()

            left = both_parts(left_ref[pl.ds(r, deep), :])
            right = four_parts(right_ref, turn * span, span)
            if turn >= count:
                left = jnp.concatenate([left, both_parts(near_left_ref[pl.ds(r, deep), :])], 1)
                right = jnp.concatenate([right, four_parts(near_right_ref, turn * span, span)], 0)
            buffer[slot] = a_ref[pl.ds(r, deep), :] - fast(left, right)
            store(i, slot).start()

    for back in range(slots, 0, -1):
        store(down * turns - back, (down * turns - back) % slots).wait()


def subtract_far(left, right, near_left, near_right, kept):
    rows, span = kept[0].shape
    parts = len(kept)
    deep = left.shape[1]
    whole = pl.BlockSpec(memory_space=pltpu.VMEM)

    def kernel(*refs):
        far_kernel(parts, *refs)

    return pl.pallas_call(
        kernel,
        in_specs=[whole] * (4 + parts),
        out_specs=pl.BlockSpec(memory_space=pltpu.HBM),
        out_shape=shape(rows, parts * span),
        scratch_shapes=[
            pltpu.VMEM((3, block_of(rows, 512), span), f32),
            pltpu.SemaphoreType.DMA((3,)),
        ],
        compiler_params=params(12),
        cost_estimate=cost(5 * rows * span * parts * deep, 8 * rows * span * parts),
        name="subtract_far",
    )(left, right, near_left, near_right, *kept)


def flip(value, bit, size, axis="row"):
    return lax.ppermute(value, axis, [(i, i ^ bit) for i in range(size)])


def from_sources(piece, col_size, source_flips, bit):
    pairs = []
    for c in range(col_size):
        for source in source_flips:
            for core in range(2):
                at = (2 * c + core) ^ source
                pairs.append((at * col_size + c, (at ^ bit) * col_size + c))
    return lax.ppermute(piece, ("row", "col"), pairs)


def shift(piece, by, size):
    return lax.ppermute(piece, "col", [(i, (i + by) % size) for i in range(size)])


def body_of(row_size, col_size):
    assert row_size == 2 * col_size

    def body(matrix, panel):
        rows, width = panel.shape
        columns = matrix.shape[1]
        small = shape(width, width)
        packed = shape(width, 2 * width)
        half = shape(width, rows // 2)
        first, second, partial, part = open_panel(panel.T, matrix)
        parts = parts_of(columns)
        apart = flip(partial, 1, row_size)
        if row_size == 8:
            wide_half = shape(width, rows // 2 + 2 * width)
            send_x, send_y, partial = small_call(
                add_cores_kernel, (wide_half, wide_half, packed), first, second, partial, apart
            )
            by_x = flip(send_x, 2, row_size)
            by_y = flip(send_y, 4, row_size)
            terms = [partial, by_x, by_y, flip(partial, 6, row_size)]
        else:
            partial = small_call(add_kernel, packed, partial, apart)
            bit = 2
            total = partial
            while bit < row_size // 2:
                total = total + flip(total, bit, row_size)
                bit *= 2
            zero = jnp.zeros_like(total)
            terms = [total, flip(total, row_size // 2, row_size), zero, zero]
        first, second, partial = lax.optimization_barrier((first, second, partial))
        low, resident = product_down(first, second, matrix, (part,), 0, parts // 2)
        if row_size == 8:
            one, two, resident = small_call(
                merge_first_kernel, (half, half), first, second, by_x, by_y, carry=resident
            )
            more_x = flip(two, 2, row_size)
            more_y = flip(one, 4, row_size)
        else:
            relation = (lax.axis_index("row") // 2) ^ lax.axis_index("col")
            held = jnp.where(relation == 0, jnp.concatenate([first, second], 1), 0.0)
            reached = [0]
            bit = 2
            while bit < row_size:
                held = held + from_sources(held, col_size, reached, bit)
                reached = reached + [r ^ bit for r in reached]
                bit *= 2
        high, resident = product_down(first, second, matrix, (), parts // 2, parts, resident)
        band, again, band_inverse, head, resident = small_call(
            eliminate_kernel, (small, small, small, small), *terms, flops=50_000_000, carry=resident
        )
        keep, give, resident = fix_down(low, high, again, resident)
        if row_size == 8:
            held, resident = small_call(
                join_kernel, shape(width, rows), one, more_y, two, more_x, carry=resident
            )
        other = flip(held, 1, row_size)
        quarter = shape(width, columns // 4)
        a, b, resident = small_call(
            halve_kernel, (quarter, quarter), keep, flip(give, 1, row_size), carry=resident
        )
        bits = []
        bit = 2
        while bit < row_size:
            bits.append(bit)
            bit *= 2
        pieces = 1 if (rows // col_size) % 128 else col_size
        late = pieces // 2
        for forward, backward in list(zip(bits, bits[::-1]))[:-1]:
            ra = flip(a, forward, row_size)
            rb = flip(b, backward, row_size)
            if bits[0] == forward:
                kct, right, *chunks, resident = across_call(
                    across_kernel,
                    (held, other, again),
                    (shape(width, columns), shape(columns, 2 * width, dtype=bf16)),
                    resident,
                    pieces,
                    late,
                    pieces - late,
                    width,
                )
            a, b, resident = small_call(
                pair_kernel, (quarter, quarter), a, ra, b, rb, carry=resident
            )
        ra = flip(a, bits[-1], row_size)
        rb = flip(b, bits[0], row_size)
        received = []
        if late:
            received = [shift(chunks[at], late + at, col_size) for at in range(pieces - late)]
            chunks = []
            for at in range(late - 1, -1, -1):
                piece, resident = across_call(
                    more_kernel, (right,), (), resident, pieces, at, 1, width
                )
                chunks = [piece] + chunks
                if at:
                    received += [shift(piece, at, col_size)]
        summed, resident = small_call(
            join_kernel, shape(width, columns // 2), a, ra, b, rb, carry=resident
        )
        exchanged = flip(summed, 1, row_size)
        own, resident = small_call(inner_own_kernel, small, kct, summed, carry=resident)
        xct, inner, resident = small_call(
            inner_kernel,
            (shape(width, columns), small),
            kct,
            summed,
            exchanged,
            own,
            carry=resident,
        )
        tall = packing(width, rows // pieces)[1]
        mine, resident = small_call(
            line_kernel,
            shape(width + tall, rows // pieces),
            chunks[0],
            *received,
            inner,
            carry=resident,
        )
        if pieces == 1:
            whole = [lax.psum(mine, "col")]
        else:
            whole = [mine] + [shift(mine, by, col_size) for by in range(1, col_size)]
        st, resident = small_call(
            invert_kernel, small, head, again, band_inverse, flops=50_000_000, carry=resident
        )
        xparts, kparts, krt, near_left, resident = small_call(
            wide_kernel,
            (
                shape(2 * width, columns, dtype=bf16),
                shape(2 * width, columns, dtype=bf16),
                shape(width, rows),
                shape(rows, 2 * width, dtype=bf16),
            ),
            st,
            xct,
            kct,
            first,
            second,
            again,
            mib=12,
            carry=resident,
        )
        resident = subtract_near(near_left, xparts, resident)
        left, resident = small_call(
            left_kernel, shape(rows, 2 * width, dtype=bf16), st, krt, *whole, mib=12, carry=resident
        )
        return subtract_far(left, kparts, near_left, xparts, resident), band

    return body


def solution(mesh):
    body = body_of(mesh.shape["row"], mesh.shape["col"])

    return jax.shard_map(
        body,
        mesh=mesh,
        in_specs=(P("row", "col"), P("row", None)),
        out_specs=(P("row", "col"), P()),
        check_vma=False,
    )
```

```python
import jax
import jax.numpy as jnp
from jax import lax
from jax.experimental import pallas as pl
from jax.experimental.pallas import tpu as pltpu
from jax.sharding import PartitionSpec as P


precise = lax.Precision.HIGHEST
f32 = jnp.float32
bf16 = jnp.bfloat16


def shape(*dims, dtype=f32):
    return jax.ShapeDtypeStruct(dims, dtype)


def params(mib):
    return pltpu.CompilerParams(vmem_limit_bytes=mib * 1024 * 1024)


def cost(flops, moved):
    return pl.CostEstimate(flops=flops, bytes_accessed=moved, transcendentals=0)


def dot(a, b):
    return jnp.dot(a, b, precision=precise, preferred_element_type=f32)


def fast(a, b):
    return jnp.dot(a, b, preferred_element_type=f32)


def split(value):
    high = value.astype(bf16)
    return high, (value - high.astype(f32)).astype(bf16)


def block_of(size, wanted):
    while size % wanted:
        wanted //= 2
    return wanted


def small_call(kernel, out, *operands, carry=(), flops=1_000_000, moved=1_000_000, mib=8):
    extra = {}
    body = kernel
    if carry:
        outs = out if isinstance(out, tuple) else (out,)
        count, more = len(operands), len(carry)
        anywhere = pl.BlockSpec(memory_space=pl.ANY)
        whole = pl.BlockSpec(memory_space=pltpu.VMEM)
        extra = dict(
            in_specs=[whole] * count + [anywhere] * more,
            out_specs=(whole,) * len(outs) + (anywhere,) * more,
            input_output_aliases={count + k: len(outs) + k for k in range(more)},
        )
        operands = operands + tuple(carry)
        out = outs + tuple(shape(*x.shape) for x in carry)

        def body(*refs):
            kernel(*refs[:count], *refs[count + more : -more])

    result = pl.pallas_call(
        body, out_shape=out, compiler_params=params(mib), cost_estimate=cost(flops, moved), **extra
    )(*operands)
    if carry:
        return tuple(result[: -len(carry)]) + (tuple(result[-len(carry) :]),)
    return result


def open_kernel(panel_ref, first_ref, second_ref, packed_ref, turned_ref, sems):
    width, rows = turned_ref.shape
    half = first_ref.shape[1]
    count = sems.shape[0]
    size = rows // count
    copies = [
        pltpu.make_async_copy(
            panel_ref.at[:, pl.ds(k * size, size)], turned_ref.at[:, pl.ds(k * size, size)], sems.at[k]
        )
        for k in range(count)
    ]
    for copy in copies:
        copy.start()
    for copy in copies:
        copy.wait()
    turned = turned_ref[...]
    first_ref[...] = turned[:, :half]
    second_ref[...] = turned[:, half:]
    gram = lax.dot_general(
        turned, turned, (((1,), (1,)), ((), ())), precision=precise, preferred_element_type=f32
    )
    head = jnp.where(lax.axis_index("row") == 0, turned[:, : 2 * width].T[:width], 0.0)
    packed_ref[...] = jnp.concatenate([gram, head], 1)


def open_panel(turned):
    width, rows = turned.shape
    whole = pl.BlockSpec(memory_space=pltpu.VMEM)
    half = shape(width, rows // 2)
    count = 1 if (rows // 4) % 128 else 4
    return pl.pallas_call(
        open_kernel,
        in_specs=[pl.BlockSpec(memory_space=pltpu.HBM)],
        out_specs=(whole,) * 3,
        out_shape=(half, half, shape(width, 2 * width)),
        scratch_shapes=[pltpu.VMEM((width, rows), f32), pltpu.SemaphoreType.DMA((count,))],
        compiler_params=params(12),
        cost_estimate=cost(100_000_000, 8 * rows * width),
        name="open",
    )(pltpu.with_memory_space_constraint(turned, pltpu.HBM))


def add_cores_kernel(first_ref, second_ref, a_ref, b_ref, x_ref, y_ref, sum_ref):
    half = first_ref.shape[1]
    total = a_ref[...] + b_ref[...]
    sum_ref[...] = total
    for source, target in ((first_ref, x_ref), (second_ref, y_ref)):
        target[:, :half] = source[...]
        target[:, half:] = total


def add_kernel(*refs):
    total = refs[0][...]
    for ref in refs[1:-1]:
        total = total + ref[...]
    refs[-1][...] = total


def spread(tile, at):
    return jnp.broadcast_to(tile[at : at + 1, :], tile.shape)


def pick(tile, at):
    return jnp.broadcast_to(tile[:, at : at + 1], tile.shape)


def sweep(tiles, order, full):
    lane = lax.broadcasted_iota(jnp.int32, (8, order), 1)
    sub = lax.broadcasted_iota(jnp.int32, (8, order), 0)
    tiles = list(tiles)
    for at in range(order // 8):
        base = 8 * at
        inside = (lane >= base) & (lane < base + 8)
        tile = tiles[at]
        others = [t for t in range(order // 8) if (t != at if full else t > at)]
        picked = {t: [pick(tiles[t], base + q) for q in range(8)] for t in others}
        columns = [pick(tile, base + q) for q in range(8)]
        rows = jnp.where(inside, jnp.where(lane - base == sub, 1.0, 0.0), tile)
        lower, upper = rows, tile
        for q in range(8):
            here = sub == q
            inverse = 1.0 / spread(columns[q], q)
            scaled = spread(rows, q) * inverse
            if not full:
                lower = jnp.where(here, rows, lower)
                upper = jnp.where(
                    sub > q, upper - columns[q] * (spread(upper, q) * inverse), upper
                )
            rows = jnp.where(here, scaled, rows - columns[q] * scaled)
            for p in range(q + 1, 8):
                part = spread(columns[p], q) * inverse
                columns[p] = jnp.where(here, part, columns[p] - columns[q] * part)
        finals = [spread(rows, q) for q in range(8)]
        for t in others:
            value = jnp.where(inside, 0.0, tiles[t])
            for q in range(8):
                value = value - picked[t][q] * finals[q]
            tiles[t] = value
        tiles[at] = rows if full else jnp.where(inside & (lane - base >= sub), upper, lower)
    return tiles


def eliminate_kernel(a_ref, b_ref, c_ref, d_ref, band_ref, again_ref, inverse_ref, head_ref):
    order = band_ref.shape[0]
    lane = lax.broadcasted_iota(jnp.int32, (8, order), 1)
    sub = lax.broadcasted_iota(jnp.int32, (8, order), 0)
    skip = b_ref.shape[1] - a_ref.shape[1]
    total = (a_ref[...] + b_ref[:, skip:]) + (c_ref[:, skip:] + d_ref[...])
    head_ref[...] = total[:, order:]
    gram = total[:, :order]
    tiles = sweep([gram[8 * t : 8 * t + 8, :] for t in range(order // 8)], order, False)
    for t in range(order // 8):
        row_at = sub + 8 * t
        diagonal = jnp.sum(jnp.where(lane == row_at, tiles[t], 0.0), axis=1, keepdims=True)
        length = jnp.sqrt(diagonal)
        scaled = tiles[t] / length
        band = jnp.where(lane > row_at, -scaled, jnp.where(lane == row_at, -length, 0.0))
        band_ref[8 * t : 8 * t + 8, :] = band
        again_ref[8 * t : 8 * t + 8, :] = band
        inverse_ref[8 * t : 8 * t + 8, :] = jnp.where(
            lane < row_at, -scaled, jnp.where(lane == row_at, -1.0 / length, 0.0)
        )


def invert_kernel(head_ref, band_ref, inverse_ref, out_ref):
    order = head_ref.shape[0]
    tiles = [
        head_ref[8 * t : 8 * t + 8, :] - band_ref[8 * t : 8 * t + 8, :] for t in range(order // 8)
    ]
    tiles = sweep(tiles, order, True)
    out_ref[...] = -dot(jnp.concatenate(tiles, 0), inverse_ref[...])


def parts_of(columns):
    return 2 if columns % 512 else 4


def down_kernel(first_ref, second_ref, a_ref, low_ref, high_ref, *refs):
    kept, sems = refs[:-1], refs[-1]
    width = low_ref.shape[0]
    span = kept[0].shape[1]
    count = sems.shape[0] // len(kept)
    size = span // count

    def load(at, i):
        start = pl.multiple_of(i * size, size)
        source = a_ref.at[:, pl.ds(pl.multiple_of(at * span + start, size), size)]
        target = kept[at].at[:, pl.ds(start, size)]
        return pltpu.make_async_copy(source, target, sems.at[at * count + i])

    for at in range(len(kept)):
        for i in range(count):
            load(at, i).start()
    kh, kl = split(jnp.concatenate([first_ref[...], second_ref[...]], 1))
    left = jnp.concatenate([kh, kl], 0)
    for at, ref in enumerate(kept):
        half, place = divmod(at, len(kept) // 2)
        out = (low_ref, high_ref)[half]

        @pl.loop(0, count)
        def _(i):
            load(at, i).wait()
            start = pl.multiple_of(i * size, size)
            ah, al = split(ref[:, pl.ds(start, size)])
            term = fast(left, ah) + fast(left, al)
            into = pl.ds(pl.multiple_of(place * span + start, size), size)
            out[:, into] = term[:width] + term[width:]


def product_down(first, second, a):
    rows, columns = a.shape
    width = first.shape[0]
    parts = parts_of(columns)
    span = columns // parts
    size = block_of(span, 256)
    whole = pl.BlockSpec(memory_space=pltpu.VMEM)
    low, high, *kept = pl.pallas_call(
        down_kernel,
        in_specs=[whole, whole, pl.BlockSpec(memory_space=pltpu.HBM)],
        out_specs=(whole,) * (2 + parts),
        out_shape=(shape(width, columns // 2),) * 2 + (shape(rows, span),) * parts,
        scratch_shapes=[pltpu.SemaphoreType.DMA((columns // size,))],
        compiler_params=params(12),
        cost_estimate=cost(8 * rows * columns * width, 4 * rows * columns),
        name="product_down",
    )(first, second, pltpu.with_memory_space_constraint(a, pltpu.HBM))
    return low, high, tuple(kept)


def fix_kernel(parts, low_ref, high_ref, band_ref, *refs):
    tops, keep_ref, give_ref = refs[:parts], refs[parts], refs[parts + 1]
    row = lax.axis_index("row")
    core = lax.rem(row, 2)
    first, second = low_ref[...], high_ref[...]
    span = tops[0].shape[1]

    @pl.when(row == 0)
    def _():
        rh, rl = split(band_ref[...].T)
        left = jnp.concatenate([rh, rl, rh, rl], 1)
        for at, top in enumerate(tops):
            half, place = divmod(at, parts // 2)
            ah, al = split(top[...])
            value = (first, second)[half][:, place * span : (place + 1) * span]
            (keep_ref, give_ref)[half][:, place * span : (place + 1) * span] = value - fast(
                left, jnp.concatenate([ah, ah, al, al], 0)
            )

    @pl.when((row != 0) & (core == 0))
    def _():
        keep_ref[...] = first
        give_ref[...] = second

    @pl.when(core == 1)
    def _():
        keep_ref[...] = second
        give_ref[...] = first


def fix_down(low, high, band, kept):
    width, half = low.shape
    parts = len(kept)
    side = pl.BlockSpec((width, half), lambda i: (0, 0))
    top = pl.BlockSpec((width, kept[0].shape[1]), lambda i: (0, 0))
    anywhere = pl.BlockSpec(memory_space=pl.ANY)

    def kernel(*refs):
        fix_kernel(parts, *refs)

    keep, give, *kept = pl.pallas_call(
        kernel,
        grid=(1,),
        in_specs=[side, side, pl.BlockSpec((width, width), lambda i: (0, 0))] + [top] * parts,
        out_specs=(side, side) + (anywhere,) * parts,
        out_shape=(shape(width, half),) * 2 + tuple(shape(*x.shape) for x in kept),
        input_output_aliases={3 + k: 2 + k for k in range(parts)},
        compiler_params=params(12),
        cost_estimate=cost(24 * width * width * half, 32 * width * half),
        name="fix_down",
    )(low, high, band, *kept)
    return keep, give, tuple(kept)


def rows_product(right_ref, halves, outs):
    span = halves[0].shape[1]
    width = right_ref.shape[1] // 2
    chunk = block_of(span, 512)
    total = None
    for at, a_ref in enumerate(halves):
        for c in range(0, span, chunk):
            ah, al = split(a_ref[:, c : c + chunk])
            right = right_ref[at * span + c : at * span + c + chunk, :]
            term = fast(ah, right) + fast(al, right)
            total = term if total is None else total + term
    result = (total[:, :width] + total[:, width:]).T
    for at, out_ref in enumerate(outs):

        @pl.when(pl.program_id(0) == at)
        def _():
            out_ref[...] = result


def across_kernel(parts, held_ref, other_ref, band_ref, *refs):
    kct_ref, right_ref = refs[parts : parts + 2]
    width, half = held_ref.shape
    columns = 2 * half
    chunk = block_of(columns, 512)

    @pl.when(pl.program_id(0) == 0)
    def _():
        core = lax.rem(lax.axis_index("row"), 2)

        @pl.when(core == 0)
        def _():
            kct_ref[:, :half] = held_ref[...]
            kct_ref[:, half:] = other_ref[...]

        @pl.when(core == 1)
        def _():
            kct_ref[:, :half] = other_ref[...]
            kct_ref[:, half:] = held_ref[...]

        @pl.when(lax.axis_index("col") == 0)
        def _():
            kct_ref[:, :width] = kct_ref[:, :width] - band_ref[...].T

        for c in range(0, columns, chunk):
            right_ref[c : c + chunk, :] = jnp.concatenate(split(kct_ref[:, c : c + chunk].T), 1)

    rows_product(right_ref, refs[:parts], refs[parts + 2 : -parts])


def more_kernel(parts, right_ref, *refs):
    rows_product(right_ref, refs[:parts], refs[parts:-parts])


def across_call(kernel, operands, extra, kept, pieces, start, count, width):
    rows, span = kept[0].shape
    parts = len(kept)
    size = rows // pieces

    def turn(i):
        return (lax.rem(i + start + lax.axis_index("col"), pieces), 0)

    def fixed(array):
        return pl.BlockSpec(array.shape, lambda i: (0, 0))

    def body(*refs):
        kernel(parts, *refs)

    outs = tuple(extra) + (shape(width, size),) * count
    at, to = len(operands), len(outs)
    results = pl.pallas_call(
        body,
        grid=(count,),
        in_specs=[fixed(x) for x in operands] + [pl.BlockSpec((size, span), turn)] * parts,
        out_specs=tuple(fixed(x) for x in outs) + (pl.BlockSpec(memory_space=pl.ANY),) * parts,
        out_shape=outs + (shape(rows, span),) * parts,
        input_output_aliases={at + k: to + k for k in range(parts)},
        compiler_params=params(22),
        cost_estimate=cost(8 * size * count * span * parts * width, 4 * size * count * span * parts),
    )(*operands, *kept)
    return (*results[:to], tuple(results[to:]))


def merge_first_kernel(first_ref, second_ref, by_x_ref, by_y_ref, a_ref, b_ref):
    half = a_ref.shape[1]
    relation = lax.div(lax.axis_index("row"), 2) ^ lax.axis_index("col")
    for at, own, got, out in (
        (1, first_ref, by_x_ref, a_ref),
        (2, second_ref, by_y_ref, b_ref),
    ):
        out[...] = jnp.where(
            relation == 0, own[...], jnp.where(relation == at, got[:, :half], 0.0)
        )


def join_kernel(a_ref, b_ref, c_ref, d_ref, out_ref):
    half = a_ref.shape[1]
    out_ref[:, :half] = a_ref[...] + b_ref[...]
    out_ref[:, half:] = c_ref[...] + d_ref[...]


def halve_kernel(keep_ref, other_ref, a_ref, b_ref):
    half = a_ref.shape[1]
    a_ref[...] = keep_ref[:, :half] + other_ref[:, :half]
    b_ref[...] = keep_ref[:, half:] + other_ref[:, half:]


def pair_kernel(a_ref, b_ref, c_ref, d_ref, e_ref, f_ref):
    e_ref[...] = a_ref[...] + b_ref[...]
    f_ref[...] = c_ref[...] + d_ref[...]


def half_product(kct_ref, x_ref, core):
    half = x_ref.shape[1]
    start = pl.multiple_of(core * half, half)
    return lax.dot_general(
        kct_ref[:, pl.ds(start, half)],
        x_ref[...],
        (((1,), (1,)), ((), ())),
        precision=precise,
        preferred_element_type=f32,
    )


def inner_own_kernel(kct_ref, held_ref, inner_ref):
    inner_ref[...] = half_product(kct_ref, held_ref, lax.rem(lax.axis_index("row"), 2))


def inner_kernel(kct_ref, held_ref, other_ref, own_ref, xct_ref, inner_ref):
    half = held_ref.shape[1]
    core = lax.rem(lax.axis_index("row"), 2)

    @pl.when(core == 0)
    def _():
        xct_ref[:, :half] = held_ref[...]
        xct_ref[:, half:] = other_ref[...]

    @pl.when(core == 1)
    def _():
        xct_ref[:, :half] = other_ref[...]
        xct_ref[:, half:] = held_ref[...]

    inner_ref[...] = own_ref[...] + half_product(kct_ref, other_ref, 1 - core)


def wide_kernel(
    st_ref, xct_ref, kct_ref, first_ref, second_ref, band_ref, x_ref, k_ref, rows_ref, left_ref
):
    width, columns = kct_ref.shape
    st = st_ref[...]
    chunk = block_of(columns, 512)
    for c in range(0, columns, chunk):
        for ref, value in (
            (x_ref, dot(st, xct_ref[:, c : c + chunk])),
            (k_ref, kct_ref[:, c : c + chunk]),
        ):
            ref[:, c : c + chunk] = jnp.concatenate(split(value), 0)
    half = first_ref.shape[1]
    rows_ref[:, :half] = first_ref[...]
    rows_ref[:, half:] = second_ref[...]

    @pl.when(lax.axis_index("row") == 0)
    def _():
        rows_ref[:, :width] = rows_ref[:, :width] - band_ref[...].T

    rows = rows_ref.shape[1]
    deep = block_of(rows, 512)
    for r in range(0, rows, deep):
        left_ref[r : r + deep, :] = jnp.concatenate(split(rows_ref[:, r : r + deep].T), 1)


def both_parts(left):
    return jnp.concatenate([left, left], 1)


def four_parts(right_ref, start, size):
    width = right_ref.shape[0] // 2
    high = right_ref[:width, pl.ds(start, size)]
    low = right_ref[width:, pl.ds(start, size)]
    return jnp.concatenate([high, high, low, low], 0)


def near_kernel(count, left_ref, right_ref, *refs):
    total = (len(refs)) // 2
    rows, span = refs[0].shape
    deep = block_of(rows, 512)
    chunk = block_of(span, 512)
    if span % 256 == 0 and span <= 1024:
        chunk = span
    for at in range(count):
        a_ref, out_ref = refs[at], refs[total + at]

        @pl.loop(0, span // chunk)
        def _(i):
            c = pl.multiple_of(i * chunk, chunk)
            right = four_parts(right_ref, pl.multiple_of(at * span + c, 128), chunk)
            for r in range(0, rows, deep):
                out_ref[r : r + deep, pl.ds(c, chunk)] = a_ref[
                    r : r + deep, pl.ds(c, chunk)
                ] - fast(both_parts(left_ref[r : r + deep, :]), right)


def subtract_near(left, right, kept):
    rows, span = kept[0].shape
    parts = len(kept)
    count = parts
    deep = left.shape[1]
    whole = pl.BlockSpec(memory_space=pltpu.VMEM)
    places = [whole] * count + [pl.BlockSpec(memory_space=pl.ANY)] * (parts - count)

    def kernel(*refs):
        near_kernel(count, *refs)

    return tuple(
        pl.pallas_call(
            kernel,
            in_specs=[whole] * 2 + places,
            out_specs=tuple(places),
            out_shape=(shape(rows, span),) * parts,
            input_output_aliases={2 + k: k for k in range(parts)},
            compiler_params=params(12),
            cost_estimate=cost(4 * rows * span * count * deep, 8 * rows * span * count),
            name="subtract_near",
        )(left, right, *kept)
    )


def core_blocks(width):
    half = width // 2
    return [(0, 0), (0, half), (half, half)], half


def packing(width, size):
    half = width // 2
    beside = 1
    while 6 * beside * half <= size and 2 * beside <= half // 8:
        beside *= 2
    return beside, half // beside


def line_kernel(*refs):
    *chunks, inner_ref, out_ref = refs
    width, size = chunks[0].shape
    beside, tall = packing(width, size)
    blocks, half = core_blocks(width)
    total = chunks[0][...]
    for ref in chunks[1:]:
        total = total + ref[...]
    out_ref[:width, :] = total
    below = [
        inner_ref[r + k * tall : r + (k + 1) * tall, c : c + half]
        for r, c in blocks
        for k in range(beside)
    ]
    spare = size - half * len(below)
    if spare:
        below.append(jnp.zeros((tall, spare), f32))
    out_ref[width:, :] = jnp.concatenate(below, 1)


def left_kernel(st_ref, krt_ref, *refs):
    chunks, left_ref = refs[:-1], refs[-1]
    pieces = len(chunks)
    width, size = st_ref.shape[0], chunks[0].shape[1]
    beside, _ = packing(width, size)
    half = core_blocks(width)[1]
    packed = chunks[0][width:, :]
    for ref in chunks[1:]:
        packed = packed + ref[width:, :]
    near, cross, far = (
        jnp.concatenate(
            [packed[:, (b * beside + k) * half : (b * beside + k + 1) * half] for k in range(beside)],
            0,
        )
        for b in range(3)
    )
    inner = jnp.concatenate(
        [jnp.concatenate([near, cross], 1), jnp.concatenate([cross.T, far], 1)], 0
    )
    st = st_ref[...]
    scaled = [dot(st, ref[:width, :]) for ref in chunks]
    cm = dot(dot(st, inner), st.T)
    col = lax.axis_index("col")
    for at in range(pieces):
        start = pl.multiple_of(lax.rem(col + pieces - at, pieces) * size, size)
        value = scaled[at] - dot(cm, krt_ref[:, pl.ds(start, size)])
        left_ref[pl.ds(start, size), :] = jnp.concatenate(split(value.T), 1)


def far_kernel(count, left_ref, right_ref, near_left_ref, near_right_ref, *refs):
    *kept, out_ref, buffer, sems = refs
    rows, span = kept[0].shape
    slots, deep, _ = buffer.shape
    turns = len(kept)
    down = rows // deep

    def store(i, slot):
        turn, pair = lax.rem(i, turns), lax.div(i, turns)
        r = pl.multiple_of(pair * deep, deep)
        c = pl.multiple_of(turn * span, span)
        return pltpu.make_async_copy(
            buffer.at[slot], out_ref.at[pl.ds(r, deep), pl.ds(c, span)], sems.at[slot]
        )

    @pl.loop(0, down)
    def _(pair):
        r = pl.multiple_of(pair * deep, deep)
        for turn, a_ref in enumerate(kept):
            i = pair * turns + turn
            slot = lax.rem(i, slots)

            @pl.when(i >= slots)
            def _():
                store(i - slots, slot).wait()

            left = both_parts(left_ref[pl.ds(r, deep), :])
            right = four_parts(right_ref, turn * span, span)
            if turn >= count:
                left = jnp.concatenate([left, both_parts(near_left_ref[pl.ds(r, deep), :])], 1)
                right = jnp.concatenate([right, four_parts(near_right_ref, turn * span, span)], 0)
            buffer[slot] = a_ref[pl.ds(r, deep), :] - fast(left, right)
            store(i, slot).start()

    for back in range(slots, 0, -1):
        store(down * turns - back, (down * turns - back) % slots).wait()


def subtract_far(left, right, near_left, near_right, kept):
    rows, span = kept[0].shape
    parts = len(kept)
    deep = left.shape[1]
    whole = pl.BlockSpec(memory_space=pltpu.VMEM)

    def kernel(*refs):
        far_kernel(parts, *refs)

    return pl.pallas_call(
        kernel,
        in_specs=[whole] * (4 + parts),
        out_specs=pl.BlockSpec(memory_space=pltpu.HBM),
        out_shape=shape(rows, parts * span),
        scratch_shapes=[
            pltpu.VMEM((3, block_of(rows, 512), span), f32),
            pltpu.SemaphoreType.DMA((3,)),
        ],
        compiler_params=params(12),
        cost_estimate=cost(5 * rows * span * parts * deep, 8 * rows * span * parts),
        name="subtract_far",
    )(left, right, near_left, near_right, *kept)


def flip(value, bit, size, axis="row"):
    return lax.ppermute(value, axis, [(i, i ^ bit) for i in range(size)])


def from_sources(piece, col_size, source_flips, bit):
    pairs = []
    for c in range(col_size):
        for source in source_flips:
            for core in range(2):
                at = (2 * c + core) ^ source
                pairs.append((at * col_size + c, (at ^ bit) * col_size + c))
    return lax.ppermute(piece, ("row", "col"), pairs)


def shift(piece, by, size):
    return lax.ppermute(piece, "col", [(i, (i + by) % size) for i in range(size)])


def body_of(row_size, col_size):
    assert row_size == 2 * col_size

    def body(matrix, panel):
        rows, width = panel.shape
        columns = matrix.shape[1]
        small = shape(width, width)
        packed = shape(width, 2 * width)
        half = shape(width, rows // 2)
        first, second, partial = open_panel(panel.T)
        apart = flip(partial, 1, row_size)
        if row_size == 8:
            wide_half = shape(width, rows // 2 + 2 * width)
            send_x, send_y, partial = small_call(
                add_cores_kernel, (wide_half, wide_half, packed), first, second, partial, apart
            )
            by_x = flip(send_x, 2, row_size)
            by_y = flip(send_y, 4, row_size)
            terms = [partial, by_x, by_y, flip(partial, 6, row_size)]
        else:
            partial = small_call(add_kernel, packed, partial, apart)
            bit = 2
            total = partial
            while bit < row_size // 2:
                total = total + flip(total, bit, row_size)
                bit *= 2
            zero = jnp.zeros_like(total)
            terms = [total, flip(total, row_size // 2, row_size), zero, zero]
        first, second, partial = lax.optimization_barrier((first, second, partial))
        low, high, resident = product_down(first, second, matrix)
        if row_size == 8:
            one, two, resident = small_call(
                merge_first_kernel, (half, half), first, second, by_x, by_y, carry=resident
            )
            more_x = flip(two, 2, row_size)
            more_y = flip(one, 4, row_size)
        else:
            relation = (lax.axis_index("row") // 2) ^ lax.axis_index("col")
            held = jnp.where(relation == 0, jnp.concatenate([first, second], 1), 0.0)
            reached = [0]
            bit = 2
            while bit < row_size:
                held = held + from_sources(held, col_size, reached, bit)
                reached = reached + [r ^ bit for r in reached]
                bit *= 2
        band, again, band_inverse, head, resident = small_call(
            eliminate_kernel, (small, small, small, small), *terms, flops=50_000_000, carry=resident
        )
        keep, give, resident = fix_down(low, high, again, resident)
        if row_size == 8:
            held, resident = small_call(
                join_kernel, shape(width, rows), one, more_y, two, more_x, carry=resident
            )
        other = flip(held, 1, row_size)
        quarter = shape(width, columns // 4)
        a, b, resident = small_call(
            halve_kernel, (quarter, quarter), keep, flip(give, 1, row_size), carry=resident
        )
        bits = []
        bit = 2
        while bit < row_size:
            bits.append(bit)
            bit *= 2
        pieces = 1 if (rows // col_size) % 128 else col_size
        late = pieces // 2
        for forward, backward in list(zip(bits, bits[::-1]))[:-1]:
            ra = flip(a, forward, row_size)
            rb = flip(b, backward, row_size)
            if bits[0] == forward:
                kct, right, *chunks, resident = across_call(
                    across_kernel,
                    (held, other, again),
                    (shape(width, columns), shape(columns, 2 * width, dtype=bf16)),
                    resident,
                    pieces,
                    late,
                    pieces - late,
                    width,
                )
            a, b, resident = small_call(
                pair_kernel, (quarter, quarter), a, ra, b, rb, carry=resident
            )
        ra = flip(a, bits[-1], row_size)
        rb = flip(b, bits[0], row_size)
        received = []
        if late:
            received = [shift(chunks[at], late + at, col_size) for at in range(pieces - late)]
            chunks = []
            for at in range(late - 1, -1, -1):
                piece, resident = across_call(
                    more_kernel, (right,), (), resident, pieces, at, 1, width
                )
                chunks = [piece] + chunks
                if at:
                    received += [shift(piece, at, col_size)]
        summed, resident = small_call(
            join_kernel, shape(width, columns // 2), a, ra, b, rb, carry=resident
        )
        exchanged = flip(summed, 1, row_size)
        own, resident = small_call(inner_own_kernel, small, kct, summed, carry=resident)
        xct, inner, resident = small_call(
            inner_kernel,
            (shape(width, columns), small),
            kct,
            summed,
            exchanged,
            own,
            carry=resident,
        )
        tall = packing(width, rows // pieces)[1]
        mine, resident = small_call(
            line_kernel,
            shape(width + tall, rows // pieces),
            chunks[0],
            *received,
            inner,
            carry=resident,
        )
        if pieces == 1:
            whole = [lax.psum(mine, "col")]
        else:
            whole = [mine] + [shift(mine, by, col_size) for by in range(1, col_size)]
        st, resident = small_call(
            invert_kernel, small, head, again, band_inverse, flops=50_000_000, carry=resident
        )
        xparts, kparts, krt, near_left, resident = small_call(
            wide_kernel,
            (
                shape(2 * width, columns, dtype=bf16),
                shape(2 * width, columns, dtype=bf16),
                shape(width, rows),
                shape(rows, 2 * width, dtype=bf16),
            ),
            st,
            xct,
            kct,
            first,
            second,
            again,
            mib=12,
            carry=resident,
        )
        resident = subtract_near(near_left, xparts, resident)
        left, resident = small_call(
            left_kernel, shape(rows, 2 * width, dtype=bf16), st, krt, *whole, mib=12, carry=resident
        )
        return subtract_far(left, kparts, near_left, xparts, resident), band

    return body


def solution(mesh):
    body = body_of(mesh.shape["row"], mesh.shape["col"])

    return jax.shard_map(
        body,
        mesh=mesh,
        in_specs=(P("row", "col"), P("row", None)),
        out_specs=(P("row", "col"), P()),
        check_vma=False,
    )
```

```python
import jax
import jax.numpy as jnp
from jax import lax
from jax.experimental import pallas as pl
from jax.experimental.pallas import tpu as pltpu
from jax.sharding import PartitionSpec as P


precise = lax.Precision.HIGHEST
f32 = jnp.float32
bf16 = jnp.bfloat16


def shape(*dims, dtype=f32):
    return jax.ShapeDtypeStruct(dims, dtype)


def params(mib):
    return pltpu.CompilerParams(vmem_limit_bytes=mib * 1024 * 1024)


def cost(flops, moved):
    return pl.CostEstimate(flops=flops, bytes_accessed=moved, transcendentals=0)


def dot(a, b):
    return jnp.dot(a, b, precision=precise, preferred_element_type=f32)


def fast(a, b):
    return jnp.dot(a, b, preferred_element_type=f32)


def split(value):
    high = value.astype(bf16)
    return high, (value - high.astype(f32)).astype(bf16)


def block_of(size, wanted):
    while size % wanted:
        wanted //= 2
    return wanted


def small_call(kernel, out, *operands, carry=(), flops=1_000_000, moved=1_000_000, mib=8):
    extra = {}
    body = kernel
    if carry:
        outs = out if isinstance(out, tuple) else (out,)
        count, more = len(operands), len(carry)
        anywhere = pl.BlockSpec(memory_space=pl.ANY)
        whole = pl.BlockSpec(memory_space=pltpu.VMEM)
        extra = dict(
            in_specs=[whole] * count + [anywhere] * more,
            out_specs=(whole,) * len(outs) + (anywhere,) * more,
            input_output_aliases={count + k: len(outs) + k for k in range(more)},
        )
        operands = operands + tuple(carry)
        out = outs + tuple(shape(*x.shape) for x in carry)

        def body(*refs):
            kernel(*refs[:count], *refs[count + more : -more])

    result = pl.pallas_call(
        body, out_shape=out, compiler_params=params(mib), cost_estimate=cost(flops, moved), **extra
    )(*operands)
    if carry:
        return tuple(result[: -len(carry)]) + (tuple(result[-len(carry) :]),)
    return result


def open_kernel(turned_ref, first_ref, second_ref, packed_ref):
    width = turned_ref.shape[0]
    half = first_ref.shape[1]
    turned = turned_ref[...]
    first_ref[...] = turned[:, :half]
    second_ref[...] = turned[:, half:]
    gram = lax.dot_general(
        turned, turned, (((1,), (1,)), ((), ())), precision=precise, preferred_element_type=f32
    )
    head = jnp.where(lax.axis_index("row") == 0, turned[:, : 2 * width].T[:width], 0.0)
    packed_ref[...] = jnp.concatenate([gram, head], 1)


def add_cores_kernel(first_ref, second_ref, a_ref, b_ref, x_ref, y_ref, sum_ref):
    half = first_ref.shape[1]
    total = a_ref[...] + b_ref[...]
    sum_ref[...] = total
    for source, target in ((first_ref, x_ref), (second_ref, y_ref)):
        target[:, :half] = source[...]
        target[:, half:] = total


def add_kernel(*refs):
    total = refs[0][...]
    for ref in refs[1:-1]:
        total = total + ref[...]
    refs[-1][...] = total


def spread(tile, at):
    return jnp.broadcast_to(tile[at : at + 1, :], tile.shape)


def pick(tile, at):
    return jnp.broadcast_to(tile[:, at : at + 1], tile.shape)


def sweep(tiles, order, full):
    lane = lax.broadcasted_iota(jnp.int32, (8, order), 1)
    sub = lax.broadcasted_iota(jnp.int32, (8, order), 0)
    tiles = list(tiles)
    for at in range(order // 8):
        base = 8 * at
        inside = (lane >= base) & (lane < base + 8)
        tile = tiles[at]
        others = [t for t in range(order // 8) if (t != at if full else t > at)]
        picked = {t: [pick(tiles[t], base + q) for q in range(8)] for t in others}
        columns = [pick(tile, base + q) for q in range(8)]
        rows = jnp.where(inside, jnp.where(lane - base == sub, 1.0, 0.0), tile)
        lower, upper = rows, tile
        for q in range(8):
            here = sub == q
            inverse = 1.0 / spread(columns[q], q)
            scaled = spread(rows, q) * inverse
            if not full:
                lower = jnp.where(here, rows, lower)
                upper = jnp.where(
                    sub > q, upper - columns[q] * (spread(upper, q) * inverse), upper
                )
            rows = jnp.where(here, scaled, rows - columns[q] * scaled)
            for p in range(q + 1, 8):
                part = spread(columns[p], q) * inverse
                columns[p] = jnp.where(here, part, columns[p] - columns[q] * part)
        finals = [spread(rows, q) for q in range(8)]
        for t in others:
            value = jnp.where(inside, 0.0, tiles[t])
            for q in range(8):
                value = value - picked[t][q] * finals[q]
            tiles[t] = value
        tiles[at] = rows if full else jnp.where(inside & (lane - base >= sub), upper, lower)
    return tiles


def eliminate_kernel(a_ref, b_ref, c_ref, d_ref, band_ref, again_ref, inverse_ref, head_ref):
    order = band_ref.shape[0]
    lane = lax.broadcasted_iota(jnp.int32, (8, order), 1)
    sub = lax.broadcasted_iota(jnp.int32, (8, order), 0)
    skip = b_ref.shape[1] - a_ref.shape[1]
    total = (a_ref[...] + b_ref[:, skip:]) + (c_ref[:, skip:] + d_ref[...])
    head_ref[...] = total[:, order:]
    gram = total[:, :order]
    tiles = sweep([gram[8 * t : 8 * t + 8, :] for t in range(order // 8)], order, False)
    for t in range(order // 8):
        row_at = sub + 8 * t
        diagonal = jnp.sum(jnp.where(lane == row_at, tiles[t], 0.0), axis=1, keepdims=True)
        length = jnp.sqrt(diagonal)
        scaled = tiles[t] / length
        band = jnp.where(lane > row_at, -scaled, jnp.where(lane == row_at, -length, 0.0))
        band_ref[8 * t : 8 * t + 8, :] = band
        again_ref[8 * t : 8 * t + 8, :] = band
        inverse_ref[8 * t : 8 * t + 8, :] = jnp.where(
            lane < row_at, -scaled, jnp.where(lane == row_at, -1.0 / length, 0.0)
        )


def invert_kernel(head_ref, band_ref, inverse_ref, out_ref):
    order = head_ref.shape[0]
    tiles = [
        head_ref[8 * t : 8 * t + 8, :] - band_ref[8 * t : 8 * t + 8, :] for t in range(order // 8)
    ]
    tiles = sweep(tiles, order, True)
    out_ref[...] = -dot(jnp.concatenate(tiles, 0), inverse_ref[...])


def parts_of(columns):
    return 2 if columns % 512 else 4


def down_kernel(first_ref, second_ref, a_ref, low_ref, high_ref, *refs):
    kept, sems = refs[:-1], refs[-1]
    width = low_ref.shape[0]
    span = kept[0].shape[1]
    count = sems.shape[0] // len(kept)
    size = span // count

    def load(at, i):
        start = pl.multiple_of(i * size, size)
        source = a_ref.at[:, pl.ds(pl.multiple_of(at * span + start, size), size)]
        target = kept[at].at[:, pl.ds(start, size)]
        return pltpu.make_async_copy(source, target, sems.at[at * count + i])

    for at in range(len(kept)):
        for i in range(count):
            load(at, i).start()
    kh, kl = split(jnp.concatenate([first_ref[...], second_ref[...]], 1))
    left = jnp.concatenate([kh, kl], 0)
    for at, ref in enumerate(kept):
        half, place = divmod(at, len(kept) // 2)
        out = (low_ref, high_ref)[half]

        @pl.loop(0, count)
        def _(i):
            load(at, i).wait()
            start = pl.multiple_of(i * size, size)
            ah, al = split(ref[:, pl.ds(start, size)])
            term = fast(left, ah) + fast(left, al)
            into = pl.ds(pl.multiple_of(place * span + start, size), size)
            out[:, into] = term[:width] + term[width:]


def product_down(first, second, a):
    rows, columns = a.shape
    width = first.shape[0]
    parts = parts_of(columns)
    span = columns // parts
    size = block_of(span, 256)
    whole = pl.BlockSpec(memory_space=pltpu.VMEM)
    low, high, *kept = pl.pallas_call(
        down_kernel,
        in_specs=[whole, whole, pl.BlockSpec(memory_space=pltpu.HBM)],
        out_specs=(whole,) * (2 + parts),
        out_shape=(shape(width, columns // 2),) * 2 + (shape(rows, span),) * parts,
        scratch_shapes=[pltpu.SemaphoreType.DMA((columns // size,))],
        compiler_params=params(12),
        cost_estimate=cost(8 * rows * columns * width, 4 * rows * columns),
        name="product_down",
    )(first, second, pltpu.with_memory_space_constraint(a, pltpu.HBM))
    return low, high, tuple(kept)


def fix_kernel(parts, low_ref, high_ref, band_ref, *refs):
    tops, keep_ref, give_ref = refs[:parts], refs[parts], refs[parts + 1]
    row = lax.axis_index("row")
    core = lax.rem(row, 2)
    first, second = low_ref[...], high_ref[...]
    span = tops[0].shape[1]

    @pl.when(row == 0)
    def _():
        rh, rl = split(band_ref[...].T)
        left = jnp.concatenate([rh, rl, rh, rl], 1)
        for at, top in enumerate(tops):
            half, place = divmod(at, parts // 2)
            ah, al = split(top[...])
            value = (first, second)[half][:, place * span : (place + 1) * span]
            (keep_ref, give_ref)[half][:, place * span : (place + 1) * span] = value - fast(
                left, jnp.concatenate([ah, ah, al, al], 0)
            )

    @pl.when((row != 0) & (core == 0))
    def _():
        keep_ref[...] = first
        give_ref[...] = second

    @pl.when(core == 1)
    def _():
        keep_ref[...] = second
        give_ref[...] = first


def fix_down(low, high, band, kept):
    width, half = low.shape
    parts = len(kept)
    side = pl.BlockSpec((width, half), lambda i: (0, 0))
    top = pl.BlockSpec((width, kept[0].shape[1]), lambda i: (0, 0))
    anywhere = pl.BlockSpec(memory_space=pl.ANY)

    def kernel(*refs):
        fix_kernel(parts, *refs)

    keep, give, *kept = pl.pallas_call(
        kernel,
        grid=(1,),
        in_specs=[side, side, pl.BlockSpec((width, width), lambda i: (0, 0))] + [top] * parts,
        out_specs=(side, side) + (anywhere,) * parts,
        out_shape=(shape(width, half),) * 2 + tuple(shape(*x.shape) for x in kept),
        input_output_aliases={3 + k: 2 + k for k in range(parts)},
        compiler_params=params(12),
        cost_estimate=cost(24 * width * width * half, 32 * width * half),
        name="fix_down",
    )(low, high, band, *kept)
    return keep, give, tuple(kept)


def rows_product(right_ref, halves, outs):
    span = halves[0].shape[1]
    width = right_ref.shape[1] // 2
    chunk = block_of(span, 512)
    total = None
    for at, a_ref in enumerate(halves):
        for c in range(0, span, chunk):
            ah, al = split(a_ref[:, c : c + chunk])
            right = right_ref[at * span + c : at * span + c + chunk, :]
            term = fast(ah, right) + fast(al, right)
            total = term if total is None else total + term
    result = (total[:, :width] + total[:, width:]).T
    for at, out_ref in enumerate(outs):

        @pl.when(pl.program_id(0) == at)
        def _():
            out_ref[...] = result


def across_kernel(parts, held_ref, other_ref, band_ref, *refs):
    kct_ref, right_ref = refs[parts : parts + 2]
    width, half = held_ref.shape
    columns = 2 * half
    chunk = block_of(columns, 512)

    @pl.when(pl.program_id(0) == 0)
    def _():
        core = lax.rem(lax.axis_index("row"), 2)

        @pl.when(core == 0)
        def _():
            kct_ref[:, :half] = held_ref[...]
            kct_ref[:, half:] = other_ref[...]

        @pl.when(core == 1)
        def _():
            kct_ref[:, :half] = other_ref[...]
            kct_ref[:, half:] = held_ref[...]

        @pl.when(lax.axis_index("col") == 0)
        def _():
            kct_ref[:, :width] = kct_ref[:, :width] - band_ref[...].T

        for c in range(0, columns, chunk):
            right_ref[c : c + chunk, :] = jnp.concatenate(split(kct_ref[:, c : c + chunk].T), 1)

    rows_product(right_ref, refs[:parts], refs[parts + 2 : -parts])


def more_kernel(parts, right_ref, *refs):
    rows_product(right_ref, refs[:parts], refs[parts:-parts])


def across_call(kernel, operands, extra, kept, pieces, start, count, width):
    rows, span = kept[0].shape
    parts = len(kept)
    size = rows // pieces

    def turn(i):
        return (lax.rem(i + start + lax.axis_index("col"), pieces), 0)

    def fixed(array):
        return pl.BlockSpec(array.shape, lambda i: (0, 0))

    def body(*refs):
        kernel(parts, *refs)

    outs = tuple(extra) + (shape(width, size),) * count
    at, to = len(operands), len(outs)
    results = pl.pallas_call(
        body,
        grid=(count,),
        in_specs=[fixed(x) for x in operands] + [pl.BlockSpec((size, span), turn)] * parts,
        out_specs=tuple(fixed(x) for x in outs) + (pl.BlockSpec(memory_space=pl.ANY),) * parts,
        out_shape=outs + (shape(rows, span),) * parts,
        input_output_aliases={at + k: to + k for k in range(parts)},
        compiler_params=params(22),
        cost_estimate=cost(8 * size * count * span * parts * width, 4 * size * count * span * parts),
    )(*operands, *kept)
    return (*results[:to], tuple(results[to:]))


def merge_first_kernel(first_ref, second_ref, by_x_ref, by_y_ref, a_ref, b_ref):
    half = a_ref.shape[1]
    relation = lax.div(lax.axis_index("row"), 2) ^ lax.axis_index("col")
    for at, own, got, out in (
        (1, first_ref, by_x_ref, a_ref),
        (2, second_ref, by_y_ref, b_ref),
    ):
        out[...] = jnp.where(
            relation == 0, own[...], jnp.where(relation == at, got[:, :half], 0.0)
        )


def join_kernel(a_ref, b_ref, c_ref, d_ref, out_ref):
    half = a_ref.shape[1]
    out_ref[:, :half] = a_ref[...] + b_ref[...]
    out_ref[:, half:] = c_ref[...] + d_ref[...]


def halve_kernel(keep_ref, other_ref, a_ref, b_ref):
    half = a_ref.shape[1]
    a_ref[...] = keep_ref[:, :half] + other_ref[:, :half]
    b_ref[...] = keep_ref[:, half:] + other_ref[:, half:]


def pair_kernel(a_ref, b_ref, c_ref, d_ref, e_ref, f_ref):
    e_ref[...] = a_ref[...] + b_ref[...]
    f_ref[...] = c_ref[...] + d_ref[...]


def half_product(kct_ref, x_ref, core):
    half = x_ref.shape[1]
    start = pl.multiple_of(core * half, half)
    return lax.dot_general(
        kct_ref[:, pl.ds(start, half)],
        x_ref[...],
        (((1,), (1,)), ((), ())),
        precision=precise,
        preferred_element_type=f32,
    )


def inner_own_kernel(kct_ref, held_ref, inner_ref):
    inner_ref[...] = half_product(kct_ref, held_ref, lax.rem(lax.axis_index("row"), 2))


def inner_kernel(kct_ref, held_ref, other_ref, own_ref, xct_ref, inner_ref):
    half = held_ref.shape[1]
    core = lax.rem(lax.axis_index("row"), 2)

    @pl.when(core == 0)
    def _():
        xct_ref[:, :half] = held_ref[...]
        xct_ref[:, half:] = other_ref[...]

    @pl.when(core == 1)
    def _():
        xct_ref[:, :half] = other_ref[...]
        xct_ref[:, half:] = held_ref[...]

    inner_ref[...] = own_ref[...] + half_product(kct_ref, other_ref, 1 - core)


def wide_kernel(
    st_ref, xct_ref, kct_ref, first_ref, second_ref, band_ref, x_ref, k_ref, rows_ref, left_ref
):
    width, columns = kct_ref.shape
    st = st_ref[...]
    chunk = block_of(columns, 512)
    for c in range(0, columns, chunk):
        for ref, value in (
            (x_ref, dot(st, xct_ref[:, c : c + chunk])),
            (k_ref, kct_ref[:, c : c + chunk]),
        ):
            ref[:, c : c + chunk] = jnp.concatenate(split(value), 0)
    half = first_ref.shape[1]
    rows_ref[:, :half] = first_ref[...]
    rows_ref[:, half:] = second_ref[...]

    @pl.when(lax.axis_index("row") == 0)
    def _():
        rows_ref[:, :width] = rows_ref[:, :width] - band_ref[...].T

    rows = rows_ref.shape[1]
    deep = block_of(rows, 512)
    for r in range(0, rows, deep):
        left_ref[r : r + deep, :] = jnp.concatenate(split(rows_ref[:, r : r + deep].T), 1)


def both_parts(left):
    return jnp.concatenate([left, left], 1)


def four_parts(right_ref, start, size):
    width = right_ref.shape[0] // 2
    high = right_ref[:width, pl.ds(start, size)]
    low = right_ref[width:, pl.ds(start, size)]
    return jnp.concatenate([high, high, low, low], 0)


def near_kernel(count, left_ref, right_ref, *refs):
    total = (len(refs)) // 2
    rows, span = refs[0].shape
    deep = block_of(rows, 512)
    chunk = block_of(span, 512)
    if span % 256 == 0 and span <= 1024:
        chunk = span
    for at in range(count):
        a_ref, out_ref = refs[at], refs[total + at]

        @pl.loop(0, span // chunk)
        def _(i):
            c = pl.multiple_of(i * chunk, chunk)
            right = four_parts(right_ref, pl.multiple_of(at * span + c, 128), chunk)
            for r in range(0, rows, deep):
                out_ref[r : r + deep, pl.ds(c, chunk)] = a_ref[
                    r : r + deep, pl.ds(c, chunk)
                ] - fast(both_parts(left_ref[r : r + deep, :]), right)


def store_slots():
    return 4


def subtract_near(left, right, kept):
    rows, span = kept[0].shape
    parts = len(kept)
    count = parts
    deep = left.shape[1]
    whole = pl.BlockSpec(memory_space=pltpu.VMEM)
    places = [whole] * count + [pl.BlockSpec(memory_space=pl.ANY)] * (parts - count)

    def kernel(*refs):
        near_kernel(count, *refs)

    return tuple(
        pl.pallas_call(
            kernel,
            in_specs=[whole] * 2 + places,
            out_specs=tuple(places),
            out_shape=(shape(rows, span),) * parts,
            input_output_aliases={2 + k: k for k in range(parts)},
            compiler_params=params(12),
            cost_estimate=cost(4 * rows * span * count * deep, 8 * rows * span * count),
            name="subtract_near",
        )(left, right, *kept)
    )


def core_blocks(width):
    half = width // 2
    return [(0, 0), (0, half), (half, half)], half


def packing(width, size):
    half = width // 2
    beside = 1
    while 6 * beside * half <= size and 2 * beside <= half // 8:
        beside *= 2
    return beside, half // beside


def line_kernel(*refs):
    *chunks, inner_ref, out_ref = refs
    width, size = chunks[0].shape
    beside, tall = packing(width, size)
    blocks, half = core_blocks(width)
    total = chunks[0][...]
    for ref in chunks[1:]:
        total = total + ref[...]
    out_ref[:width, :] = total
    below = [
        inner_ref[r + k * tall : r + (k + 1) * tall, c : c + half]
        for r, c in blocks
        for k in range(beside)
    ]
    spare = size - half * len(below)
    if spare:
        below.append(jnp.zeros((tall, spare), f32))
    out_ref[width:, :] = jnp.concatenate(below, 1)


def left_kernel(st_ref, krt_ref, *refs):
    chunks, left_ref = refs[:-1], refs[-1]
    pieces = len(chunks)
    width, size = st_ref.shape[0], chunks[0].shape[1]
    beside, _ = packing(width, size)
    half = core_blocks(width)[1]
    packed = chunks[0][width:, :]
    for ref in chunks[1:]:
        packed = packed + ref[width:, :]
    near, cross, far = (
        jnp.concatenate(
            [packed[:, (b * beside + k) * half : (b * beside + k + 1) * half] for k in range(beside)],
            0,
        )
        for b in range(3)
    )
    inner = jnp.concatenate(
        [jnp.concatenate([near, cross], 1), jnp.concatenate([cross.T, far], 1)], 0
    )
    st = st_ref[...]
    scaled = [dot(st, ref[:width, :]) for ref in chunks]
    cm = dot(dot(st, inner), st.T)
    col = lax.axis_index("col")
    for at in range(pieces):
        start = pl.multiple_of(lax.rem(col + pieces - at, pieces) * size, size)
        value = scaled[at] - dot(cm, krt_ref[:, pl.ds(start, size)])
        left_ref[pl.ds(start, size), :] = jnp.concatenate(split(value.T), 1)


def far_kernel(count, left_ref, right_ref, near_left_ref, near_right_ref, *refs):
    *kept, out_ref, buffer, sems = refs
    rows, span = kept[0].shape
    slots, deep, _ = buffer.shape
    turns = len(kept)
    down = rows // deep

    def store(i, slot):
        turn, pair = lax.rem(i, turns), lax.div(i, turns)
        r = pl.multiple_of(pair * deep, deep)
        c = pl.multiple_of(turn * span, span)
        return pltpu.make_async_copy(
            buffer.at[slot], out_ref.at[pl.ds(r, deep), pl.ds(c, span)], sems.at[slot]
        )

    @pl.loop(0, down)
    def _(pair):
        r = pl.multiple_of(pair * deep, deep)
        for turn, a_ref in enumerate(kept):
            i = pair * turns + turn
            slot = lax.rem(i, slots)

            @pl.when(i >= slots)
            def _():
                store(i - slots, slot).wait()

            left = both_parts(left_ref[pl.ds(r, deep), :])
            right = four_parts(right_ref, turn * span, span)
            if turn >= count:
                left = jnp.concatenate([left, both_parts(near_left_ref[pl.ds(r, deep), :])], 1)
                right = jnp.concatenate([right, four_parts(near_right_ref, turn * span, span)], 0)
            buffer[slot] = a_ref[pl.ds(r, deep), :] - fast(left, right)
            store(i, slot).start()

    for back in range(slots, 0, -1):
        store(down * turns - back, (down * turns - back) % slots).wait()


def subtract_far(left, right, near_left, near_right, kept):
    rows, span = kept[0].shape
    parts = len(kept)
    deep = left.shape[1]
    whole = pl.BlockSpec(memory_space=pltpu.VMEM)

    def kernel(*refs):
        far_kernel(parts, *refs)

    return pl.pallas_call(
        kernel,
        in_specs=[whole] * (4 + parts),
        out_specs=pl.BlockSpec(memory_space=pltpu.HBM),
        out_shape=shape(rows, parts * span),
        scratch_shapes=[
            pltpu.VMEM((store_slots(), block_of(rows, 512), span), f32),
            pltpu.SemaphoreType.DMA((store_slots(),)),
        ],
        compiler_params=params(12),
        cost_estimate=cost(5 * rows * span * parts * deep, 8 * rows * span * parts),
        name="subtract_far",
    )(left, right, near_left, near_right, *kept)


def flip(value, bit, size, axis="row"):
    return lax.ppermute(value, axis, [(i, i ^ bit) for i in range(size)])


def from_sources(piece, col_size, source_flips, bit):
    pairs = []
    for c in range(col_size):
        for source in source_flips:
            for core in range(2):
                at = (2 * c + core) ^ source
                pairs.append((at * col_size + c, (at ^ bit) * col_size + c))
    return lax.ppermute(piece, ("row", "col"), pairs)


def shift(piece, by, size):
    return lax.ppermute(piece, "col", [(i, (i + by) % size) for i in range(size)])


def body_of(row_size, col_size):
    assert row_size == 2 * col_size

    def body(matrix, panel):
        rows, width = panel.shape
        columns = matrix.shape[1]
        small = shape(width, width)
        packed = shape(width, 2 * width)
        half = shape(width, rows // 2)
        first, second, partial = small_call(
            open_kernel, (half, half, packed), panel.T, flops=100_000_000, mib=12
        )
        apart = flip(partial, 1, row_size)
        if row_size == 8:
            wide_half = shape(width, rows // 2 + 2 * width)
            send_x, send_y, partial = small_call(
                add_cores_kernel, (wide_half, wide_half, packed), first, second, partial, apart
            )
            by_x = flip(send_x, 2, row_size)
            by_y = flip(send_y, 4, row_size)
            terms = [partial, by_x, by_y, flip(partial, 6, row_size)]
        else:
            partial = small_call(add_kernel, packed, partial, apart)
            bit = 2
            total = partial
            while bit < row_size // 2:
                total = total + flip(total, bit, row_size)
                bit *= 2
            zero = jnp.zeros_like(total)
            terms = [total, flip(total, row_size // 2, row_size), zero, zero]
        first, second, partial = lax.optimization_barrier((first, second, partial))
        low, high, resident = product_down(first, second, matrix)
        if row_size == 8:
            one, two, resident = small_call(
                merge_first_kernel, (half, half), first, second, by_x, by_y, carry=resident
            )
            more_x = flip(two, 2, row_size)
            more_y = flip(one, 4, row_size)
        else:
            relation = (lax.axis_index("row") // 2) ^ lax.axis_index("col")
            held = jnp.where(relation == 0, jnp.concatenate([first, second], 1), 0.0)
            reached = [0]
            bit = 2
            while bit < row_size:
                held = held + from_sources(held, col_size, reached, bit)
                reached = reached + [r ^ bit for r in reached]
                bit *= 2
        band, again, band_inverse, head, resident = small_call(
            eliminate_kernel, (small, small, small, small), *terms, flops=50_000_000, carry=resident
        )
        keep, give, resident = fix_down(low, high, again, resident)
        if row_size == 8:
            held, resident = small_call(
                join_kernel, shape(width, rows), one, more_y, two, more_x, carry=resident
            )
        other = flip(held, 1, row_size)
        quarter = shape(width, columns // 4)
        a, b, resident = small_call(
            halve_kernel, (quarter, quarter), keep, flip(give, 1, row_size), carry=resident
        )
        bits = []
        bit = 2
        while bit < row_size:
            bits.append(bit)
            bit *= 2
        pieces = 1 if (rows // col_size) % 128 else col_size
        late = pieces // 2
        for forward, backward in list(zip(bits, bits[::-1]))[:-1]:
            ra = flip(a, forward, row_size)
            rb = flip(b, backward, row_size)
            if bits[0] == forward:
                kct, right, *chunks, resident = across_call(
                    across_kernel,
                    (held, other, again),
                    (shape(width, columns), shape(columns, 2 * width, dtype=bf16)),
                    resident,
                    pieces,
                    late,
                    pieces - late,
                    width,
                )
            a, b, resident = small_call(
                pair_kernel, (quarter, quarter), a, ra, b, rb, carry=resident
            )
        ra = flip(a, bits[-1], row_size)
        rb = flip(b, bits[0], row_size)
        received = []
        if late:
            received = [shift(chunks[at], late + at, col_size) for at in range(pieces - late)]
            chunks = []
            for at in range(late - 1, -1, -1):
                piece, resident = across_call(
                    more_kernel, (right,), (), resident, pieces, at, 1, width
                )
                chunks = [piece] + chunks
                if at:
                    received += [shift(piece, at, col_size)]
        summed, resident = small_call(
            join_kernel, shape(width, columns // 2), a, ra, b, rb, carry=resident
        )
        exchanged = flip(summed, 1, row_size)
        own, resident = small_call(inner_own_kernel, small, kct, summed, carry=resident)
        xct, inner, resident = small_call(
            inner_kernel,
            (shape(width, columns), small),
            kct,
            summed,
            exchanged,
            own,
            carry=resident,
        )
        tall = packing(width, rows // pieces)[1]
        mine, resident = small_call(
            line_kernel,
            shape(width + tall, rows // pieces),
            chunks[0],
            *received,
            inner,
            carry=resident,
        )
        if pieces == 1:
            whole = [lax.psum(mine, "col")]
        else:
            whole = [mine] + [shift(mine, by, col_size) for by in range(1, col_size)]
        st, resident = small_call(
            invert_kernel, small, head, again, band_inverse, flops=50_000_000, carry=resident
        )
        xparts, kparts, krt, near_left, resident = small_call(
            wide_kernel,
            (
                shape(2 * width, columns, dtype=bf16),
                shape(2 * width, columns, dtype=bf16),
                shape(width, rows),
                shape(rows, 2 * width, dtype=bf16),
            ),
            st,
            xct,
            kct,
            first,
            second,
            again,
            mib=12,
            carry=resident,
        )
        resident = subtract_near(near_left, xparts, resident)
        left, resident = small_call(
            left_kernel, shape(rows, 2 * width, dtype=bf16), st, krt, *whole, mib=12, carry=resident
        )
        return subtract_far(left, kparts, near_left, xparts, resident), band

    return body


def solution(mesh):
    body = body_of(mesh.shape["row"], mesh.shape["col"])

    return jax.shard_map(
        body,
        mesh=mesh,
        in_specs=(P("row", "col"), P("row", None)),
        out_specs=(P("row", "col"), P()),
        check_vma=False,
    )
```
